32 devices in a mesh: tm: 16 (over z, x, core), rows: 2 (over y).
Axes of the slice: x: 2, y: 2, z: 4, core: 2. Of those that a mesh axis runs over, the one named last changes fastest.
Arguments:
- frames: bfloat16 [32, 16, 128, 128], P('tm', 'rows'), may hold values from -6 to 6
- conv_fine: bfloat16 [3, 3, 384, 128], replicated, may hold values from -0.109375 to 0.109375
- conv_down: bfloat16 [3, 384, 256], replicated, may hold values from -0.1875 to 0.1875
- conv_coarse: bfloat16 [3, 3, 768, 256], replicated, may hold values from -0.078125 to 0.078125
Outputs:
- coarse_out: bfloat16 [16, 8, 64, 256], P('tm', 'rows')
The draws below stay inside these ranges and needn't reach their ends.
All inputs are finite; a program needn't handle non-finite values.
Results may differ from the reference program's by a relative error of at most 0.014.
Values may be sent and summed in bfloat16 or wider, within the bound.
No kernel may reach another device: no remote copies, remote signals or barrier semaphores. Data moves between devices by JAX's collectives and lax.ppermute only.
A program may use at most 64 MiB of HBM per device.

```python
import jax
import jax.numpy as jnp
from jax import lax

C1 = 128
C2 = 256
COLS = 128
FRAMES = 32
ROWS = 16


def shard_levels(key, shape, split, least, top_value):
    def one(position, parts):
        draws = jax.random.uniform(jax.random.fold_in(jax.random.fold_in(key, 6), position), (parts,), jnp.float32, least / len(split), top_value / len(split))
        return jnp.repeat(jnp.exp(draws), shape[position] // parts).reshape((-1,) + (1,) * (len(shape) - position - 1))

    level = one(*split[0])
    for cut in split[1:]:
        level = level * one(*cut)
    return level


def noise(key, shape, spread, bound, cuts=(), dtype=jnp.bfloat16):
    drawn = spread * jax.random.normal(key, shape, jnp.float32)
    if cuts:
        drawn = drawn * shard_levels(key, shape, cuts, -0.22, 0.18)
    return jnp.clip(drawn, -bound, bound).astype(dtype)


def setup_inputs(seed: int = 0) -> dict:
    seeds = jax.random.split(jax.random.key(seed), 5)
    return {
        "frames": noise(seeds[0], (FRAMES, ROWS, COLS, C1), 1.0, 6.0, ((0, 16), (1, 2))),
        "conv_fine": noise(seeds[1], (3, 3, 3 * C1, C1), (27 * C1) ** -0.5, 0.109375),
        "conv_down": noise(seeds[2], (3, 3 * C1, C2), (9 * C1) ** -0.5, 0.1875),
        "conv_coarse": noise(seeds[3], (3, 3, 3 * C2, C2), (27 * C2) ** -0.5, 0.078125),
    }


def conv_causal(field, weight, channels):
    kernel = weight.reshape(3, 3, 3, channels, weight.shape[-1])
    padded = jnp.pad(field, ((2, 0), (1, 1), (1, 1), (0, 0)))
    result = lax.conv_general_dilated(padded[None], kernel, (1, 1, 1), "VALID", dimension_numbers=("NDHWC", "DHWIO", "NDHWC"), preferred_element_type=jnp.float32)
    return result[0]


def reference(frames, conv_fine, conv_down, conv_coarse):
    fine_out = jax.nn.silu(conv_causal(frames, conv_fine, C1)).astype(jnp.bfloat16)
    frame_pairs = fine_out.astype(jnp.float32).reshape(FRAMES // 2, 2, ROWS, COLS, C1)
    pooled = ((frame_pairs[:, 0] + frame_pairs[:, 1]) * 0.5).astype(jnp.bfloat16)
    padded = jnp.pad(pooled, ((0, 0), (0, 1), (0, 1), (0, 0)))
    kernel = conv_down.reshape(3, 3, C1, C2)
    reduced = lax.conv_general_dilated(padded, kernel, (2, 2), "VALID", dimension_numbers=("NHWC", "HWIO", "NHWC"), preferred_element_type=jnp.float32).astype(jnp.bfloat16)
    coarse_out = jax.nn.silu(conv_causal(reduced, conv_coarse, C2)).astype(jnp.bfloat16)
    return coarse_out
```

```python
import functools

import jax
import jax.numpy as jnp
from jax import lax
from jax.experimental import pallas as pl
from jax.experimental.pallas import tpu as pltpu
from jax.sharding import PartitionSpec as P

F32 = jnp.float32
BF16 = jnp.bfloat16


def moved(value, steps, hop):
    tm, rows = lax.axis_size("tm"), lax.axis_size("rows")
    pairs = [
        (t * rows + r, (t + steps) * rows + r + hop)
        for t in range(tm - steps)
        for r in range(rows)
        if 0 <= r + hop < rows
    ]
    return lax.ppermute(value, ("tm", "rows"), pairs)


def swapped(value, steps):
    tm = lax.axis_size("tm")
    pairs = [(t * 2 + r, (t + steps) * 2 + 1 - r) for t in range(tm - steps) for r in range(2)]
    return lax.ppermute(value, ("tm", "rows"), pairs)


def rims(cells, dim, above, below, steps):
    count = cells.shape[dim]
    if lax.axis_size("rows") == 2:
        width = max(above, below)
        first = jnp.where(lax.axis_index("rows") == 0, count - width, 0)
        both = swapped(lax.dynamic_slice_in_dim(cells, first, width, axis=dim), steps)
        return both, both
    head = lax.slice_in_dim(cells, 0, below, axis=dim)
    tail = lax.slice_in_dim(cells, count - above, count, axis=dim)
    return moved(tail, steps, 1), moved(head, steps, -1)


def shifted_columns(flat, cols):
    wide = flat.astype(F32)
    column = lax.broadcasted_iota(jnp.int32, wide.shape, 0) % cols
    left = jnp.where(column == 0, 0.0, pltpu.roll(wide, 1, 0))
    right = jnp.where(column == cols - 1, 0.0, pltpu.roll(wide, wide.shape[0] - 1, 0))
    return left.astype(BF16), right.astype(BF16)


def put_taps(taps, first, lanes, flat, cols):
    channels = flat.shape[1]
    left, right = shifted_columns(flat, cols)
    size = flat.shape[0]
    for tap, part in enumerate((left, flat, right)):
        taps[first : first + size, lanes + tap * channels : lanes + (tap + 1) * channels] = part


def fill_fine(edges, frames, above, below, taps):
    frame_count, rows, cols, channels = frames.shape
    for f in range(frame_count):
        lanes = f * 3 * channels
        top = above[f, above.shape[1] - 1]
        top = jnp.where(edges[0] != 0, top, jnp.zeros_like(top))
        put_taps(taps, 0, lanes, top, cols)
        put_taps(taps, cols, lanes, frames[f].reshape(rows * cols, channels), cols)
        low = below[f, 0:2].reshape(2 * cols, channels)
        low = jnp.where(edges[1] != 0, low, jnp.zeros_like(low))
        put_taps(taps, (rows + 1) * cols, lanes, low, cols)


def fine_sum(taps, weight, first_tap, size, cols):
    total = None
    for b in range(3):
        zero = jnp.zeros_like(weight[0, b])
        pick = lambda tap: weight[tap, b] if 0 <= tap <= 2 else zero
        right = jnp.concatenate(
            [
                jnp.concatenate([pick(first_tap), pick(first_tap - 1)], axis=1),
                jnp.concatenate([pick(first_tap + 1), pick(first_tap)], axis=1),
            ],
            axis=0,
        )
        part = jnp.dot(taps[b * cols : b * cols + size], right, preferred_element_type=F32)
        total = part if total is None else total + part
    return total


def fine_own_kernel(edges, frames, above, below, weight, out, taps):
    cols = frames.shape[2]
    fill_fine(edges, frames, above, below, taps)
    out[...] = fine_sum(taps, weight, 2, out.shape[0], cols)


def silu(v):
    return v / (1.0 + jnp.exp(-v))


def fine_rest_kernel(edges, frames, above, below, weight, own, down, out, taps, pooled):
    _, rows, cols, channels = frames.shape
    fill_fine(edges, frames, above, below, taps)
    total = own[...] + fine_sum(taps, weight, 0, own.shape[0], cols)
    fine = silu(total).astype(BF16).astype(F32)
    mean = ((fine[:, :channels] + fine[:, channels:]) * 0.5).astype(BF16).astype(F32)
    pad = pooled.shape[1] - cols
    for r in range(rows + 1):
        row = mean[r * cols : (r + 1) * cols]
        if r == rows:
            row = jnp.where(edges[1] != 0, row, 0.0)
        pooled[r, 0:cols] = row
        pooled[r, cols : cols + pad] = jnp.zeros((pad, channels), F32)
    strips = []
    for p in range(rows // 2):
        pieces = [
            pooled[2 * p + b, pl.ds(e, cols // 2, stride=2), :].astype(BF16)
            for b in range(3)
            for e in range(3)
        ]
        strips.append(jnp.concatenate(pieces, axis=1))
    left = jnp.concatenate(strips, axis=0)
    right = down[...].reshape(-1, down.shape[-1])
    out[...] = jnp.dot(left, right, preferred_element_type=F32).astype(BF16).reshape(out.shape)


def coarse_kernel(edges, *refs):
    fields, weight, out, taps = refs[:9], refs[9], refs[10], refs[11]
    half_rows, half_cols, channels = fields[0].shape[1:]
    total = None
    for a in range(3):
        body, above, below = fields[3 * a : 3 * a + 3]
        top = above[0, 0]
        top = jnp.where(edges[0] != 0, top, jnp.zeros_like(top))
        low = below[0, 0]
        low = jnp.where(edges[1] != 0, low, jnp.zeros_like(low))
        flat = body[0].reshape(half_rows * half_cols, channels)
        put_taps(taps, 0, 0, top, half_cols)
        put_taps(taps, half_cols, 0, flat, half_cols)
        put_taps(taps, (half_rows + 1) * half_cols, 0, low, half_cols)
        for b in range(3):
            left = taps[b * half_cols : (b + half_rows) * half_cols]
            part = jnp.dot(left, weight[a, b], preferred_element_type=F32)
            total = part if total is None else total + part
    out[...] = silu(total).astype(BF16).reshape(out.shape)


def call(kernel, out_shape, scratch, flops, args):
    size = sum(a.size * a.dtype.itemsize for a in args)
    specs = [pl.BlockSpec(memory_space=pltpu.SMEM)]
    specs += [pl.BlockSpec(memory_space=pltpu.VMEM)] * (len(args) - 1)
    return pl.pallas_call(
        kernel,
        out_shape=out_shape,
        in_specs=specs,
        out_specs=pl.BlockSpec(memory_space=pltpu.VMEM),
        scratch_shapes=scratch,
        cost_estimate=pl.CostEstimate(flops=flops, bytes_accessed=size, transcendentals=0),
        compiler_params=pltpu.CompilerParams(vmem_limit_bytes=40 * 1024 * 1024),
    )(*args)


def local(frames, conv_fine, conv_down, conv_coarse):
    _, rows, cols, channels = frames.shape
    wide = conv_down.shape[-1]
    strip, strips = lax.axis_index("rows"), lax.axis_size("rows")
    edges = jnp.stack([strip > 0, strip < strips - 1]).astype(jnp.int32)

    earlier = moved(frames, 1, 0)
    above, below = rims(frames, 1, 1, 2, 0)
    above_1, below_1 = rims(frames, 1, 1, 2, 1)
    size = (rows + 1) * cols
    taps = pltpu.VMEM(((rows + 3) * cols, 6 * channels), BF16)
    flops = 2 * size * 18 * channels * 2 * channels
    own = call(
        fine_own_kernel,
        jax.ShapeDtypeStruct((size, 2 * channels), F32),
        [taps],
        flops,
        (edges, frames, above, below, conv_fine),
    )
    half_rows, half_cols = rows // 2, cols // 2
    reduced = call(
        fine_rest_kernel,
        jax.ShapeDtypeStruct((1, half_rows, half_cols, wide), BF16),
        [taps, pltpu.VMEM((rows + 1, cols + 8, channels), F32)],
        flops,
        (edges, earlier, above_1, below_1, conv_fine, own, conv_down),
    )
    back_2 = moved(reduced, 2, 0)
    back_1 = moved(reduced, 1, 0)
    fields = []
    for steps, body in ((2, back_2), (1, back_1), (0, reduced)):
        fields += [body, *rims(reduced, 1, 1, 1, steps)]
    return call(
        coarse_kernel,
        jax.ShapeDtypeStruct((1, half_rows, half_cols, wide), BF16),
        [pltpu.VMEM(((half_rows + 2) * half_cols, 3 * wide), BF16)],
        2 * half_rows * half_cols * 27 * wide * wide,
        (edges, *fields, conv_coarse),
    )


def solution(mesh):
    placed = (P("tm", "rows", None, None), P(), P(), P())
    return jax.shard_map(
        local, mesh=mesh, in_specs=placed, out_specs=P("tm", "rows", None, None), check_vma=False
    )
```

```python
import functools

import jax
import jax.numpy as jnp
from jax import lax
from jax.experimental import pallas as pl
from jax.experimental.pallas import tpu as pltpu
from jax.sharding import PartitionSpec as P

F32 = jnp.float32
BF16 = jnp.bfloat16


def moved(value, steps, hop):
    tm, rows = lax.axis_size("tm"), lax.axis_size("rows")
    pairs = [
        (t * rows + r, (t + steps) * rows + r + hop)
        for t in range(tm - steps)
        for r in range(rows)
        if 0 <= r + hop < rows
    ]
    return lax.ppermute(value, ("tm", "rows"), pairs)


def swapped(value, steps):
    tm = lax.axis_size("tm")
    pairs = [(t * 2 + r, (t + steps) * 2 + 1 - r) for t in range(tm - steps) for r in range(2)]
    return lax.ppermute(value, ("tm", "rows"), pairs)


def edge_kernel(cells, out, sem):
    width = out.shape[1]
    first = (1 - lax.axis_index("rows")) * (cells.shape[1] - width)
    copy = pltpu.make_async_copy(cells.at[:, pl.ds(first, width)], out, sem)
    copy.start()
    copy.wait()


def edge_rows(cells, width):
    return pl.pallas_call(
        edge_kernel,
        out_shape=jax.ShapeDtypeStruct((cells.shape[0], width, *cells.shape[2:]), cells.dtype),
        in_specs=[pl.BlockSpec(memory_space=pltpu.HBM)],
        out_specs=pl.BlockSpec(memory_space=pltpu.VMEM),
        scratch_shapes=[pltpu.SemaphoreType.DMA],
        cost_estimate=pl.CostEstimate(flops=4 * 10**9, bytes_accessed=1 << 20, transcendentals=0),
    )(cells)


def frame_rims(frames):
    rows = frames.shape[1]
    if lax.axis_size("rows") == 2:
        sent = edge_rows(frames, 2)
        return [(both, both) for both in (swapped(sent, 0), swapped(sent, 1))]
    head, tail = frames[:, :2], frames[:, rows - 1 :]
    return [(moved(tail, steps, 1), moved(head, steps, -1)) for steps in (0, 1)]


def shifted_columns(flat, cols):
    wide = flat.astype(F32)
    column = lax.broadcasted_iota(jnp.int32, wide.shape, 0) % cols
    left = jnp.where(column == 0, 0.0, pltpu.roll(wide, 1, 0))
    right = jnp.where(column == cols - 1, 0.0, pltpu.roll(wide, wide.shape[0] - 1, 0))
    return left.astype(BF16), right.astype(BF16)


def put_taps(taps, first, lanes, flat, cols):
    channels = flat.shape[1]
    left, right = shifted_columns(flat, cols)
    size = flat.shape[0]
    for tap, part in enumerate((left, flat, right)):
        taps[first : first + size, lanes + tap * channels : lanes + (tap + 1) * channels] = part


def fill_fine(edges, frames, above, below, taps):
    frame_count, rows, cols, channels = frames.shape
    for f in range(frame_count):
        lanes = f * 3 * channels
        top = above[f, above.shape[1] - 1]
        top = jnp.where(edges[0] != 0, top, jnp.zeros_like(top))
        put_taps(taps, 0, lanes, top, cols)
        put_taps(taps, cols, lanes, frames[f].reshape(rows * cols, channels), cols)
        low = below[f, 0:2].reshape(2 * cols, channels)
        low = jnp.where(edges[1] != 0, low, jnp.zeros_like(low))
        put_taps(taps, (rows + 1) * cols, lanes, low, cols)


def fine_sum(taps, weight, first_tap, size, cols):
    total = None
    for b in range(3):
        zero = jnp.zeros_like(weight[0, b])
        pick = lambda tap: weight[tap, b] if 0 <= tap <= 2 else zero
        right = jnp.concatenate(
            [
                jnp.concatenate([pick(first_tap), pick(first_tap - 1)], axis=1),
                jnp.concatenate([pick(first_tap + 1), pick(first_tap)], axis=1),
            ],
            axis=0,
        )
        part = jnp.dot(taps[b * cols : b * cols + size], right, preferred_element_type=F32)
        total = part if total is None else total + part
    return total


def fine_own_kernel(edges, frames, above, below, weight, out, taps):
    fill_fine(edges, frames, above, below, taps)
    out[...] = fine_sum(taps, weight, 2, out.shape[0], frames.shape[2])


def silu(v):
    return v / (1.0 + jnp.exp(-v))


def fine_rest_kernel(edges, frames, above, below, weight, own, down, out, taps, pooled):
    _, rows, cols, channels = frames.shape
    fill_fine(edges, frames, above, below, taps)
    total = own[...] + fine_sum(taps, weight, 0, own.shape[0], cols)
    fine = silu(total).astype(BF16).astype(F32)
    mean = ((fine[:, :channels] + fine[:, channels:]) * 0.5).astype(BF16).astype(F32)
    pad = pooled.shape[1] - cols
    for r in range(rows + 1):
        row = mean[r * cols : (r + 1) * cols]
        if r == rows:
            row = jnp.where(edges[1] != 0, row, 0.0)
        pooled[r, 0:cols] = row
        pooled[r, cols : cols + pad] = jnp.zeros((pad, channels), F32)
    strips = []
    for p in range(rows // 2):
        pieces = [
            pooled[2 * p + b, pl.ds(e, cols // 2, stride=2), :].astype(BF16)
            for b in range(3)
            for e in range(3)
        ]
        strips.append(jnp.concatenate(pieces, axis=1))
    left = jnp.concatenate(strips, axis=0)
    right = down[...].reshape(-1, down.shape[-1])
    out[...] = jnp.dot(left, right, preferred_element_type=F32).astype(BF16).reshape(out.shape)


def field_taps(field):
    _, rows, cols, channels = field.shape
    flat = field[0].reshape(rows * cols, channels)
    left, right = shifted_columns(flat, cols)
    return jnp.concatenate([left, flat, right], axis=1)


def rim_sum(edges, taps, weight, a, cols, both):
    size = taps.shape[0]
    dot = functools.partial(jnp.dot, preferred_element_type=F32)
    if both:
        return [dot(taps[:cols], weight[a, 2]), dot(taps[size - cols :], weight[a, 0])]
    row = jnp.where(edges[0] != 0, taps[:cols], taps[size - cols :])
    return [dot(row, weight[a, 2 * edges[0]])]


def body_sum(taps, weight, a, cols):
    size = taps.shape[0]
    dot = functools.partial(jnp.dot, preferred_element_type=F32)
    zero = jnp.zeros((cols, weight.shape[-1]), F32)
    upper = jnp.concatenate([zero, dot(taps[: size - cols], weight[a, 0])], axis=0)
    lower = jnp.concatenate([dot(taps[cols:], weight[a, 2]), zero], axis=0)
    return dot(taps, weight[a, 1]) + upper + lower


def coarse_own_kernel(edges, field, weight, body, rim):
    cols = field.shape[2]
    taps = field_taps(field)
    body[...] = body_sum(taps, weight, 2, cols)
    for i, part in enumerate(rim_sum(edges, taps, weight, 2, cols, rim.shape[0] == 2)):
        rim[i] = part


def coarse_rim_kernel(edges, field_0, field_1, weight, own, out):
    cols = field_0.shape[2]
    sums = [own[i] for i in range(own.shape[0])]
    for a, field in enumerate((field_0, field_1)):
        parts = rim_sum(edges, field_taps(field), weight, a, cols, own.shape[0] == 2)
        sums = [x + y for x, y in zip(sums, parts)]
    for i, x in enumerate(sums):
        out[i] = x.astype(BF16)


def coarse_body_kernel(edges, field_0, field_1, weight, own, out):
    cols = field_0.shape[2]
    total = own[...]
    for a, field in enumerate((field_0, field_1)):
        total = total + body_sum(field_taps(field), weight, a, cols)
    out[...] = total


def finish_kernel(edges, total, above, below, out):
    _, rows, cols, channels = out.shape
    for p in range(rows):
        row = total[p * cols : (p + 1) * cols]
        if p == 0:
            row = row + jnp.where(edges[0] != 0, above[0].astype(F32), 0.0)
        if p == rows - 1:
            row = row + jnp.where(edges[1] != 0, below[0].astype(F32), 0.0)
        out[0, p] = silu(row).astype(BF16)


def call(kernel, out_shape, scratch, flops, args):
    size = sum(a.size * a.dtype.itemsize for a in args)
    specs = [pl.BlockSpec(memory_space=pltpu.SMEM)]
    specs += [pl.BlockSpec(memory_space=pltpu.VMEM)] * (len(args) - 1)
    return pl.pallas_call(
        kernel,
        out_shape=out_shape,
        in_specs=specs,
        out_specs=jax.tree.map(lambda _: pl.BlockSpec(memory_space=pltpu.VMEM), out_shape),
        scratch_shapes=scratch,
        cost_estimate=pl.CostEstimate(flops=flops, bytes_accessed=size, transcendentals=0),
        compiler_params=pltpu.CompilerParams(vmem_limit_bytes=40 * 1024 * 1024),
    )(*args)


def local(frames, conv_fine, conv_down, conv_coarse):
    _, rows, cols, channels = frames.shape
    wide = conv_down.shape[-1]
    strip, strips = lax.axis_index("rows"), lax.axis_size("rows")
    edges = jnp.stack([strip > 0, strip < strips - 1]).astype(jnp.int32)

    earlier = moved(frames, 1, 0)
    (above, below), (above_1, below_1) = frame_rims(frames)
    size = (rows + 1) * cols
    taps = pltpu.VMEM(((rows + 3) * cols, 6 * channels), BF16)
    flops = 2 * size * 18 * channels * 2 * channels
    own = call(
        fine_own_kernel,
        jax.ShapeDtypeStruct((size, 2 * channels), F32),
        [taps],
        flops,
        (edges, frames, above, below, conv_fine),
    )
    half_rows, half_cols = rows // 2, cols // 2
    field = jax.ShapeDtypeStruct((1, half_rows, half_cols, wide), BF16)
    reduced = call(
        fine_rest_kernel,
        field,
        [taps, pltpu.VMEM((rows + 1, cols + 8, channels), F32)],
        flops,
        (edges, earlier, above_1, below_1, conv_fine, own, conv_down),
    )
    back_2 = moved(reduced, 2, 0)
    back_1 = moved(reduced, 1, 0)
    sums = jax.ShapeDtypeStruct((half_rows * half_cols, wide), F32)
    sides = 1 if strips == 2 else 2
    flops = 2 * half_rows * half_cols * 9 * wide * wide
    own_sum, own_rim = call(
        coarse_own_kernel,
        (sums, jax.ShapeDtypeStruct((sides, half_cols, wide), F32)),
        [],
        flops,
        (edges, reduced, conv_coarse),
    )
    rim = call(
        coarse_rim_kernel,
        jax.ShapeDtypeStruct((sides, half_cols, wide), BF16),
        [],
        flops // 4,
        (edges, back_2, back_1, conv_coarse, own_rim),
    )
    if sides == 1:
        from_above = from_below = swapped(rim, 0)
    else:
        from_above, from_below = moved(rim[1:], 0, 1), moved(rim[:1], 0, -1)
    total = call(
        coarse_body_kernel, sums, [], 2 * flops, (edges, back_2, back_1, conv_coarse, own_sum)
    )
    return call(finish_kernel, field, [], sums.size, (edges, total, from_above, from_below))


def solution(mesh):
    placed = (P("tm", "rows", None, None), P(), P(), P())
    return jax.shard_map(
        local, mesh=mesh, in_specs=placed, out_specs=P("tm", "rows", None, None), check_vma=False
    )
```

```python
import functools

import jax
import jax.numpy as jnp
from jax import lax
from jax.experimental import pallas as pl
from jax.experimental.pallas import tpu as pltpu
from jax.sharding import PartitionSpec as P

F32 = jnp.float32
BF16 = jnp.bfloat16


def moved(value, steps, hop):
    tm, rows = lax.axis_size("tm"), lax.axis_size("rows")
    pairs = [
        (t * rows + r, (t + steps) * rows + r + hop)
        for t in range(tm - steps)
        for r in range(rows)
        if 0 <= r + hop < rows
    ]
    return lax.ppermute(value, ("tm", "rows"), pairs)


def swapped(value, steps):
    tm = lax.axis_size("tm")
    pairs = [(t * 2 + r, (t + steps) * 2 + 1 - r) for t in range(tm - steps) for r in range(2)]
    return lax.ppermute(value, ("tm", "rows"), pairs)


def paired(value, step):
    tm, rows = lax.axis_size("tm"), lax.axis_size("rows")
    start = 0 if step > 0 else 1
    pairs = [(t * rows + r, (t + step) * rows + r) for t in range(start, tm, 2) for r in range(rows)]
    return lax.ppermute(value, ("tm", "rows"), pairs)


def place_kernel(out):
    strip = lax.axis_index("rows")
    out[0] = (strip > 0).astype(jnp.int32)
    out[1] = (strip < lax.axis_size("rows") - 1).astype(jnp.int32)
    out[2] = lax.axis_index("tm") % 2


def edge_kernel(edges, cells, out):
    width = out.shape[1]
    out[...] = cells[:, pl.ds(edges[1] * (cells.shape[1] - width), width)]


def frame_rims(edges, frames):
    rows = frames.shape[1]
    if lax.axis_size("rows") == 2:
        sent = call(
            edge_kernel,
            jax.ShapeDtypeStruct((frames.shape[0], 2, *frames.shape[2:]), BF16),
            [],
            0,
            (edges, frames),
        )
        return [(both, both) for both in (swapped(sent, 0), swapped(sent, 1))]
    head, tail = frames[:, :2], frames[:, rows - 1 :]
    return [(moved(tail, steps, 1), moved(head, steps, -1)) for steps in (0, 1)]


def column_shift(value, cols, steps):
    size = value.shape[0]
    column = lax.broadcasted_iota(jnp.int32, value.shape, 0) % cols
    edge = 0 if steps > 0 else cols - 1
    return jnp.where(column == edge, 0.0, pltpu.roll(value, steps % size, 0))


def shifted_columns(flat, cols):
    wide = flat.astype(F32)
    return column_shift(wide, cols, 1).astype(BF16), column_shift(wide, cols, -1).astype(BF16)


def tap_matrix(weight, first_tap, row_taps, e, channels):
    zero = jnp.zeros((channels, channels), BF16)

    def pick(tap, b):
        return weight[tap, b, e * channels : (e + 1) * channels] if 0 <= tap <= 2 else zero

    return jnp.concatenate(
        [
            jnp.concatenate([pick(first_tap + f, b), pick(first_tap + f - 1, b)], axis=1)
            for f in range(2)
            for b in row_taps
        ],
        axis=0,
    )


def fine_rows(row, outs, row_taps, weight, first_tap):
    channels = weight.shape[-1]
    some = next(x for f in range(2) for r in outs for b in row_taps if (x := row(f, r - 1 + b)) is not None)
    cols = some.shape[0]
    zero = jnp.zeros((cols, channels), BF16)

    def cell(f, i):
        found = row(f, i)
        return zero if found is None else found

    left = jnp.concatenate(
        [
            jnp.concatenate([cell(f, r - 1 + b) for f in range(2) for b in row_taps], axis=1)
            for r in outs
        ],
        axis=0,
    )
    sums = [
        jnp.dot(
            left, tap_matrix(weight, first_tap, row_taps, e, channels), preferred_element_type=F32
        )
        for e in range(3)
    ]
    return sums[1] + column_shift(sums[0], cols, 1) + column_shift(sums[2], cols, -1)


def chunks_of(count):
    size = next(c for c in (3, 2, 1) if count % c == 0)
    return [range(i, i + size) for i in range(0, count, size)]


def fine_own_kernel(frames, weight, out):
    _, rows, cols, _ = frames.shape

    def row(f, i):
        return frames[f, i] if 0 <= i < rows else None

    for outs in chunks_of(rows + 1):
        out[outs[0] * cols : (outs[-1] + 1) * cols] = fine_rows(row, outs, range(3), weight, 2)


def halo_row(edges, above, below, rows):
    def row(f, i):
        if i == -1:
            cells, have = above[f, above.shape[1] - 1], edges[0]
        elif i >= rows:
            cells, have = below[f, i - rows], edges[1]
        else:
            return None
        return jnp.where(have != 0, cells, jnp.zeros_like(cells))

    return row


def fine_halo_kernel(edges, above, below, weight, out, *, rows):
    cols = above.shape[2]
    row = halo_row(edges, above, below, rows)
    out[:cols] = fine_rows(row, [0], [0], weight, 2)
    out[cols:] = fine_rows(row, [rows - 1, rows], [1, 2], weight, 2)


def silu(v):
    return v / (1.0 + jnp.exp(-v))


def fine_rest_kernel(edges, frames, above, below, weight, own, halo, down, out, pooled):
    _, rows, cols, channels = frames.shape
    outside = halo_row(edges, above, below, rows)

    def row(f, i):
        return frames[f, i] if 0 <= i < rows else outside(f, i)

    pad = pooled.shape[1] - cols
    pooled[:, cols:] = jnp.zeros((rows + 1, pad, channels), F32)
    for outs in chunks_of(rows + 1):
        total = fine_rows(row, outs, range(3), weight, 0)
        for i, r in enumerate(outs):
            line = total[i * cols : (i + 1) * cols] + own[r * cols : (r + 1) * cols]
            for k, halo_r in enumerate((0, rows - 1, rows)):
                if r == halo_r:
                    line = line + halo[k * cols : (k + 1) * cols]
            fine = silu(line).astype(BF16).astype(F32)
            mean = ((fine[:, :channels] + fine[:, channels:]) * 0.5).astype(BF16).astype(F32)
            if r == rows:
                mean = jnp.where(edges[1] != 0, mean, 0.0)
            pooled[r, :cols] = mean
    strips = []
    for p in range(rows // 2):
        pieces = [
            pooled[2 * p + b, pl.ds(e, cols // 2, stride=2), :].astype(BF16)
            for b in range(3)
            for e in range(3)
        ]
        strips.append(jnp.concatenate(pieces, axis=1))
    left = jnp.concatenate(strips, axis=0)
    right = down[...].reshape(-1, down.shape[-1])
    out[...] = jnp.dot(left, right, preferred_element_type=F32).astype(BF16).reshape(out.shape)


def field_taps(field):
    _, rows, cols, channels = field.shape
    flat = field[0].reshape(rows * cols, channels)
    left, right = shifted_columns(flat, cols)
    return jnp.concatenate([left, flat, right], axis=1)


def rim_sum(edges, taps, weight, a, cols, both):
    size = taps.shape[0]
    dot = functools.partial(jnp.dot, preferred_element_type=F32)
    if both:
        return [dot(taps[:cols], weight[a, 2]), dot(taps[size - cols :], weight[a, 0])]
    row = jnp.where(edges[0] != 0, taps[:cols], taps[size - cols :])
    return [dot(row, weight[a, 2 * edges[0]])]


def body_sum(taps, weight, a, cols):
    size = taps.shape[0]
    dot = functools.partial(jnp.dot, preferred_element_type=F32)
    zero = jnp.zeros((cols, weight.shape[-1]), F32)
    upper = jnp.concatenate([zero, dot(taps[: size - cols], weight[a, 0])], axis=0)
    lower = jnp.concatenate([dot(taps[cols:], weight[a, 2]), zero], axis=0)
    return dot(taps, weight[a, 1]) + upper + lower


def coarse_first_kernel(edges, field, weight, body, rim):
    taps = field_taps(field)
    cols = field.shape[2]
    body[...] = body_sum(taps, weight, 2, cols)
    for i, part in enumerate(rim_sum(edges, taps, weight, 2, cols, rim.shape[0] == 2)):
        rim[i] = part


def coarse_next_kernel(edges, field, weight, body_in, rim_in, body, rim):
    taps = field_taps(field)
    cols = field.shape[2]
    body[...] = body_in[...] + body_sum(taps, weight, 0, cols)
    for i, part in enumerate(rim_sum(edges, taps, weight, 0, cols, rim.shape[0] == 2)):
        rim[i] = rim_in[i] + part


def middle_taps(edges, direct, relayed):
    field = jnp.where(edges[2] != 0, direct[...], relayed[...])
    return field_taps(field)


def coarse_rim_kernel(edges, direct, relayed, weight, rim, out):
    cols = direct.shape[2]
    taps = middle_taps(edges, direct, relayed)
    for i, part in enumerate(rim_sum(edges, taps, weight, 1, cols, rim.shape[0] == 2)):
        out[i] = (rim[i] + part).astype(BF16)


def coarse_last_kernel(edges, direct, relayed, weight, body, out):
    cols = direct.shape[2]
    taps = middle_taps(edges, direct, relayed)
    out[...] = body[...] + body_sum(taps, weight, 1, cols)


def finish_kernel(edges, total, above, below, out):
    _, rows, cols, channels = out.shape
    for p in range(rows):
        row = total[p * cols : (p + 1) * cols]
        if p == 0:
            row = row + jnp.where(edges[0] != 0, above[0].astype(F32), 0.0)
        if p == rows - 1:
            row = row + jnp.where(edges[1] != 0, below[0].astype(F32), 0.0)
        out[0, p] = silu(row).astype(BF16)


def call(kernel, out_shape, scratch, flops, args):
    size = sum(a.size * a.dtype.itemsize for a in args)
    specs = [
        pl.BlockSpec(memory_space=pltpu.SMEM if a.ndim == 1 else pltpu.VMEM) for a in args
    ]
    return pl.pallas_call(
        kernel,
        out_shape=out_shape,
        in_specs=specs,
        out_specs=jax.tree.map(lambda _: pl.BlockSpec(memory_space=pltpu.VMEM), out_shape),
        scratch_shapes=scratch,
        cost_estimate=pl.CostEstimate(flops=flops, bytes_accessed=size, transcendentals=0),
        compiler_params=pltpu.CompilerParams(vmem_limit_bytes=20 * 1024 * 1024),
    )(*args)


def local(frames, conv_fine, conv_down, conv_coarse):
    _, rows, cols, channels = frames.shape
    wide = conv_down.shape[-1]
    strips, times = lax.axis_size("rows"), lax.axis_size("tm")
    edges = pl.pallas_call(
        place_kernel,
        out_shape=jax.ShapeDtypeStruct((3,), jnp.int32),
        out_specs=pl.BlockSpec(memory_space=pltpu.SMEM),
        cost_estimate=pl.CostEstimate(flops=4 * 10**9, bytes_accessed=1 << 20, transcendentals=0),
        compiler_params=pltpu.CompilerParams(vmem_limit_bytes=1024 * 1024),
    )()

    earlier = moved(frames, 1, 0)
    (above, below), (above_1, below_1) = frame_rims(edges, frames)
    size = (rows + 1) * cols
    pair = jax.ShapeDtypeStruct((size, 2 * channels), F32)
    flops = 2 * size * 18 * channels * 2 * channels
    own = call(fine_own_kernel, pair, [], flops, (frames, conv_fine))
    halo = call(
        functools.partial(fine_halo_kernel, rows=rows),
        jax.ShapeDtypeStruct((3 * cols, 2 * channels), F32),
        [],
        flops // 3,
        (edges, above, below, conv_fine),
    )
    half_rows, half_cols = rows // 2, cols // 2
    shape = jax.ShapeDtypeStruct((1, half_rows, half_cols, wide), BF16)
    field = call(
        fine_rest_kernel,
        shape,
        [pltpu.VMEM((rows + 1, cols + 8, channels), F32)],
        flops,
        (edges, earlier, above_1, below_1, conv_fine, own, halo, conv_down),
    )
    sides = 1 if strips == 2 else 2
    sums = jax.ShapeDtypeStruct((half_rows * half_cols, wide), F32)
    rims = jax.ShapeDtypeStruct((sides, half_cols, wide), F32)
    flops = 2 * half_rows * half_cols * 9 * wide * wide
    field_2 = moved(field, 2, 0)
    body, rim = call(coarse_first_kernel, (sums, rims), [], flops, (edges, field, conv_coarse))
    field_2, body, rim = lax.optimization_barrier((field_2, body, rim))
    if times % 2 == 0:
        direct = paired(field, 1)
        relayed = paired(field_2, -1)
    else:
        direct = relayed = moved(field, 1, 0)
    body, rim = call(
        coarse_next_kernel, (sums, rims), [], flops, (edges, field_2, conv_coarse, body, rim)
    )
    rim = call(
        coarse_rim_kernel,
        jax.ShapeDtypeStruct(rims.shape, BF16),
        [],
        flops // 4,
        (edges, direct, relayed, conv_coarse, rim),
    )
    if sides == 1:
        from_above = from_below = swapped(rim, 0)
    else:
        from_above, from_below = moved(rim[1:], 0, 1), moved(rim[:1], 0, -1)
    total = call(coarse_last_kernel, sums, [], flops, (edges, direct, relayed, conv_coarse, body))
    return call(finish_kernel, shape, [], sums.size, (edges, total, from_above, from_below))


def solution(mesh):
    placed = (P("tm", "rows", None, None), P(), P(), P())
    return jax.shard_map(
        local, mesh=mesh, in_specs=placed, out_specs=P("tm", "rows", None, None), check_vma=False
    )
```

```python
import functools

import jax
import jax.numpy as jnp
from jax import lax
from jax.experimental import pallas as pl
from jax.experimental.pallas import tpu as pltpu
from jax.sharding import PartitionSpec as P

F32 = jnp.float32
BF16 = jnp.bfloat16


def moved(value, steps, hop):
    tm, rows = lax.axis_size("tm"), lax.axis_size("rows")
    pairs = [
        (t * rows + r, (t + steps) * rows + r + hop)
        for t in range(tm - steps)
        for r in range(rows)
        if 0 <= r + hop < rows
    ]
    return lax.ppermute(value, ("tm", "rows"), pairs)


def ring(value, steps):
    tm = lax.axis_size("tm")
    return lax.ppermute(value, "tm", [(t, (t + steps) % tm) for t in range(tm)])


def swapped(value, steps):
    tm = lax.axis_size("tm")
    pairs = [(t * 2 + r, (t + steps) * 2 + 1 - r) for t in range(tm - steps) for r in range(2)]
    return lax.ppermute(value, ("tm", "rows"), pairs)


def paired(value):
    return lax.ppermute(value, "tm", [(t, t ^ 1) for t in range(lax.axis_size("tm"))])


def has_above():
    return lax.axis_index("rows") > 0


def has_below():
    return lax.axis_index("rows") < lax.axis_size("rows") - 1


def has_earlier(steps):
    return lax.axis_index("tm") >= steps


def pace_kernel(out):
    out[...] = jnp.zeros_like(out)


def edge_kernel(_, cells, out):
    width = out.shape[1]
    first = (1 - lax.axis_index("rows")) * (cells.shape[1] - width)
    out[...] = cells[:, pl.ds(first, width)]


def frame_rims(pace, frames):
    rows = frames.shape[1]
    if lax.axis_size("rows") == 2:
        sent = call(
            edge_kernel,
            jax.ShapeDtypeStruct((frames.shape[0], 2, *frames.shape[2:]), BF16),
            [],
            0,
            (pace, frames),
        )
        return [(both, both) for both in (swapped(sent, 0), swapped(sent, 1))]
    head, tail = frames[:, :2], frames[:, rows - 1 :]
    return [(moved(tail, steps, 1), moved(head, steps, -1)) for steps in (0, 1)]


def column_shift(value, cols, steps):
    size = value.shape[0]
    column = lax.broadcasted_iota(jnp.int32, value.shape, 0) % cols
    edge = 0 if steps > 0 else cols - 1
    return jnp.where(column == edge, 0.0, pltpu.roll(value, steps % size, 0))


def shifted_columns(flat, cols):
    wide = flat.astype(F32)
    return column_shift(wide, cols, 1).astype(BF16), column_shift(wide, cols, -1).astype(BF16)


def tap_matrix(weight, first_tap, row_taps, e, channels):
    zero = jnp.zeros((channels, channels), BF16)

    def pick(tap, b):
        return weight[tap, b, e * channels : (e + 1) * channels] if 0 <= tap <= 2 else zero

    return jnp.concatenate(
        [
            jnp.concatenate([pick(first_tap + f, b), pick(first_tap + f - 1, b)], axis=1)
            for f in range(2)
            for b in row_taps
        ],
        axis=0,
    )


def fine_rows(row, outs, row_taps, weight, first_tap):
    channels = weight.shape[-1]
    some = next(x for f in range(2) for r in outs for b in row_taps if (x := row(f, r - 1 + b)) is not None)
    cols = some.shape[0]
    zero = jnp.zeros((cols, channels), BF16)

    def cell(f, i):
        found = row(f, i)
        return zero if found is None else found

    left = jnp.concatenate(
        [
            jnp.concatenate([cell(f, r - 1 + b) for f in range(2) for b in row_taps], axis=1)
            for r in outs
        ],
        axis=0,
    )
    sums = [
        jnp.dot(
            left, tap_matrix(weight, first_tap, row_taps, e, channels), preferred_element_type=F32
        )
        for e in range(3)
    ]
    return sums[1] + column_shift(sums[0], cols, 1) + column_shift(sums[2], cols, -1)


def chunks_of(count):
    size = next(c for c in (3, 2, 1) if count % c == 0)
    return [range(i, i + size) for i in range(0, count, size)]


def fine_own_kernel(frames, weight, out):
    _, rows, cols, _ = frames.shape

    def row(f, i):
        return frames[f, i] if 0 <= i < rows else None

    for outs in chunks_of(rows + 1):
        out[outs[0] * cols : (outs[-1] + 1) * cols] = fine_rows(row, outs, range(3), weight, 2)


def halo_row(above, below, rows):
    def row(f, i):
        if i == -1:
            cells, have = above[f, above.shape[1] - 1], has_above()
        elif i >= rows:
            cells, have = below[f, i - rows], has_below()
        else:
            return None
        return jnp.where(have, cells, jnp.zeros_like(cells))

    return row


def fine_halo_kernel(above, below, weight, out, *, rows):
    cols = above.shape[2]
    row = halo_row(above, below, rows)
    out[:cols] = fine_rows(row, [0], [0], weight, 2)
    out[cols:] = fine_rows(row, [rows - 1, rows], [1, 2], weight, 2)


def silu(v):
    return v / (1.0 + jnp.exp(-v))


def fine_rest_kernel(frames, above, below, weight, own, halo, down, out, pooled):
    _, rows, cols, channels = frames.shape
    outside = halo_row(above, below, rows)

    def row(f, i):
        return frames[f, i] if 0 <= i < rows else outside(f, i)

    pad = pooled.shape[1] - cols
    pooled[:, cols:] = jnp.zeros((rows + 1, pad, channels), F32)
    for outs in chunks_of(rows + 1):
        total = fine_rows(row, outs, range(3), weight, 0)
        for i, r in enumerate(outs):
            line = jnp.where(has_earlier(1), total[i * cols : (i + 1) * cols], 0.0)
            line = line + own[r * cols : (r + 1) * cols]
            for k, halo_r in enumerate((0, rows - 1, rows)):
                if r == halo_r:
                    line = line + halo[k * cols : (k + 1) * cols]
            fine = silu(line).astype(BF16).astype(F32)
            mean = ((fine[:, :channels] + fine[:, channels:]) * 0.5).astype(BF16).astype(F32)
            if r == rows:
                mean = jnp.where(has_below(), mean, 0.0)
            pooled[r, :cols] = mean
    strips = []
    for p in range(rows // 2):
        pieces = [
            pooled[2 * p + b, pl.ds(e, cols // 2, stride=2), :].astype(BF16)
            for b in range(3)
            for e in range(3)
        ]
        strips.append(jnp.concatenate(pieces, axis=1))
    left = jnp.concatenate(strips, axis=0)
    right = down[...].reshape(-1, down.shape[-1])
    out[...] = jnp.dot(left, right, preferred_element_type=F32).astype(BF16).reshape(out.shape)


def field_taps(field):
    _, rows, cols, channels = field.shape
    flat = field.reshape(rows * cols, channels)
    left, right = shifted_columns(flat, cols)
    return jnp.concatenate([left, flat, right], axis=1)


def rim_sum(taps, weight, a, cols, both):
    size = taps.shape[0]
    dot = functools.partial(jnp.dot, preferred_element_type=F32)
    if both:
        return [dot(taps[:cols], weight[a, 2]), dot(taps[size - cols :], weight[a, 0])]
    row = jnp.where(has_above(), taps[:cols], taps[size - cols :])
    return [dot(row, weight[a, 2 * lax.axis_index("rows")])]


def body_sum(taps, weight, a, cols):
    size = taps.shape[0]
    dot = functools.partial(jnp.dot, preferred_element_type=F32)
    zero = jnp.zeros((cols, weight.shape[-1]), F32)
    upper = jnp.concatenate([zero, dot(taps[: size - cols], weight[a, 0])], axis=0)
    lower = jnp.concatenate([dot(taps[cols:], weight[a, 2]), zero], axis=0)
    return dot(taps, weight[a, 1]) + upper + lower


def coarse_first_kernel(field, weight, body, rim):
    taps = field_taps(field[...])
    cols = field.shape[2]
    body[...] = body_sum(taps, weight, 2, cols)
    for i, part in enumerate(rim_sum(taps, weight, 2, cols, rim.shape[0] == 2)):
        rim[i] = part


def coarse_next_kernel(field, weight, body_in, rim_in, body, rim):
    cells = field[...]
    taps = field_taps(jnp.where(has_earlier(2), cells, jnp.zeros_like(cells)))
    cols = field.shape[2]
    body[...] = body_in[...] + body_sum(taps, weight, 0, cols)
    for i, part in enumerate(rim_sum(taps, weight, 0, cols, rim.shape[0] == 2)):
        rim[i] = rim_in[i] + part


def middle_taps(direct, relayed):
    cells = jnp.where(lax.axis_index("tm") % 2 == 1, direct[...], relayed[...])
    return field_taps(jnp.where(has_earlier(1), cells, jnp.zeros_like(cells)))


def coarse_rim_kernel(direct, relayed, weight, rim, out):
    cols = direct.shape[2]
    taps = middle_taps(direct, relayed)
    for i, part in enumerate(rim_sum(taps, weight, 1, cols, rim.shape[0] == 2)):
        out[i] = (rim[i] + part).astype(BF16)


def coarse_last_kernel(direct, relayed, weight, body, out):
    cols = direct.shape[2]
    taps = middle_taps(direct, relayed)
    out[...] = body[...] + body_sum(taps, weight, 1, cols)


def finish_kernel(total, above, below, out):
    _, rows, cols, channels = out.shape
    for p in range(rows):
        row = total[p * cols : (p + 1) * cols]
        if p == 0:
            row = row + jnp.where(has_above(), above[0].astype(F32), 0.0)
        if p == rows - 1:
            row = row + jnp.where(has_below(), below[0].astype(F32), 0.0)
        out[0, p] = silu(row).astype(BF16)


def call(kernel, out_shape, scratch, flops, args):
    size = sum(a.size * a.dtype.itemsize for a in args)
    return pl.pallas_call(
        kernel,
        out_shape=out_shape,
        in_specs=[pl.BlockSpec(memory_space=pltpu.VMEM)] * len(args),
        out_specs=jax.tree.map(lambda _: pl.BlockSpec(memory_space=pltpu.VMEM), out_shape),
        scratch_shapes=scratch,
        cost_estimate=pl.CostEstimate(flops=flops, bytes_accessed=size, transcendentals=0),
        compiler_params=pltpu.CompilerParams(vmem_limit_bytes=20 * 1024 * 1024),
    )(*args)


def local(frames, conv_fine, conv_down, conv_coarse):
    _, rows, cols, channels = frames.shape
    wide = conv_down.shape[-1]
    strips, times = lax.axis_size("rows"), lax.axis_size("tm")
    pace = call(pace_kernel, jax.ShapeDtypeStruct((8, 128), F32), [], 4 * 10**9, ())

    earlier = ring(frames, 1)
    (above, below), (above_1, below_1) = frame_rims(pace, frames)
    size = (rows + 1) * cols
    pair = jax.ShapeDtypeStruct((size, 2 * channels), F32)
    flops = 2 * size * 18 * channels * 2 * channels
    own = call(fine_own_kernel, pair, [], flops, (frames, conv_fine))
    halo = call(
        functools.partial(fine_halo_kernel, rows=rows),
        jax.ShapeDtypeStruct((3 * cols, 2 * channels), F32),
        [],
        flops // 3,
        (above, below, conv_fine),
    )
    half_rows, half_cols = rows // 2, cols // 2
    shape = jax.ShapeDtypeStruct((1, half_rows, half_cols, wide), BF16)
    field = call(
        fine_rest_kernel,
        shape,
        [pltpu.VMEM((rows + 1, cols + 8, channels), F32)],
        flops,
        (earlier, above_1, below_1, conv_fine, own, halo, conv_down),
    )
    sides = 1 if strips == 2 else 2
    sums = jax.ShapeDtypeStruct((half_rows * half_cols, wide), F32)
    rims = jax.ShapeDtypeStruct((sides, half_cols, wide), F32)
    flops = 2 * half_rows * half_cols * 9 * wide * wide
    field_2 = ring(field, 2)
    body, rim = call(coarse_first_kernel, (sums, rims), [], flops, (field, conv_coarse))
    field_2, body, rim = lax.optimization_barrier((field_2, body, rim))
    if times % 2 == 0:
        direct, relayed = paired(field), paired(field_2)
    else:
        direct = relayed = moved(field, 1, 0)
    body, rim = call(
        coarse_next_kernel, (sums, rims), [], flops, (field_2, conv_coarse, body, rim)
    )
    rim = call(
        coarse_rim_kernel,
        jax.ShapeDtypeStruct(rims.shape, BF16),
        [],
        flops // 4,
        (direct, relayed, conv_coarse, rim),
    )
    if sides == 1:
        from_above = from_below = swapped(rim, 0)
    else:
        from_above, from_below = moved(rim[1:], 0, 1), moved(rim[:1], 0, -1)
    total = call(coarse_last_kernel, sums, [], flops, (direct, relayed, conv_coarse, body))
    return call(finish_kernel, shape, [], sums.size, (total, from_above, from_below))


def solution(mesh):
    placed = (P("tm", "rows", None, None), P(), P(), P())
    return jax.shard_map(
        local, mesh=mesh, in_specs=placed, out_specs=P("tm", "rows", None, None), check_vma=False
    )
```

```python
import functools

import jax
import jax.numpy as jnp
from jax import lax
from jax.experimental import pallas as pl
from jax.experimental.pallas import tpu as pltpu
from jax.sharding import PartitionSpec as P

F32 = jnp.float32
BF16 = jnp.bfloat16


def moved(value, steps, hop):
    tm, rows = lax.axis_size("tm"), lax.axis_size("rows")
    pairs = [
        (t * rows + r, (t + steps) * rows + r + hop)
        for t in range(tm - steps)
        for r in range(rows)
        if 0 <= r + hop < rows
    ]
    return lax.ppermute(value, ("tm", "rows"), pairs)


def ring(value, steps):
    tm = lax.axis_size("tm")
    return lax.ppermute(value, "tm", [(t, (t + steps) % tm) for t in range(tm)])


def swapped(value, steps):
    tm = lax.axis_size("tm")
    pairs = [(t * 2 + r, (t + steps) * 2 + 1 - r) for t in range(tm - steps) for r in range(2)]
    return lax.ppermute(value, ("tm", "rows"), pairs)


def paired(value):
    return lax.ppermute(value, "tm", [(t, t ^ 1) for t in range(lax.axis_size("tm"))])


def has_above():
    return lax.axis_index("rows") > 0


def has_below():
    return lax.axis_index("rows") < lax.axis_size("rows") - 1


def has_earlier(steps):
    return lax.axis_index("tm") >= steps


def pace_kernel(out):
    out[...] = jnp.zeros_like(out)


def edge_kernel(_, cells, out):
    width = out.shape[1]
    first = (1 - lax.axis_index("rows")) * (cells.shape[1] - width)
    out[...] = cells[:, pl.ds(first, width)]


def frame_rims(pace, frames):
    rows = frames.shape[1]
    if lax.axis_size("rows") == 2:
        sent = call(
            edge_kernel,
            jax.ShapeDtypeStruct((frames.shape[0], 2, *frames.shape[2:]), BF16),
            [],
            0,
            (pace, frames),
        )
        return [(both, both) for both in (swapped(sent, 0), swapped(sent, 1))]
    head, tail = frames[:, :2], frames[:, rows - 1 :]
    return [(moved(tail, steps, 1), moved(head, steps, -1)) for steps in (0, 1)]


def column_shift(value, cols, steps):
    size = value.shape[0]
    column = lax.broadcasted_iota(jnp.int32, value.shape, 0) % cols
    edge = 0 if steps > 0 else cols - 1
    return jnp.where(column == edge, 0.0, pltpu.roll(value, steps % size, 0))


def shifted_columns(flat, cols):
    wide = flat.astype(F32)
    return column_shift(wide, cols, 1).astype(BF16), column_shift(wide, cols, -1).astype(BF16)


def tap_matrix(weight, first_tap, row_taps, e, channels):
    zero = jnp.zeros((channels, channels), BF16)

    def pick(tap, b):
        return weight[tap, b, e * channels : (e + 1) * channels] if 0 <= tap <= 2 else zero

    return jnp.concatenate(
        [
            jnp.concatenate([pick(first_tap + f, b), pick(first_tap + f - 1, b)], axis=1)
            for f in range(2)
            for b in row_taps
        ],
        axis=0,
    )


def fine_rows(row, outs, row_taps, weight, first_tap):
    channels = weight.shape[-1]
    some = next(x for f in range(2) for r in outs for b in row_taps if (x := row(f, r - 1 + b)) is not None)
    cols = some.shape[0]
    zero = jnp.zeros((cols, channels), BF16)

    def cell(f, i):
        found = row(f, i)
        return zero if found is None else found

    left = jnp.concatenate(
        [
            jnp.concatenate([cell(f, r - 1 + b) for f in range(2) for b in row_taps], axis=1)
            for r in outs
        ],
        axis=0,
    )
    sums = [
        jnp.dot(
            left, tap_matrix(weight, first_tap, row_taps, e, channels), preferred_element_type=F32
        )
        for e in range(3)
    ]
    return sums[1] + column_shift(sums[0], cols, 1) + column_shift(sums[2], cols, -1)


def chunks_of(count):
    size = next(c for c in (3, 2, 1) if count % c == 0)
    return [range(i, i + size) for i in range(0, count, size)]


def fine_own_kernel(frames, weight, out):
    _, rows, cols, _ = frames.shape

    def row(f, i):
        return frames[f, i] if 0 <= i < rows else None

    for outs in chunks_of(rows + 1):
        out[outs[0] * cols : (outs[-1] + 1) * cols] = fine_rows(row, outs, range(3), weight, 2)


def halo_row(above, below, rows):
    def row(f, i):
        if i == -1:
            cells, have = above[f, above.shape[1] - 1], has_above()
        elif i >= rows:
            cells, have = below[f, i - rows], has_below()
        else:
            return None
        return jnp.where(have, cells, jnp.zeros_like(cells))

    return row


def fine_halo_kernel(above, below, weight, out, *, rows):
    cols = above.shape[2]
    row = halo_row(above, below, rows)
    out[:cols] = fine_rows(row, [0], [0], weight, 2)
    out[cols:] = fine_rows(row, [rows - 1, rows], [1, 2], weight, 2)


def silu(v):
    return v / (1.0 + jnp.exp(-v))


def fine_rest_kernel(frames, above, below, weight, own, halo, down, out, rim, pooled):
    _, rows, cols, channels = frames.shape
    outside = halo_row(above, below, rows)

    def row(f, i):
        return frames[f, i] if 0 <= i < rows else outside(f, i)

    pad = pooled.shape[1] - cols
    pooled[:, cols:] = jnp.zeros((rows + 1, pad, channels), F32)
    for outs in chunks_of(rows + 1):
        total = fine_rows(row, outs, range(3), weight, 0)
        for i, r in enumerate(outs):
            line = jnp.where(has_earlier(1), total[i * cols : (i + 1) * cols], 0.0)
            line = line + own[r * cols : (r + 1) * cols]
            for k, halo_r in enumerate((0, rows - 1, rows)):
                if r == halo_r:
                    line = line + halo[k * cols : (k + 1) * cols]
            fine = silu(line).astype(BF16).astype(F32)
            mean = ((fine[:, :channels] + fine[:, channels:]) * 0.5).astype(BF16).astype(F32)
            if r == rows:
                mean = jnp.where(has_below(), mean, 0.0)
            pooled[r, :cols] = mean
    strips = []
    for p in range(rows // 2):
        pieces = [
            pooled[2 * p + b, pl.ds(e, cols // 2, stride=2), :].astype(BF16)
            for b in range(3)
            for e in range(3)
        ]
        strips.append(jnp.concatenate(pieces, axis=1))
    left = jnp.concatenate(strips, axis=0)
    right = down[...].reshape(-1, down.shape[-1])
    reduced = jnp.dot(left, right, preferred_element_type=F32).astype(BF16)
    out[...] = reduced.reshape(out.shape)
    head, tail = reduced[: cols // 2], reduced[reduced.shape[0] - cols // 2 :]
    if rim.shape[0] == 1:
        rim[0] = jnp.where(has_above(), head, tail)
    else:
        rim[0], rim[1] = head, tail


def coarse_sum(field, rim, weight, a):
    _, rows, cols, channels = field.shape
    zero = jnp.zeros((cols, channels), BF16)
    flat = jnp.concatenate(
        [
            jnp.where(has_above(), rim[0], zero),
            field.reshape(rows * cols, channels),
            jnp.where(has_below(), rim[rim.shape[0] - 1], zero),
        ],
        axis=0,
    )
    left, right = shifted_columns(flat, cols)
    taps = jnp.concatenate([left, flat, right], axis=1)
    total = None
    for b in range(3):
        part = jnp.dot(
            taps[b * cols : (b + rows) * cols], weight[a, b], preferred_element_type=F32
        )
        total = part if total is None else total + part
    return total


def coarse_first_kernel(field, rim, weight, out):
    out[...] = coarse_sum(field[...], rim[...], weight, 2)


def coarse_next_kernel(field, rim, weight, total, out):
    part = coarse_sum(field[...], rim[...], weight, 0)
    out[...] = total[...] + jnp.where(has_earlier(2), part, 0.0)


def coarse_last_kernel(direct, direct_rim, relayed, relayed_rim, weight, total, out):
    odd = lax.axis_index("tm") % 2 == 1
    field = jnp.where(odd, direct[...], relayed[...])
    rim = jnp.where(odd, direct_rim[...], relayed_rim[...])
    part = coarse_sum(field, rim, weight, 1)
    total = total[...] + jnp.where(has_earlier(1), part, 0.0)
    out[...] = silu(total).astype(BF16).reshape(out.shape)


def call(kernel, out_shape, scratch, flops, args):
    size = sum(a.size * a.dtype.itemsize for a in args)
    return pl.pallas_call(
        kernel,
        out_shape=out_shape,
        in_specs=[pl.BlockSpec(memory_space=pltpu.VMEM)] * len(args),
        out_specs=jax.tree.map(lambda _: pl.BlockSpec(memory_space=pltpu.VMEM), out_shape),
        scratch_shapes=scratch,
        cost_estimate=pl.CostEstimate(flops=flops, bytes_accessed=size, transcendentals=0),
        compiler_params=pltpu.CompilerParams(vmem_limit_bytes=20 * 1024 * 1024),
    )(*args)


def local(frames, conv_fine, conv_down, conv_coarse):
    _, rows, cols, channels = frames.shape
    wide = conv_down.shape[-1]
    strips, times = lax.axis_size("rows"), lax.axis_size("tm")
    pace = call(pace_kernel, jax.ShapeDtypeStruct((8, 128), F32), [], 4 * 10**9, ())

    earlier = ring(frames, 1)
    (above, below), (above_1, below_1) = frame_rims(pace, frames)
    size = (rows + 1) * cols
    pair = jax.ShapeDtypeStruct((size, 2 * channels), F32)
    flops = 2 * size * 18 * channels * 2 * channels
    own = call(fine_own_kernel, pair, [], flops, (frames, conv_fine))
    halo = call(
        functools.partial(fine_halo_kernel, rows=rows),
        jax.ShapeDtypeStruct((3 * cols, 2 * channels), F32),
        [],
        flops // 3,
        (above, below, conv_fine),
    )
    half_rows, half_cols = rows // 2, cols // 2
    shape = jax.ShapeDtypeStruct((1, half_rows, half_cols, wide), BF16)
    sides = 1 if strips == 2 else 2
    field, ends = call(
        fine_rest_kernel,
        (shape, jax.ShapeDtypeStruct((sides, half_cols, wide), BF16)),
        [pltpu.VMEM((rows + 1, cols + 8, channels), F32)],
        flops,
        (earlier, above_1, below_1, conv_fine, own, halo, conv_down),
    )
    field_2 = ring(field, 2)
    if sides == 1:
        rim = swapped(ends, 0)
    else:
        rim = jnp.concatenate([moved(ends[1:], 0, 1), moved(ends[:1], 0, -1)], axis=0)
    rim_2 = ring(rim, 2)
    sums = jax.ShapeDtypeStruct((half_rows * half_cols, wide), F32)
    flops = 2 * half_rows * half_cols * 9 * wide * wide
    total = call(coarse_first_kernel, sums, [], flops, (field, rim, conv_coarse))
    if times % 2 == 0:
        direct, direct_rim = paired(field), paired(rim)
    else:
        direct, direct_rim = ring(field, 1), ring(rim, 1)
    field_2, rim_2, total, direct, direct_rim = lax.optimization_barrier(
        (field_2, rim_2, total, direct, direct_rim)
    )
    if times % 2 == 0:
        relayed, relayed_rim = paired(field_2), paired(rim_2)
    else:
        relayed, relayed_rim = direct, direct_rim
    total = call(coarse_next_kernel, sums, [], flops, (field_2, rim_2, conv_coarse, total))
    return call(
        coarse_last_kernel,
        shape,
        [],
        flops,
        (direct, direct_rim, relayed, relayed_rim, conv_coarse, total),
    )


def solution(mesh):
    placed = (P("tm", "rows", None, None), P(), P(), P())
    return jax.shard_map(
        local, mesh=mesh, in_specs=placed, out_specs=P("tm", "rows", None, None), check_vma=False
    )
```

```python
import functools

import jax
import jax.numpy as jnp
from jax import lax
from jax.experimental import pallas as pl
from jax.experimental.pallas import tpu as pltpu
from jax.sharding import PartitionSpec as P


F32 = jnp.float32
BF16 = jnp.bfloat16


def moved(value, steps, hop):
    tm, rows = lax.axis_size("tm"), lax.axis_size("rows")
    pairs = [
        (t * rows + r, (t + steps) * rows + r + hop)
        for t in range(tm - steps)
        for r in range(rows)
        if 0 <= r + hop < rows
    ]
    return lax.ppermute(value, ("tm", "rows"), pairs)


def ring(value, steps):
    tm = lax.axis_size("tm")
    return lax.ppermute(value, "tm", [(t, (t + steps) % tm) for t in range(tm)])


def swapped(value, steps):
    tm = lax.axis_size("tm")
    pairs = [(t * 2 + r, (t + steps) * 2 + 1 - r) for t in range(tm - steps) for r in range(2)]
    return lax.ppermute(value, ("tm", "rows"), pairs)


def paired(value):
    return lax.ppermute(value, "tm", [(t, t ^ 1) for t in range(lax.axis_size("tm"))])


def has_above():
    return lax.axis_index("rows") > 0


def has_below():
    return lax.axis_index("rows") < lax.axis_size("rows") - 1


def has_earlier(steps):
    return lax.axis_index("tm") >= steps


def pace_kernel(out):
    out[...] = jnp.zeros_like(out)


def edge_kernel(_, cells, out):
    width = out.shape[1]
    first = (1 - lax.axis_index("rows")) * (cells.shape[1] - width)
    out[...] = cells[:, pl.ds(first, width)]


def frame_rims(pace, frames):
    rows = frames.shape[1]
    if lax.axis_size("rows") == 2:
        sent = call(
            edge_kernel,
            jax.ShapeDtypeStruct((frames.shape[0], 2, *frames.shape[2:]), BF16),
            [],
            0,
            (pace, frames),
        )
        return [(both, both) for both in (swapped(sent, 0), swapped(sent, 1))]
    head, tail = frames[:, :2], frames[:, rows - 1 :]
    return [(moved(tail, steps, 1), moved(head, steps, -1)) for steps in (0, 1)]


def column_shift(value, cols, steps):
    size = value.shape[0]
    column = lax.broadcasted_iota(jnp.int32, value.shape, 0) % cols
    edge = 0 if steps > 0 else cols - 1
    return jnp.where(column == edge, 0.0, pltpu.roll(value, steps % size, 0))


def shifted_columns(flat, cols):
    wide = flat.astype(F32)
    return column_shift(wide, cols, 1).astype(BF16), column_shift(wide, cols, -1).astype(BF16)


def tap_matrix(weight, first_tap, row_taps, e, channels):
    zero = jnp.zeros((channels, channels), BF16)

    def pick(tap, b):
        return weight[tap, b, e * channels : (e + 1) * channels] if 0 <= tap <= 2 else zero

    return jnp.concatenate(
        [
            jnp.concatenate([pick(first_tap + f, b), pick(first_tap + f - 1, b)], axis=1)
            for f in range(2)
            for b in row_taps
        ],
        axis=0,
    )


def fine_rows(row, outs, row_taps, weight, first_tap):
    channels = weight.shape[-1]
    some = next(x for f in range(2) for r in outs for b in row_taps if (x := row(f, r - 1 + b)) is not None)
    cols = some.shape[0]
    zero = jnp.zeros((cols, channels), BF16)

    def cell(f, i):
        found = row(f, i)
        return zero if found is None else found

    left = jnp.concatenate(
        [
            jnp.concatenate([cell(f, r - 1 + b) for f in range(2) for b in row_taps], axis=1)
            for r in outs
        ],
        axis=0,
    )
    sums = [
        jnp.dot(
            left, tap_matrix(weight, first_tap, row_taps, e, channels), preferred_element_type=F32
        )
        for e in range(3)
    ]
    return sums[1] + column_shift(sums[0], cols, 1) + column_shift(sums[2], cols, -1)


def chunks_of(count):
    size = next(c for c in (3, 2, 1) if count % c == 0)
    return [range(i, i + size) for i in range(0, count, size)]


def fine_own_kernel(frames, weight, out):
    _, rows, cols, _ = frames.shape

    def row(f, i):
        return frames[f, i] if 0 <= i < rows else None

    for outs in chunks_of(rows + 1):
        out[outs[0] * cols : (outs[-1] + 1) * cols] = fine_rows(row, outs, range(3), weight, 2)


def halo_row(above, below, rows):
    def row(f, i):
        if i == -1:
            cells, have = above[f, above.shape[1] - 1], has_above()
        elif i >= rows:
            cells, have = below[f, i - rows], has_below()
        else:
            return None
        return jnp.where(have, cells, jnp.zeros_like(cells))

    return row


def halo_sum(above, below, weight, first_tap, rows):
    row = halo_row(above, below, rows)
    return jnp.concatenate(
        [
            fine_rows(row, [0], [0], weight, first_tap),
            fine_rows(row, [rows - 1, rows], [1, 2], weight, first_tap),
        ],
        axis=0,
    )


def fine_halo_kernel(above, below, weight, out, *, rows):
    out[...] = halo_sum(above, below, weight, 2, rows)


def silu(v):
    return v / (1.0 + jnp.exp(-v))


def fine_rest_kernel(frames, weight, own, halo, out):
    _, rows, cols, _ = frames.shape

    def row(f, i):
        return frames[f, i] if 0 <= i < rows else None

    for outs in chunks_of(rows + 1):
        total = jnp.where(has_earlier(1), fine_rows(row, outs, range(3), weight, 0), 0.0)
        for i, r in enumerate(outs):
            line = total[i * cols : (i + 1) * cols] + own[r * cols : (r + 1) * cols]
            for k, halo_r in enumerate((0, rows - 1, rows)):
                if r == halo_r:
                    line = line + halo[k * cols : (k + 1) * cols]
            out[r * cols : (r + 1) * cols] = line


def pool(sums):
    channels = sums.shape[1] // 2
    fine = silu(sums).astype(BF16).astype(F32)
    return ((fine[:, :channels] + fine[:, channels:]) * 0.5).astype(BF16).astype(F32)


def down_conv(pooled, half_rows, half_cols, down):
    strips = []
    for p in range(half_rows):
        pieces = [
            pooled[2 * p + b, pl.ds(e, half_cols, stride=2), :].astype(BF16)
            for b in range(3)
            for e in range(3)
        ]
        strips.append(jnp.concatenate(pieces, axis=1))
    left = jnp.concatenate(strips, axis=0)
    right = down[...].reshape(-1, down.shape[-1])
    return jnp.dot(left, right, preferred_element_type=F32).astype(BF16)


def ends_kernel(above, below, weight, sums, down, out, halo, pooled):
    cols = above.shape[2]
    rows = sums.shape[0] // cols - 1
    added = halo_sum(above, below, weight, 0, rows)
    halo[...] = added
    channels = pooled.shape[2]
    pooled[:, cols:] = jnp.zeros((3, pooled.shape[1] - cols, channels), F32)
    zero = jnp.zeros((cols, added.shape[1]), F32)
    if out.shape[0] == 1:
        starts = [(jnp.where(has_above(), 0, rows - 2), added)]
    else:
        first = jnp.concatenate([added[:cols], zero, zero], axis=0)
        last = jnp.concatenate([zero, added[cols:]], axis=0)
        starts = [(0, first), (rows - 2, last)]
    for side, (start, more) in enumerate(starts):
        begin = pl.multiple_of(start * cols, cols)
        mean = pool(sums[pl.ds(begin, 3 * cols), :] + more)
        for i in range(3):
            line = mean[i * cols : (i + 1) * cols]
            if side == 1 and i == 2:
                line = jnp.where(has_below(), line, 0.0)
            pooled[i, :cols] = line
        out[side] = down_conv(pooled, 1, cols // 2, down)


def reduce_kernel(sums, halo, down, out, pooled):
    _, half_rows, half_cols, _ = out.shape
    rows, cols = 2 * half_rows, 2 * half_cols
    channels = pooled.shape[2]
    pooled[:, cols:] = jnp.zeros((rows + 1, pooled.shape[1] - cols, channels), F32)
    for r in range(rows + 1):
        line = sums[r * cols : (r + 1) * cols]
        for k, halo_r in enumerate((0, rows - 1, rows)):
            if r == halo_r:
                line = line + halo[k * cols : (k + 1) * cols]
        mean = pool(line)
        if r == rows:
            mean = jnp.where(has_below(), mean, 0.0)
        pooled[r, :cols] = mean
    out[...] = down_conv(pooled, half_rows, half_cols, down).reshape(out.shape)


def coarse_sum(field, rim, weight, a):
    _, rows, cols, channels = field.shape
    zero = jnp.zeros((cols, channels), BF16)
    flat = jnp.concatenate(
        [
            jnp.where(has_above(), rim[0], zero),
            field.reshape(rows * cols, channels),
            jnp.where(has_below(), rim[rim.shape[0] - 1], zero),
        ],
        axis=0,
    )
    left, right = shifted_columns(flat, cols)
    taps = jnp.concatenate([left, flat, right], axis=1)
    total = None
    for b in range(3):
        part = jnp.dot(
            taps[b * cols : (b + rows) * cols], weight[a, b], preferred_element_type=F32
        )
        total = part if total is None else total + part
    return total


def coarse_first_kernel(field, rim, weight, out):
    out[...] = coarse_sum(field[...], rim[...], weight, 2)


def coarse_next_kernel(field, rim, weight, total, out):
    part = coarse_sum(field[...], rim[...], weight, 0)
    out[...] = total[...] + jnp.where(has_earlier(2), part, 0.0)


def coarse_last_kernel(direct, direct_rim, relayed, relayed_rim, weight, total, out):
    odd = lax.axis_index("tm") % 2 == 1
    field = jnp.where(odd, direct[...], relayed[...])
    rim = jnp.where(odd, direct_rim[...], relayed_rim[...])
    part = coarse_sum(field, rim, weight, 1)
    total = total[...] + jnp.where(has_earlier(1), part, 0.0)
    out[...] = silu(total).astype(BF16).reshape(out.shape)


def call(kernel, out_shape, scratch, flops, args):
    size = sum(a.size * a.dtype.itemsize for a in args)
    return pl.pallas_call(
        kernel,
        out_shape=out_shape,
        in_specs=[pl.BlockSpec(memory_space=pltpu.VMEM)] * len(args),
        out_specs=jax.tree.map(lambda _: pl.BlockSpec(memory_space=pltpu.VMEM), out_shape),
        scratch_shapes=scratch,
        cost_estimate=pl.CostEstimate(flops=flops, bytes_accessed=size, transcendentals=0),
        compiler_params=pltpu.CompilerParams(vmem_limit_bytes=20 * 1024 * 1024),
    )(*args)


def local(frames, conv_fine, conv_down, conv_coarse):
    _, rows, cols, channels = frames.shape
    wide = conv_down.shape[-1]
    strips, times = lax.axis_size("rows"), lax.axis_size("tm")
    pace = call(pace_kernel, jax.ShapeDtypeStruct((8, 128), F32), [], 4 * 10**9, ())

    earlier = ring(frames, 1)
    (above, below), (above_1, below_1) = frame_rims(pace, frames)
    size = (rows + 1) * cols
    pair = jax.ShapeDtypeStruct((size, 2 * channels), F32)
    flops = 2 * size * 18 * channels * 2 * channels
    own = call(fine_own_kernel, pair, [], flops, (frames, conv_fine))
    halo = call(
        functools.partial(fine_halo_kernel, rows=rows),
        jax.ShapeDtypeStruct((3 * cols, 2 * channels), F32),
        [],
        flops // 3,
        (above, below, conv_fine),
    )
    half_rows, half_cols = rows // 2, cols // 2
    shape = jax.ShapeDtypeStruct((1, half_rows, half_cols, wide), BF16)
    sides = 1 if strips == 2 else 2
    halo_sums = jax.ShapeDtypeStruct((3 * cols, 2 * channels), F32)
    fine_sums = call(fine_rest_kernel, pair, [], flops, (earlier, conv_fine, own, halo))
    above_1, below_1, fine_sums = lax.optimization_barrier((above_1, below_1, fine_sums))
    ends, halo_1 = call(
        ends_kernel,
        (jax.ShapeDtypeStruct((sides, half_cols, wide), BF16), halo_sums),
        [pltpu.VMEM((3, cols + 8, channels), F32)],
        flops // 3,
        (above_1, below_1, conv_fine, fine_sums, conv_down),
    )
    field = call(
        reduce_kernel,
        shape,
        [pltpu.VMEM((rows + 1, cols + 8, channels), F32)],
        flops // 3,
        (fine_sums, halo_1, conv_down),
    )
    field_2 = moved(field, 2, 0)
    if sides == 1:
        rim = swapped(ends, 0)
    else:
        rim = jnp.concatenate([moved(ends[1:], 0, 1), moved(ends[:1], 0, -1)], axis=0)
    rim_2 = moved(rim, 2, 0)
    sums = jax.ShapeDtypeStruct((half_rows * half_cols, wide), F32)
    flops = 2 * half_rows * half_cols * 9 * wide * wide
    total = call(coarse_first_kernel, sums, [], flops, (field, rim, conv_coarse))
    if times % 2 == 0:
        direct, direct_rim = paired(field), paired(rim)
    else:
        direct, direct_rim = ring(field, 1), ring(rim, 1)
    field_2, rim_2, total, direct, direct_rim = lax.optimization_barrier(
        (field_2, rim_2, total, direct, direct_rim)
    )
    if times % 2 == 0:
        relayed, relayed_rim = paired(field_2), paired(rim_2)
    else:
        relayed, relayed_rim = direct, direct_rim
    total = call(coarse_next_kernel, sums, [], flops, (field_2, rim_2, conv_coarse, total))
    return call(
        coarse_last_kernel,
        shape,
        [],
        flops,
        (direct, direct_rim, relayed, relayed_rim, conv_coarse, total),
    )


def solution(mesh):
    placed = (P("tm", "rows", None, None), P(), P(), P())
    return jax.shard_map(local, mesh=mesh, in_specs=placed, out_specs=P("tm", "rows", None, None), check_vma=False)
```

```python
import functools

import jax
import jax.numpy as jnp
from jax import lax
from jax.experimental import pallas as pl
from jax.experimental.pallas import tpu as pltpu
from jax.sharding import PartitionSpec as P


F32 = jnp.float32
BF16 = jnp.bfloat16


def moved(value, steps, hop):
    tm, rows = lax.axis_size("tm"), lax.axis_size("rows")
    pairs = [
        (t * rows + r, (t + steps) * rows + r + hop)
        for t in range(tm - steps)
        for r in range(rows)
        if 0 <= r + hop < rows
    ]
    return lax.ppermute(value, ("tm", "rows"), pairs)


def ring(value, steps):
    tm = lax.axis_size("tm")
    return lax.ppermute(value, "tm", [(t, (t + steps) % tm) for t in range(tm)])


def swapped(value, steps):
    tm = lax.axis_size("tm")
    pairs = [(t * 2 + r, (t + steps) * 2 + 1 - r) for t in range(tm - steps) for r in range(2)]
    return lax.ppermute(value, ("tm", "rows"), pairs)


def paired(value):
    return lax.ppermute(value, "tm", [(t, t ^ 1) for t in range(lax.axis_size("tm"))])


def has_above():
    return lax.axis_index("rows") > 0


def has_below():
    return lax.axis_index("rows") < lax.axis_size("rows") - 1


def has_earlier(steps):
    return lax.axis_index("tm") >= steps


def pace_kernel(out):
    out[...] = jnp.zeros_like(out)


def edge_kernel(_, cells, out):
    width = out.shape[1]
    first = (1 - lax.axis_index("rows")) * (cells.shape[1] - width)
    out[...] = cells[:, pl.ds(first, width)]


def frame_rims(pace, frames):
    rows = frames.shape[1]
    if lax.axis_size("rows") == 2:
        sent = call(
            edge_kernel,
            jax.ShapeDtypeStruct((frames.shape[0], 2, *frames.shape[2:]), BF16),
            [],
            0,
            (pace, frames),
        )
        return [(both, both) for both in (swapped(sent, 0), swapped(sent, 1))]
    head, tail = frames[:, :2], frames[:, rows - 1 :]
    return [(moved(tail, steps, 1), moved(head, steps, -1)) for steps in (0, 1)]


def column_shift(value, cols, steps):
    size = value.shape[0]
    column = lax.broadcasted_iota(jnp.int32, value.shape, 0) % cols
    edge = 0 if steps > 0 else cols - 1
    return jnp.where(column == edge, 0.0, pltpu.roll(value, steps % size, 0))


def shifted_columns(flat, cols):
    wide = flat.astype(F32)
    return column_shift(wide, cols, 1).astype(BF16), column_shift(wide, cols, -1).astype(BF16)


def tap_matrix(weight, first_tap, row_taps, e, channels):
    zero = jnp.zeros((channels, channels), BF16)

    def pick(tap, b):
        return weight[tap, b, e * channels : (e + 1) * channels] if 0 <= tap <= 2 else zero

    return jnp.concatenate(
        [
            jnp.concatenate([pick(first_tap + f, b), pick(first_tap + f - 1, b)], axis=1)
            for f in range(2)
            for b in row_taps
        ],
        axis=0,
    )


def fine_rows(row, outs, row_taps, weight, first_tap):
    channels = weight.shape[-1]
    some = next(x for f in range(2) for r in outs for b in row_taps if (x := row(f, r - 1 + b)) is not None)
    cols = some.shape[0]
    zero = jnp.zeros((cols, channels), BF16)

    def cell(f, i):
        found = row(f, i)
        return zero if found is None else found

    left = jnp.concatenate(
        [
            jnp.concatenate([cell(f, r - 1 + b) for f in range(2) for b in row_taps], axis=1)
            for r in outs
        ],
        axis=0,
    )
    sums = [
        jnp.dot(
            left, tap_matrix(weight, first_tap, row_taps, e, channels), preferred_element_type=F32
        )
        for e in range(3)
    ]
    return sums[1] + column_shift(sums[0], cols, 1) + column_shift(sums[2], cols, -1)


def chunks_of(count):
    size = next(c for c in (3, 2, 1) if count % c == 0)
    return [range(i, i + size) for i in range(0, count, size)]


def fine_own_kernel(frames, weight, out):
    _, rows, cols, _ = frames.shape

    def row(f, i):
        return frames[f, i] if 0 <= i < rows else None

    for outs in chunks_of(rows + 1):
        out[outs[0] * cols : (outs[-1] + 1) * cols] = fine_rows(row, outs, range(3), weight, 2)


def halo_row(above, below, rows):
    def row(f, i):
        if i == -1:
            cells, have = above[f, above.shape[1] - 1], has_above()
        elif i >= rows:
            cells, have = below[f, i - rows], has_below()
        else:
            return None
        return jnp.where(have, cells, jnp.zeros_like(cells))

    return row


def halo_sum(above, below, weight, first_tap, rows):
    row = halo_row(above, below, rows)
    return jnp.concatenate(
        [
            fine_rows(row, [0], [0], weight, first_tap),
            fine_rows(row, [rows - 1, rows], [1, 2], weight, first_tap),
        ],
        axis=0,
    )


def fine_halo_kernel(above, below, weight, out, *, rows):
    out[...] = halo_sum(above, below, weight, 2, rows)


def silu(v):
    return v / (1.0 + jnp.exp(-v))


def fine_rest_kernel(frames, weight, own, halo, out):
    _, rows, cols, _ = frames.shape

    def row(f, i):
        return frames[f, i] if 0 <= i < rows else None

    for outs in chunks_of(rows + 1):
        total = jnp.where(has_earlier(1), fine_rows(row, outs, range(3), weight, 0), 0.0)
        for i, r in enumerate(outs):
            line = total[i * cols : (i + 1) * cols] + own[r * cols : (r + 1) * cols]
            for k, halo_r in enumerate((0, rows - 1, rows)):
                if r == halo_r:
                    line = line + halo[k * cols : (k + 1) * cols]
            out[r * cols : (r + 1) * cols] = line


def pool(sums):
    channels = sums.shape[1] // 2
    fine = silu(sums).astype(BF16).astype(F32)
    return ((fine[:, :channels] + fine[:, channels:]) * 0.5).astype(BF16).astype(F32)


def down_conv(pooled, half_rows, half_cols, down):
    strips = []
    for p in range(half_rows):
        pieces = [
            pooled[2 * p + b, pl.ds(e, half_cols, stride=2), :].astype(BF16)
            for b in range(3)
            for e in range(3)
        ]
        strips.append(jnp.concatenate(pieces, axis=1))
    left = jnp.concatenate(strips, axis=0)
    right = down[...].reshape(-1, down.shape[-1])
    return jnp.dot(left, right, preferred_element_type=F32).astype(BF16)


def ends_kernel(above, below, weight, sums, down, out, halo, pooled):
    cols = above.shape[2]
    rows = sums.shape[0] // cols - 1
    added = halo_sum(above, below, weight, 0, rows)
    halo[...] = added
    channels = pooled.shape[2]
    pooled[:, cols:] = jnp.zeros((3, pooled.shape[1] - cols, channels), F32)
    zero = jnp.zeros((cols, added.shape[1]), F32)
    if out.shape[0] == 1:
        starts = [(jnp.where(has_above(), 0, rows - 2), added)]
    else:
        first = jnp.concatenate([added[:cols], zero, zero], axis=0)
        last = jnp.concatenate([zero, added[cols:]], axis=0)
        starts = [(0, first), (rows - 2, last)]
    for side, (start, more) in enumerate(starts):
        begin = pl.multiple_of(start * cols, cols)
        mean = pool(sums[pl.ds(begin, 3 * cols), :] + more)
        for i in range(3):
            line = mean[i * cols : (i + 1) * cols]
            if side == 1 and i == 2:
                line = jnp.where(has_below(), line, 0.0)
            pooled[i, :cols] = line
        out[side] = down_conv(pooled, 1, cols // 2, down)


def reduce_kernel(sums, halo, down, out, pooled):
    _, half_rows, half_cols, _ = out.shape
    rows, cols = 2 * half_rows, 2 * half_cols
    channels = pooled.shape[2]
    pooled[:, cols:] = jnp.zeros((rows + 1, pooled.shape[1] - cols, channels), F32)
    for r in range(rows + 1):
        line = sums[r * cols : (r + 1) * cols]
        for k, halo_r in enumerate((0, rows - 1, rows)):
            if r == halo_r:
                line = line + halo[k * cols : (k + 1) * cols]
        mean = pool(line)
        if r == rows:
            mean = jnp.where(has_below(), mean, 0.0)
        pooled[r, :cols] = mean
    out[...] = down_conv(pooled, half_rows, half_cols, down).reshape(out.shape)


def join_kernel(field, rim, out):
    rows = field.shape[1]
    out[0, :rows] = field[0]
    out[0, rows:] = rim[...]


def coarse_sum(joined, rows, weight, a):
    _, count, cols, channels = joined.shape
    zero = jnp.zeros((cols, channels), BF16)
    flat = jnp.concatenate(
        [
            jnp.where(has_above(), joined[0, rows], zero),
            joined[0, :rows].reshape(rows * cols, channels),
            jnp.where(has_below(), joined[0, count - 1], zero),
        ],
        axis=0,
    )
    left, right = shifted_columns(flat, cols)
    taps = jnp.concatenate([left, flat, right], axis=1)
    total = None
    for b in range(3):
        part = jnp.dot(
            taps[b * cols : (b + rows) * cols], weight[a, b], preferred_element_type=F32
        )
        total = part if total is None else total + part
    return total


def coarse_first_kernel(joined, weight, out):
    out[...] = coarse_sum(joined[...], out.shape[0] // joined.shape[2], weight, 2)


def coarse_next_kernel(joined, weight, total, out):
    part = coarse_sum(joined[...], out.shape[0] // joined.shape[2], weight, 0)
    out[...] = total[...] + jnp.where(has_earlier(2), part, 0.0)


def coarse_last_kernel(direct, relayed, weight, total, out):
    odd = lax.axis_index("tm") % 2 == 1
    part = coarse_sum(jnp.where(odd, direct[...], relayed[...]), out.shape[1], weight, 1)
    total = total[...] + jnp.where(has_earlier(1), part, 0.0)
    out[...] = silu(total).astype(BF16).reshape(out.shape)


def call(kernel, out_shape, scratch, flops, args):
    size = sum(a.size * a.dtype.itemsize for a in args)
    return pl.pallas_call(
        kernel,
        out_shape=out_shape,
        in_specs=[pl.BlockSpec(memory_space=pltpu.VMEM)] * len(args),
        out_specs=jax.tree.map(lambda _: pl.BlockSpec(memory_space=pltpu.VMEM), out_shape),
        scratch_shapes=scratch,
        cost_estimate=pl.CostEstimate(flops=flops, bytes_accessed=size, transcendentals=0),
        compiler_params=pltpu.CompilerParams(vmem_limit_bytes=20 * 1024 * 1024),
    )(*args)


def local(frames, conv_fine, conv_down, conv_coarse):
    _, rows, cols, channels = frames.shape
    wide = conv_down.shape[-1]
    strips, times = lax.axis_size("rows"), lax.axis_size("tm")
    pace = call(pace_kernel, jax.ShapeDtypeStruct((8, 128), F32), [], 4 * 10**9, ())

    earlier = ring(frames, 1)
    (above, below), (above_1, below_1) = frame_rims(pace, frames)
    size = (rows + 1) * cols
    pair = jax.ShapeDtypeStruct((size, 2 * channels), F32)
    flops = 2 * size * 18 * channels * 2 * channels
    own = call(fine_own_kernel, pair, [], flops, (frames, conv_fine))
    halo = call(
        functools.partial(fine_halo_kernel, rows=rows),
        jax.ShapeDtypeStruct((3 * cols, 2 * channels), F32),
        [],
        flops // 3,
        (above, below, conv_fine),
    )
    half_rows, half_cols = rows // 2, cols // 2
    shape = jax.ShapeDtypeStruct((1, half_rows, half_cols, wide), BF16)
    sides = 1 if strips == 2 else 2
    halo_sums = jax.ShapeDtypeStruct((3 * cols, 2 * channels), F32)
    fine_sums = call(fine_rest_kernel, pair, [], flops, (earlier, conv_fine, own, halo))
    above_1, below_1, fine_sums = lax.optimization_barrier((above_1, below_1, fine_sums))
    ends, halo_1 = call(
        ends_kernel,
        (jax.ShapeDtypeStruct((sides, half_cols, wide), BF16), halo_sums),
        [pltpu.VMEM((3, cols + 8, channels), F32)],
        flops // 3,
        (above_1, below_1, conv_fine, fine_sums, conv_down),
    )
    field = call(
        reduce_kernel,
        shape,
        [pltpu.VMEM((rows + 1, cols + 8, channels), F32)],
        flops // 3,
        (fine_sums, halo_1, conv_down),
    )
    if sides == 1:
        rim = swapped(ends, 0)
    else:
        rim = jnp.concatenate([moved(ends[1:], 0, 1), moved(ends[:1], 0, -1)], axis=0)
    joined_shape = jax.ShapeDtypeStruct((1, half_rows + sides, half_cols, wide), BF16)
    joined = call(join_kernel, joined_shape, [], 0, (field, rim))
    sums = jax.ShapeDtypeStruct((half_rows * half_cols, wide), F32)
    flops = 2 * half_rows * half_cols * 9 * wide * wide
    joined_2 = moved(joined, 2, 0)
    total = call(coarse_first_kernel, sums, [], flops, (joined, conv_coarse))
    direct = paired(joined) if times % 2 == 0 else ring(joined, 1)
    joined_2, total, direct = lax.optimization_barrier((joined_2, total, direct))
    relayed = paired(joined_2) if times % 2 == 0 else direct
    total = call(coarse_next_kernel, sums, [], flops, (joined_2, conv_coarse, total))
    return call(coarse_last_kernel, shape, [], flops, (direct, relayed, conv_coarse, total))


def solution(mesh):
    placed = (P("tm", "rows", None, None), P(), P(), P())
    return jax.shard_map(local, mesh=mesh, in_specs=placed, out_specs=P("tm", "rows", None, None), check_vma=False)
```

```python
import functools

import jax
import jax.numpy as jnp
from jax import lax
from jax.experimental import pallas as pl
from jax.experimental.pallas import tpu as pltpu
from jax.sharding import PartitionSpec as P


F32 = jnp.float32
BF16 = jnp.bfloat16


def moved(value, steps, hop):
    tm, rows = lax.axis_size("tm"), lax.axis_size("rows")
    pairs = [
        (t * rows + r, (t + steps) * rows + r + hop)
        for t in range(tm - steps)
        for r in range(rows)
        if 0 <= r + hop < rows
    ]
    return lax.ppermute(value, ("tm", "rows"), pairs)


def ring(value, steps):
    tm = lax.axis_size("tm")
    return lax.ppermute(value, "tm", [(t, (t + steps) % tm) for t in range(tm)])


def swapped(value, steps):
    tm = lax.axis_size("tm")
    pairs = [(t * 2 + r, (t + steps) * 2 + 1 - r) for t in range(tm - steps) for r in range(2)]
    return lax.ppermute(value, ("tm", "rows"), pairs)


def paired(value):
    return lax.ppermute(value, "tm", [(t, t ^ 1) for t in range(lax.axis_size("tm"))])


def has_above():
    return lax.axis_index("rows") > 0


def has_below():
    return lax.axis_index("rows") < lax.axis_size("rows") - 1


def has_earlier(steps):
    return lax.axis_index("tm") >= steps


def pace_kernel(out):
    out[...] = jnp.zeros_like(out)


def edge_kernel(_, cells, out):
    width = out.shape[1]
    first = (1 - lax.axis_index("rows")) * (cells.shape[1] - width)
    out[...] = cells[:, pl.ds(first, width)]


def frame_rims(pace, frames):
    rows = frames.shape[1]
    if lax.axis_size("rows") == 2:
        sent = call(
            edge_kernel,
            jax.ShapeDtypeStruct((frames.shape[0], 2, *frames.shape[2:]), BF16),
            [],
            0,
            (pace, frames),
        )
        return [(both, both) for both in (swapped(sent, 0), swapped(sent, 1))]
    head, tail = frames[:, :2], frames[:, rows - 1 :]
    return [(moved(tail, steps, 1), moved(head, steps, -1)) for steps in (0, 1)]


def column_shift(value, cols, steps):
    size = value.shape[0]
    column = lax.broadcasted_iota(jnp.int32, value.shape, 0) % cols
    edge = 0 if steps > 0 else cols - 1
    return jnp.where(column == edge, 0.0, pltpu.roll(value, steps % size, 0))


def shifted_columns(flat, cols):
    wide = flat.astype(F32)
    return column_shift(wide, cols, 1).astype(BF16), column_shift(wide, cols, -1).astype(BF16)


def tap_matrix(weight, first_tap, row_taps, e, channels):
    zero = jnp.zeros((channels, channels), BF16)

    def pick(tap, b):
        return weight[tap, b, e * channels : (e + 1) * channels] if 0 <= tap <= 2 else zero

    return jnp.concatenate(
        [
            jnp.concatenate([pick(first_tap + f, b), pick(first_tap + f - 1, b)], axis=1)
            for f in range(2)
            for b in row_taps
        ],
        axis=0,
    )


def fine_rows(row, outs, row_taps, weight, first_tap):
    channels = weight.shape[-1]
    some = next(x for f in range(2) for r in outs for b in row_taps if (x := row(f, r - 1 + b)) is not None)
    cols = some.shape[0]
    zero = jnp.zeros((cols, channels), BF16)

    def cell(f, i):
        found = row(f, i)
        return zero if found is None else found

    left = jnp.concatenate(
        [
            jnp.concatenate([cell(f, r - 1 + b) for f in range(2) for b in row_taps], axis=1)
            for r in outs
        ],
        axis=0,
    )
    sums = [
        jnp.dot(
            left, tap_matrix(weight, first_tap, row_taps, e, channels), preferred_element_type=F32
        )
        for e in range(3)
    ]
    return sums[1] + column_shift(sums[0], cols, 1) + column_shift(sums[2], cols, -1)


def chunks_of(count):
    size = next(c for c in (3, 2, 1) if count % c == 0)
    return [range(i, i + size) for i in range(0, count, size)]


def fine_own_kernel(frames, weight, out):
    _, rows, cols, _ = frames.shape

    def row(f, i):
        return frames[f, i] if 0 <= i < rows else None

    for outs in chunks_of(rows + 1):
        out[outs[0] * cols : (outs[-1] + 1) * cols] = fine_rows(row, outs, range(3), weight, 2)


def halo_row(above, below, rows):
    def row(f, i):
        if i == -1:
            cells, have = above[f, above.shape[1] - 1], has_above()
        elif i >= rows:
            cells, have = below[f, i - rows], has_below()
        else:
            return None
        return jnp.where(have, cells, jnp.zeros_like(cells))

    return row


def halo_sum(above, below, weight, first_tap, rows):
    row = halo_row(above, below, rows)
    return jnp.concatenate(
        [
            fine_rows(row, [0], [0], weight, first_tap),
            fine_rows(row, [rows - 1, rows], [1, 2], weight, first_tap),
        ],
        axis=0,
    )


def fine_halo_kernel(above, below, weight, out, *, rows):
    out[...] = halo_sum(above, below, weight, 2, rows)


def silu(v):
    return v / (1.0 + jnp.exp(-v))


def fine_rest_kernel(frames, weight, own, halo, out):
    _, rows, cols, _ = frames.shape

    def row(f, i):
        return frames[f, i] if 0 <= i < rows else None

    for outs in chunks_of(rows + 1):
        total = jnp.where(has_earlier(1), fine_rows(row, outs, range(3), weight, 0), 0.0)
        for i, r in enumerate(outs):
            line = total[i * cols : (i + 1) * cols] + own[r * cols : (r + 1) * cols]
            for k, halo_r in enumerate((0, rows - 1, rows)):
                if r == halo_r:
                    line = line + halo[k * cols : (k + 1) * cols]
            out[r * cols : (r + 1) * cols] = line


def pool(sums):
    channels = sums.shape[1] // 2
    fine = silu(sums).astype(BF16).astype(F32)
    return ((fine[:, :channels] + fine[:, channels:]) * 0.5).astype(BF16).astype(F32)


def down_conv(pooled, half_rows, half_cols, down):
    strips = []
    for p in range(half_rows):
        pieces = [
            pooled[2 * p + b, pl.ds(e, half_cols, stride=2), :].astype(BF16)
            for b in range(3)
            for e in range(3)
        ]
        strips.append(jnp.concatenate(pieces, axis=1))
    left = jnp.concatenate(strips, axis=0)
    right = down[...].reshape(-1, down.shape[-1])
    return jnp.dot(left, right, preferred_element_type=F32).astype(BF16)


def ends_kernel(above, below, weight, sums, down, out, halo, pooled):
    cols = above.shape[2]
    rows = sums.shape[0] // cols - 1
    added = halo_sum(above, below, weight, 0, rows)
    halo[...] = added
    channels = pooled.shape[2]
    pooled[:, cols:] = jnp.zeros((3, pooled.shape[1] - cols, channels), F32)
    zero = jnp.zeros((cols, added.shape[1]), F32)
    if out.shape[0] == 1:
        starts = [(jnp.where(has_above(), 0, rows - 2), added)]
    else:
        first = jnp.concatenate([added[:cols], zero, zero], axis=0)
        last = jnp.concatenate([zero, added[cols:]], axis=0)
        starts = [(0, first), (rows - 2, last)]
    for side, (start, more) in enumerate(starts):
        begin = pl.multiple_of(start * cols, cols)
        mean = pool(sums[pl.ds(begin, 3 * cols), :] + more)
        for i in range(3):
            line = mean[i * cols : (i + 1) * cols]
            if side == 1 and i == 2:
                line = jnp.where(has_below(), line, 0.0)
            pooled[i, :cols] = line
        out[side] = down_conv(pooled, 1, cols // 2, down)


def reduce_kernel(sums, halo, down, out, pooled):
    _, half_rows, half_cols, _ = out.shape
    rows, cols = 2 * half_rows, 2 * half_cols
    channels = pooled.shape[2]
    pooled[:, cols:] = jnp.zeros((rows + 1, pooled.shape[1] - cols, channels), F32)
    for r in range(rows + 1):
        line = sums[r * cols : (r + 1) * cols]
        for k, halo_r in enumerate((0, rows - 1, rows)):
            if r == halo_r:
                line = line + halo[k * cols : (k + 1) * cols]
        mean = pool(line)
        if r == rows:
            mean = jnp.where(has_below(), mean, 0.0)
        pooled[r, :cols] = mean
    out[...] = down_conv(pooled, half_rows, half_cols, down).reshape(out.shape)


def coarse_sum(field, rim, weight, a):
    _, rows, cols, channels = field.shape
    zero = jnp.zeros((cols, channels), BF16)
    flat = jnp.concatenate(
        [
            jnp.where(has_above(), rim[0], zero),
            field.reshape(rows * cols, channels),
            jnp.where(has_below(), rim[rim.shape[0] - 1], zero),
        ],
        axis=0,
    )
    left, right = shifted_columns(flat, cols)
    taps = jnp.concatenate([left, flat, right], axis=1)
    total = None
    for b in range(3):
        part = jnp.dot(
            taps[b * cols : (b + rows) * cols], weight[a, b], preferred_element_type=F32
        )
        total = part if total is None else total + part
    return total


def coarse_first_kernel(field, rim, weight, out):
    out[...] = coarse_sum(field[...], rim[...], weight, 2)


def coarse_next_kernel(field, rim, weight, total, out):
    part = coarse_sum(field[...], rim[...], weight, 0)
    out[...] = total[...] + jnp.where(has_earlier(2), part, 0.0)


def coarse_last_kernel(direct, direct_rim, relayed, relayed_rim, weight, total, out):
    odd = lax.axis_index("tm") % 2 == 1
    field = jnp.where(odd, direct[...], relayed[...])
    rim = jnp.where(odd, direct_rim[...], relayed_rim[...])
    part = coarse_sum(field, rim, weight, 1)
    total = total[...] + jnp.where(has_earlier(1), part, 0.0)
    out[...] = silu(total).astype(BF16).reshape(out.shape)


def call(kernel, out_shape, scratch, flops, args):
    size = sum(a.size * a.dtype.itemsize for a in args)
    return pl.pallas_call(
        kernel,
        out_shape=out_shape,
        in_specs=[pl.BlockSpec(memory_space=pltpu.VMEM)] * len(args),
        out_specs=jax.tree.map(lambda _: pl.BlockSpec(memory_space=pltpu.VMEM), out_shape),
        scratch_shapes=scratch,
        cost_estimate=pl.CostEstimate(flops=flops, bytes_accessed=size, transcendentals=0),
        compiler_params=pltpu.CompilerParams(vmem_limit_bytes=20 * 1024 * 1024),
    )(*args)


def local(frames, conv_fine, conv_down, conv_coarse):
    _, rows, cols, channels = frames.shape
    wide = conv_down.shape[-1]
    strips, times = lax.axis_size("rows"), lax.axis_size("tm")
    pace = call(pace_kernel, jax.ShapeDtypeStruct((8, 128), F32), [], 4 * 10**9, ())

    earlier = ring(frames, 1)
    (above, below), (above_1, below_1) = frame_rims(pace, frames)
    size = (rows + 1) * cols
    pair = jax.ShapeDtypeStruct((size, 2 * channels), F32)
    flops = 2 * size * 18 * channels * 2 * channels
    own = call(fine_own_kernel, pair, [], flops, (frames, conv_fine))
    halo = call(
        functools.partial(fine_halo_kernel, rows=rows),
        jax.ShapeDtypeStruct((3 * cols, 2 * channels), F32),
        [],
        flops // 3,
        (above, below, conv_fine),
    )
    half_rows, half_cols = rows // 2, cols // 2
    shape = jax.ShapeDtypeStruct((1, half_rows, half_cols, wide), BF16)
    sides = 1 if strips == 2 else 2
    halo_sums = jax.ShapeDtypeStruct((3 * cols, 2 * channels), F32)
    fine_sums = call(fine_rest_kernel, pair, [], flops, (earlier, conv_fine, own, halo))
    above_1, below_1, fine_sums = lax.optimization_barrier((above_1, below_1, fine_sums))
    ends, halo_1 = call(
        ends_kernel,
        (jax.ShapeDtypeStruct((sides, half_cols, wide), BF16), halo_sums),
        [pltpu.VMEM((3, cols + 8, channels), F32)],
        flops // 3,
        (above_1, below_1, conv_fine, fine_sums, conv_down),
    )
    field = call(
        reduce_kernel,
        shape,
        [pltpu.VMEM((rows + 1, cols + 8, channels), F32)],
        flops // 3,
        (fine_sums, halo_1, conv_down),
    )
    field_2 = moved(field, 2, 0)
    if sides == 1:
        rim = swapped(ends, 0)
    else:
        rim = jnp.concatenate([moved(ends[1:], 0, 1), moved(ends[:1], 0, -1)], axis=0)
    rim_2 = moved(rim, 2, 0)
    sums = jax.ShapeDtypeStruct((half_rows * half_cols, wide), F32)
    flops = 2 * half_rows * half_cols * 9 * wide * wide
    total = call(coarse_first_kernel, sums, [], flops, (field, rim, conv_coarse))
    near = paired if times % 2 == 0 else functools.partial(ring, steps=1)
    direct = near(field)
    direct_rim = near(rim)
    field_2, rim_2, total, direct, direct_rim = lax.optimization_barrier(
        (field_2, rim_2, total, direct, direct_rim)
    )
    if times % 2 == 0:
        relayed, relayed_rim = paired(field_2), paired(rim_2)
    else:
        relayed, relayed_rim = direct, direct_rim
    total = call(coarse_next_kernel, sums, [], flops, (field_2, rim_2, conv_coarse, total))
    return call(
        coarse_last_kernel,
        shape,
        [],
        flops,
        (direct, direct_rim, relayed, relayed_rim, conv_coarse, total),
    )


def solution(mesh):
    placed = (P("tm", "rows", None, None), P(), P(), P())
    return jax.shard_map(local, mesh=mesh, in_specs=placed, out_specs=P("tm", "rows", None, None), check_vma=False)
```

```python
import functools

import jax
import jax.numpy as jnp
from jax import lax
from jax.experimental import pallas as pl
from jax.experimental.pallas import tpu as pltpu
from jax.sharding import PartitionSpec as P


F32 = jnp.float32
BF16 = jnp.bfloat16


def moved(value, steps, hop):
    tm, rows = lax.axis_size("tm"), lax.axis_size("rows")
    pairs = [
        (t * rows + r, (t + steps) * rows + r + hop)
        for t in range(tm - steps)
        for r in range(rows)
        if 0 <= r + hop < rows
    ]
    return lax.ppermute(value, ("tm", "rows"), pairs)


def ring(value, steps):
    tm = lax.axis_size("tm")
    return lax.ppermute(value, "tm", [(t, (t + steps) % tm) for t in range(tm)])


def swapped(value, steps):
    tm = lax.axis_size("tm")
    pairs = [(t * 2 + r, (t + steps) * 2 + 1 - r) for t in range(tm - steps) for r in range(2)]
    return lax.ppermute(value, ("tm", "rows"), pairs)


def paired(value):
    return lax.ppermute(value, "tm", [(t, t ^ 1) for t in range(lax.axis_size("tm"))])


def has_above():
    return lax.axis_index("rows") > 0


def has_below():
    return lax.axis_index("rows") < lax.axis_size("rows") - 1


def has_earlier(steps):
    return lax.axis_index("tm") >= steps


def pace_kernel(out):
    out[...] = jnp.zeros_like(out)


def edge_kernel(_, cells, out):
    width = out.shape[1]
    first = (1 - lax.axis_index("rows")) * (cells.shape[1] - width)
    out[...] = cells[:, pl.ds(first, width)]


def frame_rims(pace, frames):
    rows = frames.shape[1]
    if lax.axis_size("rows") == 2:
        sent = call(
            edge_kernel,
            jax.ShapeDtypeStruct((frames.shape[0], 2, *frames.shape[2:]), BF16),
            [],
            0,
            (pace, frames),
        )
        return [(both, both) for both in (swapped(sent, 0), swapped(sent, 1))]
    head, tail = frames[:, :2], frames[:, rows - 1 :]
    return [(moved(tail, steps, 1), moved(head, steps, -1)) for steps in (0, 1)]


def column_shift(value, cols, steps):
    size = value.shape[0]
    column = lax.broadcasted_iota(jnp.int32, value.shape, 0) % cols
    edge = 0 if steps > 0 else cols - 1
    return jnp.where(column == edge, 0.0, pltpu.roll(value, steps % size, 0))


def shifted_columns(flat, cols):
    wide = flat.astype(F32)
    return column_shift(wide, cols, 1).astype(BF16), column_shift(wide, cols, -1).astype(BF16)


def tap_matrix(weight, first_tap, row_taps, e, channels):
    zero = jnp.zeros((channels, channels), BF16)

    def pick(tap, b):
        return weight[tap, b, e * channels : (e + 1) * channels] if 0 <= tap <= 2 else zero

    return jnp.concatenate(
        [
            jnp.concatenate([pick(first_tap + f, b), pick(first_tap + f - 1, b)], axis=1)
            for f in range(2)
            for b in row_taps
        ],
        axis=0,
    )


def fine_rows(row, outs, row_taps, weight, first_tap):
    channels = weight.shape[-1]
    some = next(x for f in range(2) for r in outs for b in row_taps if (x := row(f, r - 1 + b)) is not None)
    cols = some.shape[0]
    zero = jnp.zeros((cols, channels), BF16)

    def cell(f, i):
        found = row(f, i)
        return zero if found is None else found

    left = jnp.concatenate(
        [
            jnp.concatenate([cell(f, r - 1 + b) for f in range(2) for b in row_taps], axis=1)
            for r in outs
        ],
        axis=0,
    )
    sums = [
        jnp.dot(
            left, tap_matrix(weight, first_tap, row_taps, e, channels), preferred_element_type=F32
        )
        for e in range(3)
    ]
    return sums[1] + column_shift(sums[0], cols, 1) + column_shift(sums[2], cols, -1)


def chunks_of(count):
    size = next(c for c in (3, 2, 1) if count % c == 0)
    return [range(i, i + size) for i in range(0, count, size)]


def fine_own_kernel(frames, weight, out):
    _, rows, cols, _ = frames.shape

    def row(f, i):
        return frames[f, i] if 0 <= i < rows else None

    for outs in chunks_of(rows + 1):
        out[outs[0] * cols : (outs[-1] + 1) * cols] = fine_rows(row, outs, range(3), weight, 2)


def halo_row(above, below, rows):
    def row(f, i):
        if i == -1:
            cells, have = above[f, above.shape[1] - 1], has_above()
        elif i >= rows:
            cells, have = below[f, i - rows], has_below()
        else:
            return None
        return jnp.where(have, cells, jnp.zeros_like(cells))

    return row


def halo_sum(above, below, weight, first_tap, rows):
    row = halo_row(above, below, rows)
    return jnp.concatenate(
        [
            fine_rows(row, [0], [0], weight, first_tap),
            fine_rows(row, [rows - 1, rows], [1, 2], weight, first_tap),
        ],
        axis=0,
    )


def fine_halo_kernel(above, below, weight, out, *, rows):
    out[...] = halo_sum(above, below, weight, 2, rows)


def silu(v):
    return v / (1.0 + jnp.exp(-v))


def fine_rest_kernel(frames, weight, own, halo, out):
    _, rows, cols, _ = frames.shape

    def row(f, i):
        return frames[f, i] if 0 <= i < rows else None

    for outs in chunks_of(rows + 1):
        total = jnp.where(has_earlier(1), fine_rows(row, outs, range(3), weight, 0), 0.0)
        for i, r in enumerate(outs):
            line = total[i * cols : (i + 1) * cols] + own[r * cols : (r + 1) * cols]
            for k, halo_r in enumerate((0, rows - 1, rows)):
                if r == halo_r:
                    line = line + halo[k * cols : (k + 1) * cols]
            out[r * cols : (r + 1) * cols] = line


def pool(sums):
    channels = sums.shape[1] // 2
    fine = silu(sums).astype(BF16).astype(F32)
    return ((fine[:, :channels] + fine[:, channels:]) * 0.5).astype(BF16).astype(F32)


def down_conv(pooled, half_rows, half_cols, down):
    strips = []
    for p in range(half_rows):
        pieces = [
            pooled[2 * p + b, pl.ds(e, half_cols, stride=2), :].astype(BF16)
            for b in range(3)
            for e in range(3)
        ]
        strips.append(jnp.concatenate(pieces, axis=1))
    left = jnp.concatenate(strips, axis=0)
    right = down[...].reshape(-1, down.shape[-1])
    return jnp.dot(left, right, preferred_element_type=F32).astype(BF16)


def ends_kernel(above, below, weight, sums, down, out, halo, pooled):
    cols = above.shape[2]
    rows = sums.shape[0] // cols - 1
    added = halo_sum(above, below, weight, 0, rows)
    halo[...] = added
    channels = pooled.shape[2]
    pooled[:, cols:] = jnp.zeros((3, pooled.shape[1] - cols, channels), F32)
    zero = jnp.zeros((cols, added.shape[1]), F32)
    if out.shape[0] == 1:
        starts = [(jnp.where(has_above(), 0, rows - 2), added)]
    else:
        first = jnp.concatenate([added[:cols], zero, zero], axis=0)
        last = jnp.concatenate([zero, added[cols:]], axis=0)
        starts = [(0, first), (rows - 2, last)]
    for side, (start, more) in enumerate(starts):
        begin = pl.multiple_of(start * cols, cols)
        mean = pool(sums[pl.ds(begin, 3 * cols), :] + more)
        for i in range(3):
            line = mean[i * cols : (i + 1) * cols]
            if side == 1 and i == 2:
                line = jnp.where(has_below(), line, 0.0)
            pooled[i, :cols] = line
        out[side] = down_conv(pooled, 1, cols // 2, down)


def reduce_kernel(sums, halo, down, out, pooled):
    _, half_rows, half_cols, _ = out.shape
    rows, cols = 2 * half_rows, 2 * half_cols
    channels = pooled.shape[2]
    pooled[:, cols:] = jnp.zeros((rows + 1, pooled.shape[1] - cols, channels), F32)
    for r in range(rows + 1):
        line = sums[r * cols : (r + 1) * cols]
        for k, halo_r in enumerate((0, rows - 1, rows)):
            if r == halo_r:
                line = line + halo[k * cols : (k + 1) * cols]
        mean = pool(line)
        if r == rows:
            mean = jnp.where(has_below(), mean, 0.0)
        pooled[r, :cols] = mean
    out[...] = down_conv(pooled, half_rows, half_cols, down).reshape(out.shape)


def column_taps(flat, cols):
    left, right = shifted_columns(flat, cols)
    return jnp.concatenate([left, flat, right], axis=1)


def coarse_sum(field, weight, a):
    _, rows, cols, channels = field.shape
    zero = jnp.zeros((cols, 3 * channels), BF16)
    taps = column_taps(field.reshape(rows * cols, channels), cols)
    taps = jnp.concatenate([zero, taps, zero], axis=0)
    total = None
    for b in range(3):
        part = jnp.dot(
            taps[b * cols : (b + rows) * cols], weight[a, b], preferred_element_type=F32
        )
        total = part if total is None else total + part
    return total


def coarse_first_kernel(field, weight, out):
    out[...] = coarse_sum(field[...], weight, 2)


def coarse_next_kernel(field, weight, total, out):
    part = coarse_sum(field[...], weight, 0)
    out[...] = total[...] + jnp.where(has_earlier(2), part, 0.0)


def from_pair(direct, relayed):
    return jnp.where(lax.axis_index("tm") % 2 == 1, direct[...], relayed[...])


def coarse_body_kernel(direct, relayed, weight, total, out, ends):
    _, rows, cols, _ = out.shape
    part = coarse_sum(from_pair(direct, relayed), weight, 1)
    sums = total[...] + jnp.where(has_earlier(1), part, 0.0)
    out[...] = silu(sums).astype(BF16).reshape(out.shape)
    head, tail = sums[:cols], sums[(rows - 1) * cols :]
    if ends.shape[0] == 1:
        ends[0] = jnp.where(has_above(), head, tail)
    else:
        ends[0], ends[1] = head, tail


def coarse_ends_kernel(rim_0, direct, relayed, rim_2, weight, sums, _, out, row, sem):
    rows, cols = out.shape[1:3]
    sides = sums.shape[0]
    rims = [
        jnp.where(has_earlier(2), rim_0[...], jnp.zeros_like(rim_0[...])),
        jnp.where(has_earlier(1), from_pair(direct, relayed), jnp.zeros_like(direct[...])),
        rim_2[...],
    ]
    strip = lax.axis_index("rows")
    copies = []
    for side in range(sides):
        taps = jnp.concatenate([column_taps(rim[side], cols) for rim in rims], axis=1)
        if sides == 1:
            b, p = 2 * (1 - strip), (rows - 1) * (1 - strip)
        else:
            b, p = 2 * side, (rows - 1) * side
            taps = jnp.where((has_above(), has_below())[side], taps, jnp.zeros_like(taps))
        kernel = weight[:, b].reshape(taps.shape[1], -1)
        total = sums[side] + jnp.dot(taps, kernel, preferred_element_type=F32)
        row[side] = silu(total).astype(BF16)
        copies.append(pltpu.make_async_copy(row.at[side], out.at[0, p], sem.at[side]))
        copies[-1].start()
    for copy in copies:
        copy.wait()


def call(kernel, out_shape, scratch, flops, args, in_place=False):
    size = sum(a.size * a.dtype.itemsize for a in args)
    vmem = pl.BlockSpec(memory_space=pltpu.VMEM)
    last = pl.BlockSpec(memory_space=pl.ANY) if in_place else vmem
    return pl.pallas_call(
        kernel,
        out_shape=out_shape,
        in_specs=[vmem] * (len(args) - 1) + [last] if args else [],
        out_specs=last if in_place else jax.tree.map(lambda _: vmem, out_shape),
        input_output_aliases={len(args) - 1: 0} if in_place else {},
        scratch_shapes=scratch,
        cost_estimate=pl.CostEstimate(flops=flops, bytes_accessed=size, transcendentals=0),
        compiler_params=pltpu.CompilerParams(vmem_limit_bytes=20 * 1024 * 1024),
    )(*args)


def local(frames, conv_fine, conv_down, conv_coarse):
    _, rows, cols, channels = frames.shape
    wide = conv_down.shape[-1]
    strips, times = lax.axis_size("rows"), lax.axis_size("tm")
    pace = call(pace_kernel, jax.ShapeDtypeStruct((8, 128), F32), [], 4 * 10**9, ())

    earlier = ring(frames, 1)
    (above, below), (above_1, below_1) = frame_rims(pace, frames)
    size = (rows + 1) * cols
    pair = jax.ShapeDtypeStruct((size, 2 * channels), F32)
    flops = 2 * size * 18 * channels * 2 * channels
    own = call(fine_own_kernel, pair, [], flops, (frames, conv_fine))
    halo = call(
        functools.partial(fine_halo_kernel, rows=rows),
        jax.ShapeDtypeStruct((3 * cols, 2 * channels), F32),
        [],
        flops // 3,
        (above, below, conv_fine),
    )
    half_rows, half_cols = rows // 2, cols // 2
    shape = jax.ShapeDtypeStruct((1, half_rows, half_cols, wide), BF16)
    sides = 1 if strips == 2 else 2
    halo_sums = jax.ShapeDtypeStruct((3 * cols, 2 * channels), F32)
    fine_sums = call(fine_rest_kernel, pair, [], flops, (earlier, conv_fine, own, halo))
    above_1, below_1, fine_sums = lax.optimization_barrier((above_1, below_1, fine_sums))
    ends, halo_1 = call(
        ends_kernel,
        (jax.ShapeDtypeStruct((sides, half_cols, wide), BF16), halo_sums),
        [pltpu.VMEM((3, cols + 8, channels), F32)],
        flops // 3,
        (above_1, below_1, conv_fine, fine_sums, conv_down),
    )
    field = call(
        reduce_kernel,
        shape,
        [pltpu.VMEM((rows + 1, cols + 8, channels), F32)],
        flops // 3,
        (fine_sums, halo_1, conv_down),
    )
    field_2 = moved(field, 2, 0)
    if sides == 1:
        rim = swapped(ends, 0)
    else:
        rim = jnp.concatenate([moved(ends[1:], 0, 1), moved(ends[:1], 0, -1)], axis=0)
    rim_2 = moved(rim, 2, 0)
    sums = jax.ShapeDtypeStruct((half_rows * half_cols, wide), F32)
    flops = 2 * half_rows * half_cols * 9 * wide * wide
    total = call(coarse_first_kernel, sums, [], flops, (field, conv_coarse))
    near = paired if times % 2 == 0 else functools.partial(ring, steps=1)
    direct = near(field)
    direct_rim = near(rim)
    field_2, total, direct, direct_rim = lax.optimization_barrier(
        (field_2, total, direct, direct_rim)
    )
    relayed = paired(field_2) if times % 2 == 0 else direct
    total = call(coarse_next_kernel, sums, [], flops, (field_2, conv_coarse, total))
    rims = jax.ShapeDtypeStruct((sides, half_cols, wide), F32)
    body, body_ends = call(
        coarse_body_kernel, (shape, rims), [], flops, (direct, relayed, conv_coarse, total)
    )
    rim_2, body, body_ends = lax.optimization_barrier((rim_2, body, body_ends))
    relayed_rim = paired(rim_2) if times % 2 == 0 else direct_rim
    return call(
        coarse_ends_kernel,
        shape,
        [pltpu.VMEM(ends.shape, BF16), pltpu.SemaphoreType.DMA((sides,))],
        flops // 4,
        (rim_2, direct_rim, relayed_rim, rim, conv_coarse, body_ends, body),
        in_place=True,
    )


def solution(mesh):
    placed = (P("tm", "rows", None, None), P(), P(), P())
    return jax.shard_map(local, mesh=mesh, in_specs=placed, out_specs=P("tm", "rows", None, None), check_vma=False)
```

```python
import functools

import jax
import jax.numpy as jnp
from jax import lax
from jax.experimental import pallas as pl
from jax.experimental.pallas import tpu as pltpu
from jax.sharding import PartitionSpec as P


F32 = jnp.float32
BF16 = jnp.bfloat16


def moved(value, steps, hop):
    tm, rows = lax.axis_size("tm"), lax.axis_size("rows")
    pairs = [
        (t * rows + r, (t + steps) * rows + r + hop)
        for t in range(tm - steps)
        for r in range(rows)
        if 0 <= r + hop < rows
    ]
    return lax.ppermute(value, ("tm", "rows"), pairs)


def ring(value, steps):
    tm = lax.axis_size("tm")
    return lax.ppermute(value, "tm", [(t, (t + steps) % tm) for t in range(tm)])


def swapped(value, steps):
    tm = lax.axis_size("tm")
    pairs = [(t * 2 + r, (t + steps) * 2 + 1 - r) for t in range(tm - steps) for r in range(2)]
    return lax.ppermute(value, ("tm", "rows"), pairs)


def paired(value):
    return lax.ppermute(value, "tm", [(t, t ^ 1) for t in range(lax.axis_size("tm"))])


def has_above():
    return lax.axis_index("rows") > 0


def has_below():
    return lax.axis_index("rows") < lax.axis_size("rows") - 1


def has_earlier(steps):
    return lax.axis_index("tm") >= steps


def pace_kernel(out):
    out[...] = jnp.zeros_like(out)


def edge_kernel(_, cells, out):
    width = out.shape[1]
    first = (1 - lax.axis_index("rows")) * (cells.shape[1] - width)
    out[...] = cells[:, pl.ds(first, width)]


def frame_rims(pace, frames):
    rows = frames.shape[1]
    if lax.axis_size("rows") == 2:
        sent = call(
            edge_kernel,
            jax.ShapeDtypeStruct((frames.shape[0], 1, *frames.shape[2:]), BF16),
            [],
            0,
            (pace, frames),
        )
        return [(both, both) for both in (swapped(sent, 0), swapped(sent, 1))]
    head, tail = frames[:, :1], frames[:, rows - 1 :]
    return [(moved(tail, steps, 1), moved(head, steps, -1)) for steps in (0, 1)]


def column_shift(value, cols, steps):
    size = value.shape[0]
    column = lax.broadcasted_iota(jnp.int32, value.shape, 0) % cols
    edge = 0 if steps > 0 else cols - 1
    return jnp.where(column == edge, 0.0, pltpu.roll(value, steps % size, 0))


def shifted_columns(flat, cols):
    wide = flat.astype(F32)
    return column_shift(wide, cols, 1).astype(BF16), column_shift(wide, cols, -1).astype(BF16)


def tap_matrix(weight, first_tap, row_taps, e, channels):
    zero = jnp.zeros((channels, channels), BF16)

    def pick(tap, b):
        return weight[tap, b, e * channels : (e + 1) * channels] if 0 <= tap <= 2 else zero

    return jnp.concatenate(
        [
            jnp.concatenate([pick(first_tap + f, b), pick(first_tap + f - 1, b)], axis=1)
            for f in range(2)
            for b in row_taps
        ],
        axis=0,
    )


def fine_rows(row, outs, row_taps, weight, first_tap):
    channels = weight.shape[-1]
    some = next(x for f in range(2) for r in outs for b in row_taps if (x := row(f, r - 1 + b)) is not None)
    cols = some.shape[0]
    zero = jnp.zeros((cols, channels), BF16)

    def cell(f, i):
        found = row(f, i)
        return zero if found is None else found

    left = jnp.concatenate(
        [
            jnp.concatenate([cell(f, r - 1 + b) for f in range(2) for b in row_taps], axis=1)
            for r in outs
        ],
        axis=0,
    )
    sums = [
        jnp.dot(
            left, tap_matrix(weight, first_tap, row_taps, e, channels), preferred_element_type=F32
        )
        for e in range(3)
    ]
    return sums[1] + column_shift(sums[0], cols, 1) + column_shift(sums[2], cols, -1)


def chunks_of(count):
    size = next(c for c in (4, 3, 2, 1) if count % c == 0)
    return [range(i, i + size) for i in range(0, count, size)]


def fine_own_kernel(frames, weight, out):
    _, rows, cols, _ = frames.shape

    def row(f, i):
        return frames[f, i] if 0 <= i < rows else None

    for outs in chunks_of(rows):
        out[outs[0] * cols : (outs[-1] + 1) * cols] = fine_rows(row, outs, range(3), weight, 2)


def halo_sums(above, below, weight, first_tap, rows):
    def row(f, i):
        if i == -1:
            cells, have = above[f, 0], has_above()
        else:
            cells, have = below[f, 0], has_below()
        return jnp.where(have, cells, jnp.zeros_like(cells))

    return (
        fine_rows(row, [0], [0], weight, first_tap),
        fine_rows(row, [rows - 1], [2], weight, first_tap),
    )


def fine_halo_kernel(above, below, weight, out, *, rows):
    out[0], out[1] = halo_sums(above, below, weight, 2, rows)


def silu(v):
    return v / (1.0 + jnp.exp(-v))


def fine_rest_kernel(frames, weight, own, halo, out):
    _, rows, cols, _ = frames.shape

    def row(f, i):
        return frames[f, i] if 0 <= i < rows else None

    for outs in chunks_of(rows):
        total = jnp.where(has_earlier(1), fine_rows(row, outs, range(3), weight, 0), 0.0)
        for i, r in enumerate(outs):
            line = total[i * cols : (i + 1) * cols] + own[r * cols : (r + 1) * cols]
            for k, halo_r in enumerate((0, rows - 1)):
                if r == halo_r:
                    line = line + halo[k]
            out[r * cols : (r + 1) * cols] = line


def pool(sums):
    channels = sums.shape[1] // 2
    fine = silu(sums).astype(BF16).astype(F32)
    return ((fine[:, :channels] + fine[:, channels:]) * 0.5).astype(BF16).astype(F32)


def down_taps(pooled, first, row_taps, half_cols):
    pieces = [
        pooled[first + i, pl.ds(e, half_cols, stride=2), :].astype(BF16)
        for i in range(row_taps)
        for e in range(3)
    ]
    return jnp.concatenate(pieces, axis=1)


def put_pooled(pooled, lines):
    cols = lines[0].shape[0]
    pad = pooled.shape[1] - cols
    pooled[:, cols:] = jnp.zeros((pooled.shape[0], pad, pooled.shape[2]), F32)
    for i, line in enumerate(lines):
        pooled[i, :cols] = line


def ends_kernel(above, below, weight, sums, down, sent, kept, first, pooled):
    cols = above.shape[2]
    rows = sums.shape[0] // cols
    half_cols = cols // 2
    top, bottom = halo_sums(above, below, weight, 0, rows)
    lines = []
    for r in (0, 1, 2, rows - 2, rows - 1):
        line = sums[r * cols : (r + 1) * cols]
        if r == 0:
            line = line + top
        if r == rows - 1:
            line = line + bottom
        lines.append(pool(line))
    put_pooled(pooled, lines)
    dot = functools.partial(jnp.dot, preferred_element_type=F32)
    flat = down[...].reshape(-1, down.shape[-1])
    third = down.shape[1]
    head = dot(down_taps(pooled, 0, 3, half_cols), flat).astype(BF16)
    added = dot(down_taps(pooled, 0, 1, half_cols), down[2])
    tail = dot(down_taps(pooled, 3, 2, half_cols), flat[: 2 * third])
    first[...] = head
    kept[0], kept[1] = added, tail
    if sent.shape[0] == 2:
        sent[0] = jnp.where(has_above(), head, tail.astype(BF16))
        sent[1] = added.astype(BF16)
    else:
        sent[0], sent[1], sent[2] = head, added.astype(BF16), tail.astype(BF16)


def reduce_kernel(sums, first, down, out, pooled):
    _, count, half_cols, _ = out.shape
    cols = 2 * half_cols
    put_pooled(pooled, [pool(sums[r * cols : (r + 1) * cols]) for r in range(2, 2 * count + 1)])
    left = [down_taps(pooled, 2 * p, 3, half_cols) for p in range(count - 1)]
    flat = down[...].reshape(-1, down.shape[-1])
    rest = jnp.dot(jnp.concatenate(left, axis=0), flat, preferred_element_type=F32)
    out[0, 0] = first[...]
    out[0, 1:] = rest.astype(BF16).reshape(count - 1, half_cols, -1)


def edge_rows_kernel(above, below, kept, out):
    added, tail = kept[0], kept[1]
    more = jnp.where(has_below(), below[1].astype(F32), 0.0)
    out[0, 0] = (tail + more).astype(BF16)
    upper = (above[0].astype(F32) + added).astype(BF16)
    if out.shape[1] == 2:
        out[0, 1] = jnp.where(has_above(), upper, below[0])
    else:
        out[0, 1], out[0, 2] = upper, below[0]


def coarse_sum(main, edge, weight, a):
    _, count, cols, channels = main.shape
    rows = count + 1
    zero = jnp.zeros((cols, channels), BF16)
    flat = jnp.concatenate(
        [
            jnp.where(has_above(), edge[0, 1], zero),
            main[0].reshape(count * cols, channels),
            edge[0, 0],
            jnp.where(has_below(), edge[0, edge.shape[1] - 1], zero),
        ],
        axis=0,
    )
    left, right = shifted_columns(flat, cols)
    taps = jnp.concatenate([left, flat, right], axis=1)
    total = None
    for b in range(3):
        part = jnp.dot(
            taps[b * cols : (b + rows) * cols], weight[a, b], preferred_element_type=F32
        )
        total = part if total is None else total + part
    return total


def coarse_first_kernel(main, edge, weight, out):
    out[...] = coarse_sum(main[...], edge[...], weight, 2)


def coarse_next_kernel(main, edge, weight, total, out):
    part = coarse_sum(main[...], edge[...], weight, 0)
    out[...] = total[...] + jnp.where(has_earlier(2), part, 0.0)


def coarse_last_kernel(direct, direct_rim, relayed, relayed_rim, weight, total, out):
    odd = lax.axis_index("tm") % 2 == 1
    field = jnp.where(odd, direct[...], relayed[...])
    rim = jnp.where(odd, direct_rim[...], relayed_rim[...])
    part = coarse_sum(field, rim, weight, 1)
    total = total[...] + jnp.where(has_earlier(1), part, 0.0)
    out[...] = silu(total).astype(BF16).reshape(out.shape)


def call(kernel, out_shape, scratch, flops, args):
    size = sum(a.size * a.dtype.itemsize for a in args)
    return pl.pallas_call(
        kernel,
        out_shape=out_shape,
        in_specs=[pl.BlockSpec(memory_space=pltpu.VMEM)] * len(args),
        out_specs=jax.tree.map(lambda _: pl.BlockSpec(memory_space=pltpu.VMEM), out_shape),
        scratch_shapes=scratch,
        cost_estimate=pl.CostEstimate(flops=flops, bytes_accessed=size, transcendentals=0),
        compiler_params=pltpu.CompilerParams(vmem_limit_bytes=20 * 1024 * 1024),
    )(*args)


def local(frames, conv_fine, conv_down, conv_coarse):
    _, rows, cols, channels = frames.shape
    wide = conv_down.shape[-1]
    strips, times = lax.axis_size("rows"), lax.axis_size("tm")
    pace = call(pace_kernel, jax.ShapeDtypeStruct((8, 128), F32), [], 4 * 10**9, ())

    earlier = ring(frames, 1)
    (above, below), (above_1, below_1) = frame_rims(pace, frames)
    size = rows * cols
    pair = jax.ShapeDtypeStruct((size, 2 * channels), F32)
    flops = 2 * size * 18 * channels * 2 * channels
    own = call(fine_own_kernel, pair, [], flops, (frames, conv_fine))
    halo = call(
        functools.partial(fine_halo_kernel, rows=rows),
        jax.ShapeDtypeStruct((2, cols, 2 * channels), F32),
        [],
        flops // 3,
        (above, below, conv_fine),
    )
    half_rows, half_cols = rows // 2, cols // 2
    shape = jax.ShapeDtypeStruct((1, half_rows, half_cols, wide), BF16)
    two = strips == 2
    fine_sums = call(fine_rest_kernel, pair, [], flops, (earlier, conv_fine, own, halo))
    above_1, below_1, fine_sums = lax.optimization_barrier((above_1, below_1, fine_sums))
    sent, kept, first = call(
        ends_kernel,
        (
            jax.ShapeDtypeStruct((2 if two else 3, half_cols, wide), BF16),
            jax.ShapeDtypeStruct((2, half_cols, wide), F32),
            jax.ShapeDtypeStruct((half_cols, wide), BF16),
        ),
        [pltpu.VMEM((5, cols + 8, channels), F32)],
        flops // 3,
        (above_1, below_1, conv_fine, fine_sums, conv_down),
    )
    field = call(
        reduce_kernel,
        jax.ShapeDtypeStruct((1, half_rows - 1, half_cols, wide), BF16),
        [pltpu.VMEM((rows - 3, cols + 8, channels), F32)],
        flops // 3,
        (fine_sums, first, conv_down),
    )
    field_2 = moved(field, 2, 0)
    if two:
        from_above = from_below = swapped(sent, 0)
    else:
        from_above, from_below = moved(sent[2:], 0, 1), moved(sent[:2], 0, -1)
    rim = call(
        edge_rows_kernel,
        jax.ShapeDtypeStruct((1, 2 if two else 3, half_cols, wide), BF16),
        [],
        0,
        (from_above, from_below, kept),
    )
    rim_2 = moved(rim, 2, 0)
    sums = jax.ShapeDtypeStruct((half_rows * half_cols, wide), F32)
    flops = 2 * half_rows * half_cols * 9 * wide * wide
    total = call(coarse_first_kernel, sums, [], flops, (field, rim, conv_coarse))
    near = paired if times % 2 == 0 else functools.partial(ring, steps=1)
    direct = near(field)
    direct_rim = near(rim)
    field_2, rim_2, total, direct, direct_rim = lax.optimization_barrier(
        (field_2, rim_2, total, direct, direct_rim)
    )
    if times % 2 == 0:
        relayed, relayed_rim = paired(field_2), paired(rim_2)
    else:
        relayed, relayed_rim = direct, direct_rim
    total = call(coarse_next_kernel, sums, [], flops, (field_2, rim_2, conv_coarse, total))
    return call(
        coarse_last_kernel,
        shape,
        [],
        flops,
        (direct, direct_rim, relayed, relayed_rim, conv_coarse, total),
    )


def solution(mesh):
    placed = (P("tm", "rows", None, None), P(), P(), P())
    return jax.shard_map(local, mesh=mesh, in_specs=placed, out_specs=P("tm", "rows", None, None), check_vma=False)
```

```python
import functools

import jax
import jax.numpy as jnp
from jax import lax
from jax.experimental import pallas as pl
from jax.experimental.pallas import tpu as pltpu
from jax.sharding import PartitionSpec as P


F32 = jnp.float32
BF16 = jnp.bfloat16


def moved(value, steps, hop):
    tm, rows = lax.axis_size("tm"), lax.axis_size("rows")
    pairs = [
        (t * rows + r, (t + steps) * rows + r + hop)
        for t in range(tm - steps)
        for r in range(rows)
        if 0 <= r + hop < rows
    ]
    return lax.ppermute(value, ("tm", "rows"), pairs)


def ring(value, steps):
    tm = lax.axis_size("tm")
    return lax.ppermute(value, "tm", [(t, (t + steps) % tm) for t in range(tm)])


def swapped(value, steps):
    tm = lax.axis_size("tm")
    pairs = [(t * 2 + r, (t + steps) * 2 + 1 - r) for t in range(tm - steps) for r in range(2)]
    return lax.ppermute(value, ("tm", "rows"), pairs)


def paired(value):
    return lax.ppermute(value, "tm", [(t, t ^ 1) for t in range(lax.axis_size("tm"))])


def has_above():
    return lax.axis_index("rows") > 0


def has_below():
    return lax.axis_index("rows") < lax.axis_size("rows") - 1


def has_earlier(steps):
    return lax.axis_index("tm") >= steps


def pace_kernel(out):
    out[...] = jnp.zeros_like(out)


def edge_kernel(_, cells, out):
    width = out.shape[1]
    first = (1 - lax.axis_index("rows")) * (cells.shape[1] - width)
    out[...] = cells[:, pl.ds(first, width)]


def frame_rims(pace, frames):
    rows = frames.shape[1]
    if lax.axis_size("rows") == 2:
        sent = call(
            edge_kernel,
            jax.ShapeDtypeStruct((frames.shape[0], 1, *frames.shape[2:]), BF16),
            [],
            0,
            (pace, frames),
        )
        return [(both, both) for both in (swapped(sent, 0), swapped(sent, 1))]
    head, tail = frames[:, :1], frames[:, rows - 1 :]
    return [(moved(tail, steps, 1), moved(head, steps, -1)) for steps in (0, 1)]


def column_shift(value, cols, steps):
    size = value.shape[0]
    column = lax.broadcasted_iota(jnp.int32, value.shape, 0) % cols
    edge = 0 if steps > 0 else cols - 1
    return jnp.where(column == edge, 0.0, pltpu.roll(value, steps % size, 0))


def shifted_columns(flat, cols):
    wide = flat.astype(F32)
    return column_shift(wide, cols, 1).astype(BF16), column_shift(wide, cols, -1).astype(BF16)


def tap_matrix(weight, first_tap, row_taps, e, channels):
    zero = jnp.zeros((channels, channels), BF16)

    def pick(tap, b):
        return weight[tap, b, e * channels : (e + 1) * channels] if 0 <= tap <= 2 else zero

    return jnp.concatenate(
        [
            jnp.concatenate([pick(first_tap + f, b), pick(first_tap + f - 1, b)], axis=1)
            for f in range(2)
            for b in row_taps
        ],
        axis=0,
    )


def fine_rows(row, outs, row_taps, weight, first_tap):
    channels = weight.shape[-1]
    some = next(x for f in range(2) for r in outs for b in row_taps if (x := row(f, r - 1 + b)) is not None)
    cols = some.shape[0]
    zero = jnp.zeros((cols, channels), BF16)

    def cell(f, i):
        found = row(f, i)
        return zero if found is None else found

    left = jnp.concatenate(
        [
            jnp.concatenate([cell(f, r - 1 + b) for f in range(2) for b in row_taps], axis=1)
            for r in outs
        ],
        axis=0,
    )
    sums = [
        jnp.dot(
            left, tap_matrix(weight, first_tap, row_taps, e, channels), preferred_element_type=F32
        )
        for e in range(3)
    ]
    return sums[1] + column_shift(sums[0], cols, 1) + column_shift(sums[2], cols, -1)


def chunks_of(count):
    size = next(c for c in (4, 3, 2, 1) if count % c == 0)
    return [range(i, i + size) for i in range(0, count, size)]


def fine_own_kernel(frames, weight, out):
    _, rows, cols, _ = frames.shape

    def row(f, i):
        return frames[f, i] if 0 <= i < rows else None

    for outs in chunks_of(rows):
        out[outs[0] * cols : (outs[-1] + 1) * cols] = fine_rows(row, outs, range(3), weight, 2)


def halo_sums(above, below, weight, first_tap, rows):
    def row(f, i):
        if i == -1:
            cells, have = above[f, 0], has_above()
        else:
            cells, have = below[f, 0], has_below()
        return jnp.where(have, cells, jnp.zeros_like(cells))

    return (
        fine_rows(row, [0], [0], weight, first_tap),
        fine_rows(row, [rows - 1], [2], weight, first_tap),
    )


def fine_halo_kernel(above, below, weight, out, *, rows):
    out[0], out[1] = halo_sums(above, below, weight, 2, rows)


def silu(v):
    return v / (1.0 + jnp.exp(-v))


def fine_rest_kernel(frames, weight, own, halo, out):
    _, rows, cols, _ = frames.shape

    def row(f, i):
        return frames[f, i] if 0 <= i < rows else None

    for outs in chunks_of(rows):
        total = jnp.where(has_earlier(1), fine_rows(row, outs, range(3), weight, 0), 0.0)
        for i, r in enumerate(outs):
            line = total[i * cols : (i + 1) * cols] + own[r * cols : (r + 1) * cols]
            for k, halo_r in enumerate((0, rows - 1)):
                if r == halo_r:
                    line = line + halo[k]
            out[r * cols : (r + 1) * cols] = line


def pool(sums):
    channels = sums.shape[1] // 2
    fine = silu(sums).astype(BF16).astype(F32)
    return ((fine[:, :channels] + fine[:, channels:]) * 0.5).astype(BF16).astype(F32)


def down_taps(pooled, first, row_taps, half_cols):
    pieces = [
        pooled[first + i, pl.ds(e, half_cols, stride=2), :].astype(BF16)
        for i in range(row_taps)
        for e in range(3)
    ]
    return jnp.concatenate(pieces, axis=1)


def put_pooled(pooled, lines):
    cols = lines[0].shape[0]
    pad = pooled.shape[1] - cols
    pooled[:, cols:] = jnp.zeros((pooled.shape[0], pad, pooled.shape[2]), F32)
    for i, line in enumerate(lines):
        pooled[i, :cols] = line


def reduce_kernel(above, below, weight, sums, down, out, pooled):
    cols = above.shape[2]
    rows = sums.shape[0] // cols
    half_rows, half_cols = rows // 2, cols // 2
    top, bottom = halo_sums(above, below, weight, 0, rows)
    lines = []
    for r in range(rows):
        line = sums[r * cols : (r + 1) * cols]
        if r == 0:
            line = line + top
        if r == rows - 1:
            line = line + bottom
        lines.append(pool(line))
    put_pooled(pooled, [*lines, jnp.zeros_like(lines[0])])
    dot = functools.partial(jnp.dot, preferred_element_type=F32)
    left = [down_taps(pooled, 2 * p, 3, half_cols) for p in range(half_rows)]
    own = dot(jnp.concatenate(left, axis=0), down[...].reshape(-1, down.shape[-1]))
    out[0, :half_rows] = own.astype(BF16).reshape(half_rows, half_cols, -1)
    out[0, half_rows] = dot(down_taps(pooled, 0, 1, half_cols), down[2]).astype(BF16)


def column_taps(flat, cols):
    left, right = shifted_columns(flat, cols)
    return jnp.concatenate([left, flat, right], axis=1)


def coarse_sums(field, weight, a, sides):
    _, count, cols, channels = field.shape
    rows = count - 1
    taps = column_taps(field.reshape(count * cols, channels), cols)
    body, more = taps[: rows * cols], taps[rows * cols :]
    zero = jnp.zeros_like(more)
    tall = jnp.concatenate([jnp.where(has_above(), more, zero), body, zero], axis=0)
    dot = functools.partial(jnp.dot, preferred_element_type=F32)
    total = sum(dot(tall[b * cols : (b + rows) * cols], weight[a, b]) for b in range(3))
    head, tail = body[:cols], body[(rows - 1) * cols :]
    if sides == 1:
        up = has_above()
        first = jnp.concatenate([jnp.where(up, more, tail), jnp.where(up, head, zero)], axis=0)
        ends = [dot(first, weight[a, 2 * lax.axis_index("rows")])]
        second = [dot(jnp.where(up, more, zero), weight[a, 1])]
    else:
        first = jnp.concatenate([tail, zero], axis=0), jnp.concatenate([more, head], axis=0)
        ends = [dot(first[0], weight[a, 0]), dot(first[1], weight[a, 2])]
        second = [jnp.zeros((cols, weight.shape[-1]), F32), dot(more, weight[a, 1])]
    ends = [
        jnp.concatenate([end[:cols], end[cols:] + add], axis=0) for end, add in zip(ends, second)
    ]
    return total, ends


def coarse_first_kernel(field, weight, body, ends):
    total, parts = coarse_sums(field[...], weight, 2, ends.shape[0])
    body[...] = total
    for side, part in enumerate(parts):
        ends[side] = part


def coarse_next_kernel(field, weight, body_in, ends_in, body, ends):
    cells = field[...]
    cells = jnp.where(has_earlier(2), cells, jnp.zeros_like(cells))
    total, parts = coarse_sums(cells, weight, 0, ends.shape[0])
    body[...] = body_in[...] + total
    for side, part in enumerate(parts):
        ends[side] = ends_in[side] + part


def middle(direct, relayed):
    cells = jnp.where(lax.axis_index("tm") % 2 == 1, direct[...], relayed[...])
    return jnp.where(has_earlier(1), cells, jnp.zeros_like(cells))


def coarse_ends_kernel(direct, relayed, weight, ends, out):
    _, parts = coarse_sums(middle(direct, relayed), weight, 1, ends.shape[0])
    for side, part in enumerate(parts):
        out[side] = (ends[side] + part).astype(BF16)


def end_starts(rows, sides):
    return [(rows - 2) * (1 - lax.axis_index("rows"))] if sides == 1 else [0, rows - 2]


def coarse_body_kernel(direct, relayed, weight, body, out, ends, sums):
    _, rows, cols, _ = out.shape
    total, _ = coarse_sums(middle(direct, relayed), weight, 1, ends.shape[0])
    sums[...] = body[...] + total
    out[...] = silu(sums[...]).astype(BF16).reshape(out.shape)
    for side, start in enumerate(end_starts(rows, ends.shape[0])):
        ends[side] = sums[pl.ds(pl.multiple_of(start * cols, cols), 2 * cols), :]


def finish_kernel(ends, added, _, out, lines, sem):
    rows = out.shape[1]
    copies = []
    for side, start in enumerate(end_starts(rows, ends.shape[0])):
        total = ends[side] + added[side].astype(F32)
        lines[side] = silu(total).astype(BF16).reshape(lines.shape[1:])
        copies.append(
            pltpu.make_async_copy(lines.at[side], out.at[0, pl.ds(start, 2)], sem.at[side])
        )
        copies[-1].start()
    for copy in copies:
        copy.wait()


def call(kernel, out_shape, scratch, flops, args, in_place=False):
    size = sum(a.size * a.dtype.itemsize for a in args)
    vmem = pl.BlockSpec(memory_space=pltpu.VMEM)
    last = pl.BlockSpec(memory_space=pl.ANY) if in_place else vmem
    return pl.pallas_call(
        kernel,
        out_shape=out_shape,
        in_specs=[vmem] * (len(args) - 1) + [last] if args else [],
        out_specs=last if in_place else jax.tree.map(lambda _: vmem, out_shape),
        input_output_aliases={len(args) - 1: 0} if in_place else {},
        scratch_shapes=scratch,
        cost_estimate=pl.CostEstimate(flops=flops, bytes_accessed=size, transcendentals=0),
        compiler_params=pltpu.CompilerParams(vmem_limit_bytes=20 * 1024 * 1024),
    )(*args)


def local(frames, conv_fine, conv_down, conv_coarse):
    _, rows, cols, channels = frames.shape
    wide = conv_down.shape[-1]
    strips, times = lax.axis_size("rows"), lax.axis_size("tm")
    pace = call(pace_kernel, jax.ShapeDtypeStruct((8, 128), F32), [], 4 * 10**9, ())

    earlier = ring(frames, 1)
    (above, below), (above_1, below_1) = frame_rims(pace, frames)
    size = rows * cols
    pair = jax.ShapeDtypeStruct((size, 2 * channels), F32)
    flops = 2 * size * 18 * channels * 2 * channels
    own = call(fine_own_kernel, pair, [], flops, (frames, conv_fine))
    halo = call(
        functools.partial(fine_halo_kernel, rows=rows),
        jax.ShapeDtypeStruct((2, cols, 2 * channels), F32),
        [],
        flops // 3,
        (above, below, conv_fine),
    )
    half_rows, half_cols = rows // 2, cols // 2
    shape = jax.ShapeDtypeStruct((1, half_rows, half_cols, wide), BF16)
    fine_sums = call(fine_rest_kernel, pair, [], flops, (earlier, conv_fine, own, halo))
    above_1, below_1, fine_sums = lax.optimization_barrier((above_1, below_1, fine_sums))
    field = call(
        reduce_kernel,
        jax.ShapeDtypeStruct((1, half_rows + 1, half_cols, wide), BF16),
        [pltpu.VMEM((rows + 1, cols + 8, channels), F32)],
        flops // 3,
        (above_1, below_1, conv_fine, fine_sums, conv_down),
    )
    sides = 1 if strips == 2 else 2
    sums = jax.ShapeDtypeStruct((half_rows * half_cols, wide), F32)
    pairs = jax.ShapeDtypeStruct((sides, 2 * half_cols, wide), F32)
    flops = 2 * half_rows * half_cols * 9 * wide * wide
    field_2 = moved(field, 2, 0)
    near = paired if times % 2 == 0 else functools.partial(ring, steps=1)
    direct = near(field)
    body, ends = call(coarse_first_kernel, (sums, pairs), [], flops, (field, conv_coarse))
    field_2, body, ends, direct = lax.optimization_barrier((field_2, body, ends, direct))
    relayed = paired(field_2) if times % 2 == 0 else direct
    body, ends = call(
        coarse_next_kernel, (sums, pairs), [], flops, (field_2, conv_coarse, body, ends)
    )
    sent = call(
        coarse_ends_kernel,
        jax.ShapeDtypeStruct(pairs.shape, BF16),
        [],
        flops // 4,
        (direct, relayed, conv_coarse, ends),
    )
    if sides == 1:
        added = swapped(sent, 0)
    else:
        added = jnp.concatenate([moved(sent[:1], 0, 1), moved(sent[1:], 0, -1)], axis=0)
    out, end_sums = call(
        coarse_body_kernel,
        (shape, pairs),
        [pltpu.VMEM(sums.shape, F32)],
        flops,
        (direct, relayed, conv_coarse, body),
    )
    return call(
        finish_kernel,
        shape,
        [pltpu.VMEM((sides, 2, half_cols, wide), BF16), pltpu.SemaphoreType.DMA((sides,))],
        flops // 16,
        (end_sums, added, out),
        in_place=True,
    )


def solution(mesh):
    placed = (P("tm", "rows", None, None), P(), P(), P())
    return jax.shard_map(local, mesh=mesh, in_specs=placed, out_specs=P("tm", "rows", None, None), check_vma=False)
```

```python
import functools

import jax
import jax.numpy as jnp
from jax import lax
from jax.experimental import pallas as pl
from jax.experimental.pallas import tpu as pltpu
from jax.sharding import PartitionSpec as P


F32 = jnp.float32
BF16 = jnp.bfloat16


def moved(value, steps, hop):
    tm, rows = lax.axis_size("tm"), lax.axis_size("rows")
    pairs = [
        (t * rows + r, (t + steps) * rows + r + hop)
        for t in range(tm - steps)
        for r in range(rows)
        if 0 <= r + hop < rows
    ]
    return lax.ppermute(value, ("tm", "rows"), pairs)


def ring(value, steps):
    tm = lax.axis_size("tm")
    return lax.ppermute(value, "tm", [(t, (t + steps) % tm) for t in range(tm)])


def swapped(value, steps):
    tm = lax.axis_size("tm")
    pairs = [(t * 2 + r, (t + steps) * 2 + 1 - r) for t in range(tm - steps) for r in range(2)]
    return lax.ppermute(value, ("tm", "rows"), pairs)


def by_parity(value, odd):
    tm = lax.axis_size("tm")
    if odd:
        count = tm // 2
        pairs = [(t, t if t % 2 == 0 else (t // 2 + 1) % count * 2 + 1) for t in range(tm)]
    else:
        pairs = [(t, t + 2) for t in range(0, tm - 2, 2)]
    return lax.ppermute(value, "tm", pairs)


def paired(value):
    return lax.ppermute(value, "tm", [(t, t ^ 1) for t in range(lax.axis_size("tm"))])


def has_above():
    return lax.axis_index("rows") > 0


def has_below():
    return lax.axis_index("rows") < lax.axis_size("rows") - 1


def has_earlier(steps):
    return lax.axis_index("tm") >= steps


def pace_kernel(out):
    out[...] = jnp.zeros_like(out)


def edge_kernel(_, cells, out):
    width = out.shape[1]
    first = (1 - lax.axis_index("rows")) * (cells.shape[1] - width)
    out[...] = cells[:, pl.ds(first, width)]


def frame_rims(pace, frames):
    rows = frames.shape[1]
    if lax.axis_size("rows") == 2:
        sent = call(
            edge_kernel,
            jax.ShapeDtypeStruct((frames.shape[0], 1, *frames.shape[2:]), BF16),
            [],
            0,
            (pace, frames),
        )
        return [(both, both) for both in (swapped(sent, 0), swapped(sent, 1))]
    head, tail = frames[:, :1], frames[:, rows - 1 :]
    return [(moved(tail, steps, 1), moved(head, steps, -1)) for steps in (0, 1)]


def column_shift(value, cols, steps):
    size = value.shape[0]
    column = lax.broadcasted_iota(jnp.int32, value.shape, 0) % cols
    edge = 0 if steps > 0 else cols - 1
    return jnp.where(column == edge, 0.0, pltpu.roll(value, steps % size, 0))


def shifted_columns(flat, cols):
    wide = flat.astype(F32)
    return column_shift(wide, cols, 1).astype(BF16), column_shift(wide, cols, -1).astype(BF16)


def tap_matrix(weight, first_tap, row_taps, e, channels):
    zero = jnp.zeros((channels, channels), BF16)

    def pick(tap, b):
        return weight[tap, b, e * channels : (e + 1) * channels] if 0 <= tap <= 2 else zero

    return jnp.concatenate(
        [
            jnp.concatenate([pick(first_tap + f, b), pick(first_tap + f - 1, b)], axis=1)
            for f in range(2)
            for b in row_taps
        ],
        axis=0,
    )


def fine_rows(row, outs, row_taps, weight, first_tap):
    channels = weight.shape[-1]
    some = next(x for f in range(2) for r in outs for b in row_taps if (x := row(f, r - 1 + b)) is not None)
    cols = some.shape[0]
    zero = jnp.zeros((cols, channels), BF16)

    def cell(f, i):
        found = row(f, i)
        return zero if found is None else found

    left = jnp.concatenate(
        [
            jnp.concatenate([cell(f, r - 1 + b) for f in range(2) for b in row_taps], axis=1)
            for r in outs
        ],
        axis=0,
    )
    sums = [
        jnp.dot(
            left, tap_matrix(weight, first_tap, row_taps, e, channels), preferred_element_type=F32
        )
        for e in range(3)
    ]
    return sums[1] + column_shift(sums[0], cols, 1) + column_shift(sums[2], cols, -1)


def chunks_of(count):
    size = next(c for c in (4, 3, 2, 1) if count % c == 0)
    return [range(i, i + size) for i in range(0, count, size)]


def fine_own_kernel(frames, weight, out):
    _, rows, cols, _ = frames.shape

    def row(f, i):
        return frames[f, i] if 0 <= i < rows else None

    for outs in chunks_of(rows):
        out[outs[0] * cols : (outs[-1] + 1) * cols] = fine_rows(row, outs, range(3), weight, 2)


def halo_sums(above, below, weight, first_tap, rows):
    def row(f, i):
        if i == -1:
            cells, have = above[f, 0], has_above()
        else:
            cells, have = below[f, 0], has_below()
        return jnp.where(have, cells, jnp.zeros_like(cells))

    return (
        fine_rows(row, [0], [0], weight, first_tap),
        fine_rows(row, [rows - 1], [2], weight, first_tap),
    )


def fine_halo_kernel(above, below, weight, out, *, rows):
    out[0], out[1] = halo_sums(above, below, weight, 2, rows)


def silu(v):
    return v / (1.0 + jnp.exp(-v))


def fine_rest_kernel(frames, weight, own, halo, out):
    _, rows, cols, _ = frames.shape

    def row(f, i):
        return frames[f, i] if 0 <= i < rows else None

    for outs in chunks_of(rows):
        total = jnp.where(has_earlier(1), fine_rows(row, outs, range(3), weight, 0), 0.0)
        for i, r in enumerate(outs):
            line = total[i * cols : (i + 1) * cols] + own[r * cols : (r + 1) * cols]
            for k, halo_r in enumerate((0, rows - 1)):
                if r == halo_r:
                    line = line + halo[k]
            out[r * cols : (r + 1) * cols] = line


def pool(sums):
    channels = sums.shape[1] // 2
    fine = silu(sums).astype(BF16).astype(F32)
    return ((fine[:, :channels] + fine[:, channels:]) * 0.5).astype(BF16).astype(F32)


def down_taps(pooled, first, row_taps, half_cols):
    pieces = [
        pooled[first + i, pl.ds(e, half_cols, stride=2), :].astype(BF16)
        for i in range(row_taps)
        for e in range(3)
    ]
    return jnp.concatenate(pieces, axis=1)


def put_pooled(pooled, lines):
    cols = lines[0].shape[0]
    pad = pooled.shape[1] - cols
    pooled[:, cols:] = jnp.zeros((pooled.shape[0], pad, pooled.shape[2]), F32)
    for i, line in enumerate(lines):
        pooled[i, :cols] = line


def reduce_kernel(above, below, weight, sums, down, out, pooled):
    cols = above.shape[2]
    rows = sums.shape[0] // cols
    half_rows, half_cols = rows // 2, cols // 2
    top, bottom = halo_sums(above, below, weight, 0, rows)
    lines = []
    for r in range(rows):
        line = sums[r * cols : (r + 1) * cols]
        if r == 0:
            line = line + top
        if r == rows - 1:
            line = line + bottom
        lines.append(pool(line))
    put_pooled(pooled, [*lines, jnp.zeros_like(lines[0])])
    dot = functools.partial(jnp.dot, preferred_element_type=F32)
    left = [down_taps(pooled, 2 * p, 3, half_cols) for p in range(half_rows)]
    own = dot(jnp.concatenate(left, axis=0), down[...].reshape(-1, down.shape[-1]))
    out[0, :half_rows] = own.astype(BF16).reshape(half_rows, half_cols, -1)
    out[0, half_rows] = dot(down_taps(pooled, 0, 1, half_cols), down[2]).astype(BF16)


def column_taps(flat, cols):
    left, right = shifted_columns(flat, cols)
    return jnp.concatenate([left, flat, right], axis=1)


def coarse_sums(field, weight, a, sides):
    _, count, cols, channels = field.shape
    rows = count - 1
    taps = column_taps(field.reshape(count * cols, channels), cols)
    body, more = taps[: rows * cols], taps[rows * cols :]
    zero = jnp.zeros_like(more)
    tall = jnp.concatenate([jnp.where(has_above(), more, zero), body, zero], axis=0)
    dot = functools.partial(jnp.dot, preferred_element_type=F32)
    total = sum(dot(tall[b * cols : (b + rows) * cols], weight[a, b]) for b in range(3))
    head, tail = body[:cols], body[(rows - 1) * cols :]
    if sides == 1:
        up = has_above()
        first = jnp.concatenate([jnp.where(up, more, tail), jnp.where(up, head, zero)], axis=0)
        ends = [dot(first, weight[a, 2 * lax.axis_index("rows")])]
        second = [dot(jnp.where(up, more, zero), weight[a, 1])]
    else:
        first = jnp.concatenate([tail, zero], axis=0), jnp.concatenate([more, head], axis=0)
        ends = [dot(first[0], weight[a, 0]), dot(first[1], weight[a, 2])]
        second = [jnp.zeros((cols, weight.shape[-1]), F32), dot(more, weight[a, 1])]
    ends = [
        jnp.concatenate([end[:cols], end[cols:] + add], axis=0) for end, add in zip(ends, second)
    ]
    return total, ends


def coarse_first_kernel(field, weight, body, ends):
    total, parts = coarse_sums(field[...], weight, 2, ends.shape[0])
    body[...] = total
    for side, part in enumerate(parts):
        ends[side] = part


def coarse_next_kernel(field, weight, body_in, ends_in, body, ends):
    cells = field[...]
    cells = jnp.where(has_earlier(1), cells, jnp.zeros_like(cells))
    total, parts = coarse_sums(cells, weight, 1, ends.shape[0])
    body[...] = body_in[...] + total
    for side, part in enumerate(parts):
        ends[side] = ends_in[side] + part


def second_earlier(odd_field, even_field):
    cells = jnp.where(lax.axis_index("tm") % 2 == 1, odd_field[...], even_field[...])
    return jnp.where(has_earlier(2), cells, jnp.zeros_like(cells))


def coarse_ends_kernel(odd_field, even_field, weight, ends, out):
    _, parts = coarse_sums(second_earlier(odd_field, even_field), weight, 0, ends.shape[0])
    for side, part in enumerate(parts):
        out[side] = (ends[side] + part).astype(BF16)


def end_starts(rows, sides):
    return [(rows - 2) * (1 - lax.axis_index("rows"))] if sides == 1 else [0, rows - 2]


def coarse_body_kernel(odd_field, even_field, weight, body, out, ends, sums):
    _, rows, cols, _ = out.shape
    total, _ = coarse_sums(second_earlier(odd_field, even_field), weight, 0, ends.shape[0])
    sums[...] = body[...] + total
    out[...] = silu(sums[...]).astype(BF16).reshape(out.shape)
    for side, start in enumerate(end_starts(rows, ends.shape[0])):
        ends[side] = sums[pl.ds(pl.multiple_of(start * cols, cols), 2 * cols), :]


def finish_kernel(ends, added, _, out, lines, sem):
    rows = out.shape[1]
    copies = []
    for side, start in enumerate(end_starts(rows, ends.shape[0])):
        total = ends[side] + added[side].astype(F32)
        lines[side] = silu(total).astype(BF16).reshape(lines.shape[1:])
        copies.append(
            pltpu.make_async_copy(lines.at[side], out.at[0, pl.ds(start, 2)], sem.at[side])
        )
        copies[-1].start()
    for copy in copies:
        copy.wait()


def call(kernel, out_shape, scratch, flops, args, in_place=False):
    size = sum(a.size * a.dtype.itemsize for a in args)
    vmem = pl.BlockSpec(memory_space=pltpu.VMEM)
    last = pl.BlockSpec(memory_space=pl.ANY) if in_place else vmem
    return pl.pallas_call(
        kernel,
        out_shape=out_shape,
        in_specs=[vmem] * (len(args) - 1) + [last] if args else [],
        out_specs=last if in_place else jax.tree.map(lambda _: vmem, out_shape),
        input_output_aliases={len(args) - 1: 0} if in_place else {},
        scratch_shapes=scratch,
        cost_estimate=pl.CostEstimate(flops=flops, bytes_accessed=size, transcendentals=0),
        compiler_params=pltpu.CompilerParams(vmem_limit_bytes=20 * 1024 * 1024),
    )(*args)


def local(frames, conv_fine, conv_down, conv_coarse):
    _, rows, cols, channels = frames.shape
    wide = conv_down.shape[-1]
    strips, times = lax.axis_size("rows"), lax.axis_size("tm")
    pace = call(pace_kernel, jax.ShapeDtypeStruct((8, 128), F32), [], 4 * 10**9, ())

    earlier = ring(frames, 1)
    (above, below), (above_1, below_1) = frame_rims(pace, frames)
    size = rows * cols
    pair = jax.ShapeDtypeStruct((size, 2 * channels), F32)
    flops = 2 * size * 18 * channels * 2 * channels
    own = call(fine_own_kernel, pair, [], flops, (frames, conv_fine))
    halo = call(
        functools.partial(fine_halo_kernel, rows=rows),
        jax.ShapeDtypeStruct((2, cols, 2 * channels), F32),
        [],
        flops // 3,
        (above, below, conv_fine),
    )
    half_rows, half_cols = rows // 2, cols // 2
    shape = jax.ShapeDtypeStruct((1, half_rows, half_cols, wide), BF16)
    fine_sums = call(fine_rest_kernel, pair, [], flops, (earlier, conv_fine, own, halo))
    above_1, below_1, fine_sums = lax.optimization_barrier((above_1, below_1, fine_sums))
    field = call(
        reduce_kernel,
        jax.ShapeDtypeStruct((1, half_rows + 1, half_cols, wide), BF16),
        [pltpu.VMEM((rows + 1, cols + 8, channels), F32)],
        flops // 3,
        (above_1, below_1, conv_fine, fine_sums, conv_down),
    )
    sides = 1 if strips == 2 else 2
    sums = jax.ShapeDtypeStruct((half_rows * half_cols, wide), F32)
    pairs = jax.ShapeDtypeStruct((sides, 2 * half_cols, wide), F32)
    flops = 2 * half_rows * half_cols * 9 * wide * wide
    odd_field = by_parity(field, True)
    even_field = by_parity(field, False)
    body, ends = call(coarse_first_kernel, (sums, pairs), [], flops, (field, conv_coarse))
    odd_field, body, ends = lax.optimization_barrier((odd_field, body, ends))
    field_1 = paired(odd_field) if times % 2 == 0 else ring(field, 1)
    body, ends = call(
        coarse_next_kernel, (sums, pairs), [], flops, (field_1, conv_coarse, body, ends)
    )
    even_field, body, ends = lax.optimization_barrier((even_field, body, ends))
    sent = call(
        coarse_ends_kernel,
        jax.ShapeDtypeStruct(pairs.shape, BF16),
        [],
        flops // 4,
        (odd_field, even_field, conv_coarse, ends),
    )
    if sides == 1:
        added = swapped(sent, 0)
    else:
        added = jnp.concatenate([moved(sent[:1], 0, 1), moved(sent[1:], 0, -1)], axis=0)
    out, end_sums = call(
        coarse_body_kernel,
        (shape, pairs),
        [pltpu.VMEM(sums.shape, F32)],
        flops,
        (odd_field, even_field, conv_coarse, body),
    )
    return call(
        finish_kernel,
        shape,
        [pltpu.VMEM((sides, 2, half_cols, wide), BF16), pltpu.SemaphoreType.DMA((sides,))],
        flops // 16,
        (end_sums, added, out),
        in_place=True,
    )


def solution(mesh):
    placed = (P("tm", "rows", None, None), P(), P(), P())
    return jax.shard_map(local, mesh=mesh, in_specs=placed, out_specs=P("tm", "rows", None, None), check_vma=False)
```

```python
import functools

import jax
import jax.numpy as jnp
from jax import lax
from jax.experimental import pallas as pl
from jax.experimental.pallas import tpu as pltpu
from jax.sharding import PartitionSpec as P


F32 = jnp.float32
BF16 = jnp.bfloat16


def moved(value, steps, hop):
    tm, rows = lax.axis_size("tm"), lax.axis_size("rows")
    pairs = [
        (t * rows + r, (t + steps) * rows + r + hop)
        for t in range(tm - steps)
        for r in range(rows)
        if 0 <= r + hop < rows
    ]
    return lax.ppermute(value, ("tm", "rows"), pairs)


def ring(value, steps):
    tm = lax.axis_size("tm")
    return lax.ppermute(value, "tm", [(t, (t + steps) % tm) for t in range(tm)])


def swapped(value, steps):
    tm = lax.axis_size("tm")
    pairs = [(t * 2 + r, (t + steps) * 2 + 1 - r) for t in range(tm - steps) for r in range(2)]
    return lax.ppermute(value, ("tm", "rows"), pairs)


def by_parity(value, odd):
    tm = lax.axis_size("tm")
    pairs = [(t, t + 2) for t in range(odd, tm - 2, 2)]
    if odd:
        pairs += [(t, t) for t in range(0, tm, 2)]
    return lax.ppermute(value, "tm", pairs)


def paired(value):
    return lax.ppermute(value, "tm", [(t, t ^ 1) for t in range(lax.axis_size("tm"))])


def has_above():
    return lax.axis_index("rows") > 0


def has_below():
    return lax.axis_index("rows") < lax.axis_size("rows") - 1


def has_earlier(steps):
    return lax.axis_index("tm") >= steps


def pace_kernel(out):
    out[...] = jnp.zeros_like(out)


def edge_kernel(_, cells, out):
    width = out.shape[1]
    first = (1 - lax.axis_index("rows")) * (cells.shape[1] - width)
    out[...] = cells[:, pl.ds(first, width)]


def frame_rims(pace, frames):
    rows = frames.shape[1]
    if lax.axis_size("rows") == 2:
        sent = call(
            edge_kernel,
            jax.ShapeDtypeStruct((frames.shape[0], 1, *frames.shape[2:]), BF16),
            [],
            0,
            (pace, frames),
        )
        return [(both, both) for both in (swapped(sent, 0), swapped(sent, 1))]
    head, tail = frames[:, :1], frames[:, rows - 1 :]
    return [(moved(tail, steps, 1), moved(head, steps, -1)) for steps in (0, 1)]


def column_shift(value, cols, steps):
    size = value.shape[0]
    column = lax.broadcasted_iota(jnp.int32, value.shape, 0) % cols
    edge = 0 if steps > 0 else cols - 1
    return jnp.where(column == edge, 0.0, pltpu.roll(value, steps % size, 0))


def shifted_columns(flat, cols):
    wide = flat.astype(F32)
    return column_shift(wide, cols, 1).astype(BF16), column_shift(wide, cols, -1).astype(BF16)


def tap_matrix(weight, first_tap, row_taps, e, channels):
    zero = jnp.zeros((channels, channels), BF16)

    def pick(tap, b):
        return weight[tap, b, e * channels : (e + 1) * channels] if 0 <= tap <= 2 else zero

    return jnp.concatenate(
        [
            jnp.concatenate([pick(first_tap + f, b), pick(first_tap + f - 1, b)], axis=1)
            for f in range(2)
            for b in row_taps
        ],
        axis=0,
    )


def fine_rows(row, outs, row_taps, weight, first_tap):
    channels = weight.shape[-1]
    some = next(x for f in range(2) for r in outs for b in row_taps if (x := row(f, r - 1 + b)) is not None)
    cols = some.shape[0]
    zero = jnp.zeros((cols, channels), BF16)

    def cell(f, i):
        found = row(f, i)
        return zero if found is None else found

    left = jnp.concatenate(
        [
            jnp.concatenate([cell(f, r - 1 + b) for f in range(2) for b in row_taps], axis=1)
            for r in outs
        ],
        axis=0,
    )
    sums = [
        jnp.dot(
            left, tap_matrix(weight, first_tap, row_taps, e, channels), preferred_element_type=F32
        )
        for e in range(3)
    ]
    return sums[1] + column_shift(sums[0], cols, 1) + column_shift(sums[2], cols, -1)


def chunks_of(count):
    size = next(c for c in (4, 3, 2, 1) if count % c == 0)
    return [range(i, i + size) for i in range(0, count, size)]


def fine_own_kernel(frames, weight, out):
    _, rows, cols, _ = frames.shape

    def row(f, i):
        return frames[f, i] if 0 <= i < rows else None

    for outs in chunks_of(rows):
        out[outs[0] * cols : (outs[-1] + 1) * cols] = fine_rows(row, outs, range(3), weight, 2)


def halo_sums(above, below, weight, first_tap, rows):
    def row(f, i):
        if i == -1:
            cells, have = above[f, 0], has_above()
        else:
            cells, have = below[f, 0], has_below()
        return jnp.where(have, cells, jnp.zeros_like(cells))

    return (
        fine_rows(row, [0], [0], weight, first_tap),
        fine_rows(row, [rows - 1], [2], weight, first_tap),
    )


def fine_halo_kernel(above, below, weight, out, *, rows):
    out[0], out[1] = halo_sums(above, below, weight, 2, rows)


def silu(v):
    return v / (1.0 + jnp.exp(-v))


def fine_rest_kernel(frames, weight, own, halo, out):
    _, rows, cols, _ = frames.shape

    def row(f, i):
        return frames[f, i] if 0 <= i < rows else None

    for outs in chunks_of(rows):
        total = jnp.where(has_earlier(1), fine_rows(row, outs, range(3), weight, 0), 0.0)
        for i, r in enumerate(outs):
            line = total[i * cols : (i + 1) * cols] + own[r * cols : (r + 1) * cols]
            for k, halo_r in enumerate((0, rows - 1)):
                if r == halo_r:
                    line = line + halo[k]
            out[r * cols : (r + 1) * cols] = line


def pool(sums):
    channels = sums.shape[1] // 2
    fine = silu(sums).astype(BF16).astype(F32)
    return ((fine[:, :channels] + fine[:, channels:]) * 0.5).astype(BF16).astype(F32)


def down_taps(pooled, first, row_taps, half_cols):
    pieces = [
        pooled[first + i, pl.ds(e, half_cols, stride=2), :].astype(BF16)
        for i in range(row_taps)
        for e in range(3)
    ]
    return jnp.concatenate(pieces, axis=1)


def put_pooled(pooled, lines):
    cols = lines[0].shape[0]
    pad = pooled.shape[1] - cols
    pooled[:, cols:] = jnp.zeros((pooled.shape[0], pad, pooled.shape[2]), F32)
    for i, line in enumerate(lines):
        pooled[i, :cols] = line


def reduce_kernel(above, below, weight, sums, down, out, pooled):
    cols = above.shape[2]
    rows = sums.shape[0] // cols
    half_rows, half_cols = rows // 2, cols // 2
    top, bottom = halo_sums(above, below, weight, 0, rows)
    lines = []
    for r in range(rows):
        line = sums[r * cols : (r + 1) * cols]
        if r == 0:
            line = line + top
        if r == rows - 1:
            line = line + bottom
        lines.append(pool(line))
    put_pooled(pooled, [*lines, jnp.zeros_like(lines[0])])
    dot = functools.partial(jnp.dot, preferred_element_type=F32)
    left = [down_taps(pooled, 2 * p, 3, half_cols) for p in range(half_rows)]
    own = dot(jnp.concatenate(left, axis=0), down[...].reshape(-1, down.shape[-1]))
    out[0, :half_rows] = own.astype(BF16).reshape(half_rows, half_cols, -1)
    out[0, half_rows] = dot(down_taps(pooled, 0, 1, half_cols), down[2]).astype(BF16)


def column_taps(flat, cols):
    left, right = shifted_columns(flat, cols)
    return jnp.concatenate([left, flat, right], axis=1)


def coarse_sums(field, weight, a, sides):
    _, count, cols, channels = field.shape
    rows = count - 1
    taps = column_taps(field.reshape(count * cols, channels), cols)
    body, more = taps[: rows * cols], taps[rows * cols :]
    zero = jnp.zeros_like(more)
    tall = jnp.concatenate([jnp.where(has_above(), more, zero), body, zero], axis=0)
    dot = functools.partial(jnp.dot, preferred_element_type=F32)
    total = sum(dot(tall[b * cols : (b + rows) * cols], weight[a, b]) for b in range(3))
    head, tail = body[:cols], body[(rows - 1) * cols :]
    if sides == 1:
        up = has_above()
        first = jnp.concatenate([jnp.where(up, more, tail), jnp.where(up, head, zero)], axis=0)
        ends = [dot(first, weight[a, 2 * lax.axis_index("rows")])]
        second = [dot(jnp.where(up, more, zero), weight[a, 1])]
    else:
        first = jnp.concatenate([tail, zero], axis=0), jnp.concatenate([more, head], axis=0)
        ends = [dot(first[0], weight[a, 0]), dot(first[1], weight[a, 2])]
        second = [jnp.zeros((cols, weight.shape[-1]), F32), dot(more, weight[a, 1])]
    ends = [
        jnp.concatenate([end[:cols], end[cols:] + add], axis=0) for end, add in zip(ends, second)
    ]
    return total, ends


def coarse_first_kernel(field, weight, body, ends):
    total, parts = coarse_sums(field[...], weight, 2, ends.shape[0])
    body[...] = total
    for side, part in enumerate(parts):
        ends[side] = part


def coarse_next_kernel(field, weight, body_in, ends_in, body, ends):
    cells = field[...]
    cells = jnp.where(has_earlier(1), cells, jnp.zeros_like(cells))
    total, parts = coarse_sums(cells, weight, 1, ends.shape[0])
    body[...] = body_in[...] + total
    for side, part in enumerate(parts):
        ends[side] = ends_in[side] + part


def second_earlier(odd_field, even_field):
    cells = jnp.where(lax.axis_index("tm") % 2 == 1, odd_field[...], even_field[...])
    return jnp.where(has_earlier(2), cells, jnp.zeros_like(cells))


def coarse_ends_kernel(odd_field, even_field, weight, ends, out):
    _, parts = coarse_sums(second_earlier(odd_field, even_field), weight, 0, ends.shape[0])
    for side, part in enumerate(parts):
        out[side] = (ends[side] + part).astype(BF16)


def end_starts(rows, sides):
    return [(rows - 2) * (1 - lax.axis_index("rows"))] if sides == 1 else [0, rows - 2]


def coarse_body_kernel(odd_field, even_field, weight, body, out, ends, sums):
    _, rows, cols, _ = out.shape
    total, _ = coarse_sums(second_earlier(odd_field, even_field), weight, 0, ends.shape[0])
    sums[...] = body[...] + total
    out[...] = silu(sums[...]).astype(BF16).reshape(out.shape)
    for side, start in enumerate(end_starts(rows, ends.shape[0])):
        ends[side] = sums[pl.ds(pl.multiple_of(start * cols, cols), 2 * cols), :]


def finish_kernel(ends, added, _, out, lines, sem):
    rows = out.shape[1]
    copies = []
    for side, start in enumerate(end_starts(rows, ends.shape[0])):
        total = ends[side] + added[side].astype(F32)
        lines[side] = silu(total).astype(BF16).reshape(lines.shape[1:])
        copies.append(
            pltpu.make_async_copy(lines.at[side], out.at[0, pl.ds(start, 2)], sem.at[side])
        )
        copies[-1].start()
    for copy in copies:
        copy.wait()


def call(kernel, out_shape, scratch, flops, args, in_place=False):
    size = sum(a.size * a.dtype.itemsize for a in args)
    vmem = pl.BlockSpec(memory_space=pltpu.VMEM)
    last = pl.BlockSpec(memory_space=pl.ANY) if in_place else vmem
    return pl.pallas_call(
        kernel,
        out_shape=out_shape,
        in_specs=[vmem] * (len(args) - 1) + [last] if args else [],
        out_specs=last if in_place else jax.tree.map(lambda _: vmem, out_shape),
        input_output_aliases={len(args) - 1: 0} if in_place else {},
        scratch_shapes=scratch,
        cost_estimate=pl.CostEstimate(flops=flops, bytes_accessed=size, transcendentals=0),
        compiler_params=pltpu.CompilerParams(vmem_limit_bytes=20 * 1024 * 1024),
    )(*args)


def local(frames, conv_fine, conv_down, conv_coarse):
    _, rows, cols, channels = frames.shape
    wide = conv_down.shape[-1]
    strips, times = lax.axis_size("rows"), lax.axis_size("tm")
    pace = call(pace_kernel, jax.ShapeDtypeStruct((8, 128), F32), [], 4 * 10**9, ())

    earlier = ring(frames, 1)
    (above, below), (above_1, below_1) = frame_rims(pace, frames)
    size = rows * cols
    pair = jax.ShapeDtypeStruct((size, 2 * channels), F32)
    flops = 2 * size * 18 * channels * 2 * channels
    own = call(fine_own_kernel, pair, [], flops, (frames, conv_fine))
    halo = call(
        functools.partial(fine_halo_kernel, rows=rows),
        jax.ShapeDtypeStruct((2, cols, 2 * channels), F32),
        [],
        flops // 3,
        (above, below, conv_fine),
    )
    half_rows, half_cols = rows // 2, cols // 2
    shape = jax.ShapeDtypeStruct((1, half_rows, half_cols, wide), BF16)
    fine_sums = call(fine_rest_kernel, pair, [], flops, (earlier, conv_fine, own, halo))
    above_1, below_1, fine_sums = lax.optimization_barrier((above_1, below_1, fine_sums))
    field = call(
        reduce_kernel,
        jax.ShapeDtypeStruct((1, half_rows + 1, half_cols, wide), BF16),
        [pltpu.VMEM((rows + 1, cols + 8, channels), F32)],
        flops // 3,
        (above_1, below_1, conv_fine, fine_sums, conv_down),
    )
    sides = 1 if strips == 2 else 2
    sums = jax.ShapeDtypeStruct((half_rows * half_cols, wide), F32)
    pairs = jax.ShapeDtypeStruct((sides, 2 * half_cols, wide), F32)
    flops = 2 * half_rows * half_cols * 9 * wide * wide
    odd_field = by_parity(field, 1)
    even_field = by_parity(field, 0)
    body, ends = call(coarse_first_kernel, (sums, pairs), [], flops, (field, conv_coarse))
    odd_field, body, ends = lax.optimization_barrier((odd_field, body, ends))
    field_1 = paired(odd_field) if times % 2 == 0 else ring(field, 1)
    body, ends = call(
        coarse_next_kernel, (sums, pairs), [], flops, (field_1, conv_coarse, body, ends)
    )
    even_field, body, ends = lax.optimization_barrier((even_field, body, ends))
    sent = call(
        coarse_ends_kernel,
        jax.ShapeDtypeStruct(pairs.shape, BF16),
        [],
        flops // 4,
        (odd_field, even_field, conv_coarse, ends),
    )
    if sides == 1:
        added = swapped(sent, 0)
    else:
        added = jnp.concatenate([moved(sent[:1], 0, 1), moved(sent[1:], 0, -1)], axis=0)
    out, end_sums = call(
        coarse_body_kernel,
        (shape, pairs),
        [pltpu.VMEM(sums.shape, F32)],
        flops,
        (odd_field, even_field, conv_coarse, body),
    )
    return call(
        finish_kernel,
        shape,
        [pltpu.VMEM((sides, 2, half_cols, wide), BF16), pltpu.SemaphoreType.DMA((sides,))],
        flops // 16,
        (end_sums, added, out),
        in_place=True,
    )


def solution(mesh):
    placed = (P("tm", "rows", None, None), P(), P(), P())
    return jax.shard_map(local, mesh=mesh, in_specs=placed, out_specs=P("tm", "rows", None, None), check_vma=False)
```

```python
import functools

import jax
import jax.numpy as jnp
from jax import lax
from jax.experimental import pallas as pl
from jax.experimental.pallas import tpu as pltpu
from jax.sharding import PartitionSpec as P


F32 = jnp.float32
BF16 = jnp.bfloat16


def moved(value, steps, hop):
    tm, rows = lax.axis_size("tm"), lax.axis_size("rows")
    pairs = [
        (t * rows + r, (t + steps) * rows + r + hop)
        for t in range(tm - steps)
        for r in range(rows)
        if 0 <= r + hop < rows
    ]
    return lax.ppermute(value, ("tm", "rows"), pairs)


def ring(value, steps):
    tm = lax.axis_size("tm")
    return lax.ppermute(value, "tm", [(t, (t + steps) % tm) for t in range(tm)])


def swapped(value, steps):
    tm = lax.axis_size("tm")
    pairs = [(t * 2 + r, (t + steps) * 2 + 1 - r) for t in range(tm - steps) for r in range(2)]
    return lax.ppermute(value, ("tm", "rows"), pairs)


def by_parity(value, odd):
    tm = lax.axis_size("tm")
    pairs = [(t, t + 2) for t in range(odd, tm - 2, 2)]
    if odd:
        pairs += [(t, t) for t in range(0, tm, 2)]
    return lax.ppermute(value, "tm", pairs)


def paired(value):
    return lax.ppermute(value, "tm", [(t, t ^ 1) for t in range(lax.axis_size("tm"))])


def has_above():
    return lax.axis_index("rows") > 0


def has_below():
    return lax.axis_index("rows") < lax.axis_size("rows") - 1


def has_earlier(steps):
    return lax.axis_index("tm") >= steps


def pace_kernel(out):
    out[...] = jnp.zeros_like(out)


def edge_kernel(_, cells, out):
    width = out.shape[1]
    first = (1 - lax.axis_index("rows")) * (cells.shape[1] - width)
    out[...] = cells[:, pl.ds(first, width)]


def frame_rims(pace, frames):
    rows = frames.shape[1]
    if lax.axis_size("rows") == 2:
        sent = call(
            edge_kernel,
            jax.ShapeDtypeStruct((frames.shape[0], 1, *frames.shape[2:]), BF16),
            [],
            0,
            (pace, frames),
        )
        return [(both, both) for both in (swapped(sent, 0), swapped(sent, 1))]
    head, tail = frames[:, :1], frames[:, rows - 1 :]
    return [(moved(tail, steps, 1), moved(head, steps, -1)) for steps in (0, 1)]


def column_shift(value, cols, steps):
    size = value.shape[0]
    column = lax.broadcasted_iota(jnp.int32, value.shape, 0) % cols
    edge = 0 if steps > 0 else cols - 1
    return jnp.where(column == edge, 0.0, pltpu.roll(value, steps % size, 0))


def shifted_columns(flat, cols):
    wide = flat.astype(F32)
    return column_shift(wide, cols, 1).astype(BF16), column_shift(wide, cols, -1).astype(BF16)


def tap_matrix(weight, first_tap, row_taps, e, channels):
    zero = jnp.zeros((channels, channels), BF16)

    def pick(tap, b):
        return weight[tap, b, e * channels : (e + 1) * channels] if 0 <= tap <= 2 else zero

    return jnp.concatenate(
        [
            jnp.concatenate([pick(first_tap + f, b), pick(first_tap + f - 1, b)], axis=1)
            for f in range(2)
            for b in row_taps
        ],
        axis=0,
    )


def fine_rows(row, outs, row_taps, weight, first_tap):
    channels = weight.shape[-1]
    some = next(x for f in range(2) for r in outs for b in row_taps if (x := row(f, r - 1 + b)) is not None)
    cols = some.shape[0]
    zero = jnp.zeros((cols, channels), BF16)

    def cell(f, i):
        found = row(f, i)
        return zero if found is None else found

    left = jnp.concatenate(
        [
            jnp.concatenate([cell(f, r - 1 + b) for f in range(2) for b in row_taps], axis=1)
            for r in outs
        ],
        axis=0,
    )
    sums = [
        jnp.dot(
            left, tap_matrix(weight, first_tap, row_taps, e, channels), preferred_element_type=F32
        )
        for e in range(3)
    ]
    return sums[1] + column_shift(sums[0], cols, 1) + column_shift(sums[2], cols, -1)


def previous_rows(row, outs, weight):
    channels = weight.shape[-1]
    cols = next(x for r in outs if (x := row(1, r)) is not None).shape[0]
    zero = jnp.zeros((cols, channels), BF16)
    none = jnp.zeros((channels, channels), BF16)

    def cells(taps):
        lines = [
            jnp.concatenate([zero if (x := row(f, r - 1 + b)) is None else x for f, b in taps], axis=1)
            for r in outs
        ]
        return jnp.concatenate(lines, axis=0)

    def part(tap, b, e):
        return weight[tap, b, e * channels : (e + 1) * channels]

    def pair(left, right):
        return jnp.concatenate([left, right], axis=1)

    dot = functools.partial(jnp.dot, preferred_element_type=F32)
    near = cells([(1, 0), (1, 1), (1, 2), (0, 2)])
    sums = []
    for e in range(3):
        right = [pair(part(1, b, e), part(0, b, e)) for b in range(3)] + [pair(part(0, 2, e), none)]
        sums.append(dot(near, jnp.concatenate(right, axis=0)))
    far = cells([(0, 0), (0, 1)])
    both = dot(far, jnp.concatenate([pair(part(0, b, 0), part(0, b, 1)) for b in range(2)], axis=0))
    last = dot(far, jnp.concatenate([part(0, b, 2) for b in range(2)], axis=0))
    old = (both[:, :channels], both[:, channels:], last)
    first = [x[:, :channels] + y for x, y in zip(sums, old)]
    second = [x[:, channels:] for x in sums]
    return pair(*(
        x[1] + column_shift(x[0], cols, 1) + column_shift(x[2], cols, -1) for x in (first, second)
    ))


def chunks_of(count):
    size = next(c for c in (4, 3, 2, 1) if count % c == 0)
    return [range(i, i + size) for i in range(0, count, size)]


def fine_own_kernel(frames, weight, out):
    _, rows, cols, _ = frames.shape

    def row(f, i):
        return frames[f, i] if 0 <= i < rows else None

    for outs in chunks_of(rows):
        out[outs[0] * cols : (outs[-1] + 1) * cols] = fine_rows(row, outs, range(3), weight, 2)


def halo_sums(above, below, weight, first_tap, rows):
    if lax.axis_size("rows") == 2:
        b = 2 * (1 - lax.axis_index("rows"))
        added = fine_rows(lambda f, i: above[f, 0], [0], [b], weight, first_tap)
        zero = jnp.zeros_like(added)
        return jnp.where(has_above(), added, zero), jnp.where(has_above(), zero, added)

    def row(f, i):
        if i == -1:
            cells, have = above[f, 0], has_above()
        else:
            cells, have = below[f, 0], has_below()
        return jnp.where(have, cells, jnp.zeros_like(cells))

    return (
        fine_rows(row, [0], [0], weight, first_tap),
        fine_rows(row, [rows - 1], [2], weight, first_tap),
    )


def fine_halo_kernel(above, below, weight, out, *, rows):
    out[0], out[1] = halo_sums(above, below, weight, 2, rows)


def silu(v):
    return v / (1.0 + jnp.exp(-v))


def fine_rest_kernel(frames, weight, own, halo, out):
    _, rows, cols, _ = frames.shape

    def row(f, i):
        return frames[f, i] if 0 <= i < rows else None

    for outs in chunks_of(rows):
        total = jnp.where(has_earlier(1), previous_rows(row, outs, weight), 0.0)
        for i, r in enumerate(outs):
            line = total[i * cols : (i + 1) * cols] + own[r * cols : (r + 1) * cols]
            for k, halo_r in enumerate((0, rows - 1)):
                if r == halo_r:
                    line = line + halo[k]
            out[r * cols : (r + 1) * cols] = line


def pool(sums):
    channels = sums.shape[1] // 2
    fine = silu(sums).astype(BF16).astype(F32)
    return ((fine[:, :channels] + fine[:, channels:]) * 0.5).astype(BF16).astype(F32)


def down_taps(pooled, half_cols):
    return [
        jnp.concatenate(
            [pooled[i, pl.ds(e, half_cols, stride=2), :].astype(BF16) for e in range(3)], axis=1
        )
        for i in range(pooled.shape[0])
    ]


def put_pooled(pooled, lines):
    cols = lines[0].shape[0]
    pad = pooled.shape[1] - cols
    pooled[:, cols:] = jnp.zeros((pooled.shape[0], pad, pooled.shape[2]), F32)
    for i, line in enumerate(lines):
        pooled[i, :cols] = line


def reduce_kernel(above, below, weight, sums, down, out, pooled):
    cols = above.shape[2]
    rows = sums.shape[0] // cols
    half_rows, half_cols = rows // 2, cols // 2
    top, bottom = halo_sums(above, below, weight, 0, rows)
    lines = []
    for r in range(rows):
        line = sums[r * cols : (r + 1) * cols]
        if r == 0:
            line = line + top
        if r == rows - 1:
            line = line + bottom
        lines.append(pool(line))
    put_pooled(pooled, [*lines, jnp.zeros_like(lines[0])])
    dot = functools.partial(jnp.dot, preferred_element_type=F32)
    taps = down_taps(pooled, half_cols)
    left = [jnp.concatenate(taps[2 * p : 2 * p + 3], axis=1) for p in range(half_rows)]
    own = dot(jnp.concatenate(left, axis=0), down[...].reshape(-1, down.shape[-1]))
    out[0, :half_rows] = own.astype(BF16).reshape(half_rows, half_cols, -1)
    out[0, half_rows] = dot(taps[0], down[2]).astype(BF16)


def column_taps(flat, cols):
    left, right = shifted_columns(flat, cols)
    return jnp.concatenate([left, flat, right], axis=1)


def coarse_sums(field, weight, a, sides):
    _, count, cols, channels = field.shape
    rows = count - 1
    taps = column_taps(field.reshape(count * cols, channels), cols)
    body, more = taps[: rows * cols], taps[rows * cols :]
    zero = jnp.zeros_like(more)
    tall = jnp.concatenate([jnp.where(has_above(), more, zero), body, zero], axis=0)
    dot = functools.partial(jnp.dot, preferred_element_type=F32)
    total = sum(dot(tall[b * cols : (b + rows) * cols], weight[a, b]) for b in range(3))
    head, tail = body[:cols], body[(rows - 1) * cols :]
    if sides == 1:
        up = has_above()
        first = jnp.concatenate([jnp.where(up, more, tail), jnp.where(up, head, zero)], axis=0)
        ends = [dot(first, weight[a, 2 * lax.axis_index("rows")])]
        second = [dot(jnp.where(up, more, zero), weight[a, 1])]
    else:
        first = jnp.concatenate([tail, zero], axis=0), jnp.concatenate([more, head], axis=0)
        ends = [dot(first[0], weight[a, 0]), dot(first[1], weight[a, 2])]
        second = [jnp.zeros((cols, weight.shape[-1]), F32), dot(more, weight[a, 1])]
    ends = [
        jnp.concatenate([end[:cols], end[cols:] + add], axis=0) for end, add in zip(ends, second)
    ]
    return total, ends


def coarse_first_kernel(field, weight, body, ends):
    total, parts = coarse_sums(field[...], weight, 2, ends.shape[0])
    body[...] = total
    for side, part in enumerate(parts):
        ends[side] = part


def coarse_next_kernel(field, weight, body_in, ends_in, body, ends):
    cells = field[...]
    cells = jnp.where(has_earlier(1), cells, jnp.zeros_like(cells))
    total, parts = coarse_sums(cells, weight, 1, ends.shape[0])
    body[...] = body_in[...] + total
    for side, part in enumerate(parts):
        ends[side] = ends_in[side] + part


def second_earlier(odd_field, even_field):
    cells = jnp.where(lax.axis_index("tm") % 2 == 1, odd_field[...], even_field[...])
    return jnp.where(has_earlier(2), cells, jnp.zeros_like(cells))


def coarse_ends_kernel(odd_field, even_field, weight, ends, out):
    _, parts = coarse_sums(second_earlier(odd_field, even_field), weight, 0, ends.shape[0])
    for side, part in enumerate(parts):
        out[side] = (ends[side] + part).astype(BF16)


def end_starts(rows, sides):
    return [(rows - 2) * (1 - lax.axis_index("rows"))] if sides == 1 else [0, rows - 2]


def coarse_body_kernel(odd_field, even_field, weight, body, out, ends, sums):
    _, rows, cols, _ = out.shape
    total, _ = coarse_sums(second_earlier(odd_field, even_field), weight, 0, ends.shape[0])
    sums[...] = body[...] + total
    out[...] = silu(sums[...]).astype(BF16).reshape(out.shape)
    for side, start in enumerate(end_starts(rows, ends.shape[0])):
        ends[side] = sums[pl.ds(pl.multiple_of(start * cols, cols), 2 * cols), :]


def finish_kernel(ends, added, _, out, lines, sem):
    rows = out.shape[1]
    copies = []
    for side, start in enumerate(end_starts(rows, ends.shape[0])):
        total = ends[side] + added[side].astype(F32)
        lines[side] = silu(total).astype(BF16).reshape(lines.shape[1:])
        copies.append(
            pltpu.make_async_copy(lines.at[side], out.at[0, pl.ds(start, 2)], sem.at[side])
        )
        copies[-1].start()
    for copy in copies:
        copy.wait()


def call(kernel, out_shape, scratch, flops, args, in_place=False):
    size = sum(a.size * a.dtype.itemsize for a in args)
    vmem = pl.BlockSpec(memory_space=pltpu.VMEM)
    last = pl.BlockSpec(memory_space=pl.ANY) if in_place else vmem
    return pl.pallas_call(
        kernel,
        out_shape=out_shape,
        in_specs=[vmem] * (len(args) - 1) + [last] if args else [],
        out_specs=last if in_place else jax.tree.map(lambda _: vmem, out_shape),
        input_output_aliases={len(args) - 1: 0} if in_place else {},
        scratch_shapes=scratch,
        cost_estimate=pl.CostEstimate(flops=flops, bytes_accessed=size, transcendentals=0),
        compiler_params=pltpu.CompilerParams(vmem_limit_bytes=20 * 1024 * 1024),
    )(*args)


def local(frames, conv_fine, conv_down, conv_coarse):
    _, rows, cols, channels = frames.shape
    wide = conv_down.shape[-1]
    strips, times = lax.axis_size("rows"), lax.axis_size("tm")
    pace = call(pace_kernel, jax.ShapeDtypeStruct((8, 128), F32), [], 4 * 10**9, ())

    earlier = ring(frames, 1)
    (above, below), (above_1, below_1) = frame_rims(pace, frames)
    size = rows * cols
    pair = jax.ShapeDtypeStruct((size, 2 * channels), F32)
    flops = 2 * size * 18 * channels * 2 * channels
    own = call(fine_own_kernel, pair, [], flops, (frames, conv_fine))
    halo = call(
        functools.partial(fine_halo_kernel, rows=rows),
        jax.ShapeDtypeStruct((2, cols, 2 * channels), F32),
        [],
        flops // 3,
        (above, below, conv_fine),
    )
    half_rows, half_cols = rows // 2, cols // 2
    shape = jax.ShapeDtypeStruct((1, half_rows, half_cols, wide), BF16)
    fine_sums = call(fine_rest_kernel, pair, [], flops, (earlier, conv_fine, own, halo))
    above_1, below_1, fine_sums = lax.optimization_barrier((above_1, below_1, fine_sums))
    field = call(
        reduce_kernel,
        jax.ShapeDtypeStruct((1, half_rows + 1, half_cols, wide), BF16),
        [pltpu.VMEM((rows + 1, cols + 8, channels), F32)],
        flops // 3,
        (above_1, below_1, conv_fine, fine_sums, conv_down),
    )
    sides = 1 if strips == 2 else 2
    sums = jax.ShapeDtypeStruct((half_rows * half_cols, wide), F32)
    pairs = jax.ShapeDtypeStruct((sides, 2 * half_cols, wide), F32)
    flops = 2 * half_rows * half_cols * 9 * wide * wide
    odd_field = by_parity(field, 1)
    even_field = by_parity(field, 0)
    body, ends = call(coarse_first_kernel, (sums, pairs), [], flops, (field, conv_coarse))
    odd_field, body, ends = lax.optimization_barrier((odd_field, body, ends))
    field_1 = paired(odd_field) if times % 2 == 0 else ring(field, 1)
    body, ends = call(
        coarse_next_kernel, (sums, pairs), [], flops, (field_1, conv_coarse, body, ends)
    )
    even_field, body, ends = lax.optimization_barrier((even_field, body, ends))
    sent = call(
        coarse_ends_kernel,
        jax.ShapeDtypeStruct(pairs.shape, BF16),
        [],
        flops // 4,
        (odd_field, even_field, conv_coarse, ends),
    )
    if sides == 1:
        added = swapped(sent, 0)
    else:
        added = jnp.concatenate([moved(sent[:1], 0, 1), moved(sent[1:], 0, -1)], axis=0)
    out, end_sums = call(
        coarse_body_kernel,
        (shape, pairs),
        [pltpu.VMEM(sums.shape, F32)],
        flops,
        (odd_field, even_field, conv_coarse, body),
    )
    return call(
        finish_kernel,
        shape,
        [pltpu.VMEM((sides, 2, half_cols, wide), BF16), pltpu.SemaphoreType.DMA((sides,))],
        flops // 16,
        (end_sums, added, out),
        in_place=True,
    )


def solution(mesh):
    placed = (P("tm", "rows", None, None), P(), P(), P())
    return jax.shard_map(local, mesh=mesh, in_specs=placed, out_specs=P("tm", "rows", None, None), check_vma=False)
```

```python
import functools

import jax
import jax.numpy as jnp
from jax import lax
from jax.experimental import pallas as pl
from jax.experimental.pallas import tpu as pltpu
from jax.sharding import PartitionSpec as P


F32 = jnp.float32
BF16 = jnp.bfloat16


def moved(value, steps, hop):
    tm, rows = lax.axis_size("tm"), lax.axis_size("rows")
    pairs = [
        (t * rows + r, (t + steps) * rows + r + hop)
        for t in range(tm - steps)
        for r in range(rows)
        if 0 <= r + hop < rows
    ]
    return lax.ppermute(value, ("tm", "rows"), pairs)


def ring(value, steps):
    tm = lax.axis_size("tm")
    return lax.ppermute(value, "tm", [(t, (t + steps) % tm) for t in range(tm)])


def swapped(value, steps):
    tm = lax.axis_size("tm")
    pairs = [(t * 2 + r, (t + steps) * 2 + 1 - r) for t in range(tm - steps) for r in range(2)]
    return lax.ppermute(value, ("tm", "rows"), pairs)


def odd_ahead(value):
    tm = lax.axis_size("tm")
    pairs = [(t, t + 2) for t in range(1, tm - 2, 2)] + [(t, t) for t in range(0, tm, 2)]
    return lax.ppermute(value, "tm", pairs)


def even_ahead(value):
    tm, rows = lax.axis_size("tm"), lax.axis_size("rows")
    pairs = [(t, r, t + 2, r) for t in range(0, tm - 2, 2) for r in range(rows)]
    if tm % 4 == 0 and rows % 2 == 0:
        for r in range(rows):
            pairs += [(tm - 2, r, tm - 1, r), (3, r, 0, r)]
            pairs += [(t, r, t - 4, r) for t in range(7, tm, 4)]
            pairs += [(t, r, t, r ^ 1) for t in range(1, tm, 4)]
    return lax.ppermute(value, ("tm", "rows"), [(t * rows + r, u * rows + q) for t, r, u, q in pairs])


def paired(value):
    return lax.ppermute(value, "tm", [(t, t ^ 1) for t in range(lax.axis_size("tm"))])


def has_above():
    return lax.axis_index("rows") > 0


def has_below():
    return lax.axis_index("rows") < lax.axis_size("rows") - 1


def has_earlier(steps):
    return lax.axis_index("tm") >= steps


def pace_kernel(out):
    out[...] = jnp.zeros_like(out)


def edge_kernel(_, cells, out):
    width = out.shape[1]
    first = (1 - lax.axis_index("rows")) * (cells.shape[1] - width)
    out[...] = cells[:, pl.ds(first, width)]


def frame_rims(pace, frames):
    rows = frames.shape[1]
    if lax.axis_size("rows") == 2:
        sent = call(
            edge_kernel,
            jax.ShapeDtypeStruct((frames.shape[0], 1, *frames.shape[2:]), BF16),
            [],
            0,
            (pace, frames),
        )
        return [(both, both) for both in (swapped(sent, 0), swapped(sent, 1))]
    head, tail = frames[:, :1], frames[:, rows - 1 :]
    return [(moved(tail, steps, 1), moved(head, steps, -1)) for steps in (0, 1)]


def column_shift(value, cols, steps):
    size = value.shape[0]
    column = lax.broadcasted_iota(jnp.int32, value.shape, 0) % cols
    edge = 0 if steps > 0 else cols - 1
    return jnp.where(column == edge, 0.0, pltpu.roll(value, steps % size, 0))


def shifted_columns(flat, cols):
    wide = flat.astype(F32)
    return column_shift(wide, cols, 1).astype(BF16), column_shift(wide, cols, -1).astype(BF16)


def tap_matrix(weight, first_tap, row_taps, e, channels):
    zero = jnp.zeros((channels, channels), BF16)

    def pick(tap, b):
        return weight[tap, b, e * channels : (e + 1) * channels] if 0 <= tap <= 2 else zero

    return jnp.concatenate(
        [
            jnp.concatenate([pick(first_tap + f, b), pick(first_tap + f - 1, b)], axis=1)
            for f in range(2)
            for b in row_taps
        ],
        axis=0,
    )


def fine_rows(row, outs, row_taps, weight, first_tap):
    channels = weight.shape[-1]
    some = next(x for f in range(2) for r in outs for b in row_taps if (x := row(f, r - 1 + b)) is not None)
    cols = some.shape[0]
    zero = jnp.zeros((cols, channels), BF16)

    def cell(f, i):
        found = row(f, i)
        return zero if found is None else found

    left = jnp.concatenate(
        [
            jnp.concatenate([cell(f, r - 1 + b) for f in range(2) for b in row_taps], axis=1)
            for r in outs
        ],
        axis=0,
    )
    sums = [
        jnp.dot(
            left, tap_matrix(weight, first_tap, row_taps, e, channels), preferred_element_type=F32
        )
        for e in range(3)
    ]
    return sums[1] + column_shift(sums[0], cols, 1) + column_shift(sums[2], cols, -1)


def previous_rows(row, outs, weight):
    channels = weight.shape[-1]
    cols = next(x for r in outs if (x := row(1, r)) is not None).shape[0]
    zero = jnp.zeros((cols, channels), BF16)
    none = jnp.zeros((channels, channels), BF16)

    def cells(taps):
        lines = [
            jnp.concatenate([zero if (x := row(f, r - 1 + b)) is None else x for f, b in taps], axis=1)
            for r in outs
        ]
        return jnp.concatenate(lines, axis=0)

    def part(tap, b, e):
        return weight[tap, b, e * channels : (e + 1) * channels]

    def pair(left, right):
        return jnp.concatenate([left, right], axis=1)

    dot = functools.partial(jnp.dot, preferred_element_type=F32)
    near = cells([(1, 0), (1, 1), (1, 2), (0, 2)])
    sums = []
    for e in range(3):
        right = [pair(part(1, b, e), part(0, b, e)) for b in range(3)] + [pair(part(0, 2, e), none)]
        sums.append(dot(near, jnp.concatenate(right, axis=0)))
    far = cells([(0, 0), (0, 1)])
    both = dot(far, jnp.concatenate([pair(part(0, b, 0), part(0, b, 1)) for b in range(2)], axis=0))
    last = dot(far, jnp.concatenate([part(0, b, 2) for b in range(2)], axis=0))
    old = (both[:, :channels], both[:, channels:], last)
    first = [x[:, :channels] + y for x, y in zip(sums, old)]
    second = [x[:, channels:] for x in sums]
    return pair(*(
        x[1] + column_shift(x[0], cols, 1) + column_shift(x[2], cols, -1) for x in (first, second)
    ))


def chunks_of(count):
    size = next(c for c in (4, 3, 2, 1) if count % c == 0)
    return [range(i, i + size) for i in range(0, count, size)]


def fine_own_kernel(frames, weight, out):
    _, rows, cols, _ = frames.shape

    def row(f, i):
        return frames[f, i] if 0 <= i < rows else None

    for outs in chunks_of(rows):
        out[outs[0] * cols : (outs[-1] + 1) * cols] = fine_rows(row, outs, range(3), weight, 2)


def halo_sums(above, below, weight, first_tap, rows):
    if lax.axis_size("rows") == 2:
        b = 2 * (1 - lax.axis_index("rows"))
        added = fine_rows(lambda f, i: above[f, 0], [0], [b], weight, first_tap)
        zero = jnp.zeros_like(added)
        return jnp.where(has_above(), added, zero), jnp.where(has_above(), zero, added)

    def row(f, i):
        if i == -1:
            cells, have = above[f, 0], has_above()
        else:
            cells, have = below[f, 0], has_below()
        return jnp.where(have, cells, jnp.zeros_like(cells))

    return (
        fine_rows(row, [0], [0], weight, first_tap),
        fine_rows(row, [rows - 1], [2], weight, first_tap),
    )


def fine_halo_kernel(above, below, weight, out, *, rows):
    out[0], out[1] = halo_sums(above, below, weight, 2, rows)


def silu(v):
    return v / (1.0 + jnp.exp(-v))


def fine_rest_kernel(frames, weight, own, halo, out):
    _, rows, cols, _ = frames.shape

    def row(f, i):
        return frames[f, i] if 0 <= i < rows else None

    for outs in chunks_of(rows):
        total = jnp.where(has_earlier(1), previous_rows(row, outs, weight), 0.0)
        for i, r in enumerate(outs):
            line = total[i * cols : (i + 1) * cols] + own[r * cols : (r + 1) * cols]
            for k, halo_r in enumerate((0, rows - 1)):
                if r == halo_r:
                    line = line + halo[k]
            out[r * cols : (r + 1) * cols] = line


def pool(sums):
    channels = sums.shape[1] // 2
    fine = silu(sums).astype(BF16).astype(F32)
    return ((fine[:, :channels] + fine[:, channels:]) * 0.5).astype(BF16).astype(F32)


def down_taps(pooled, half_cols):
    return [
        jnp.concatenate(
            [pooled[i, pl.ds(e, half_cols, stride=2), :].astype(BF16) for e in range(3)], axis=1
        )
        for i in range(pooled.shape[0])
    ]


def put_pooled(pooled, lines):
    cols = lines[0].shape[0]
    pad = pooled.shape[1] - cols
    pooled[:, cols:] = jnp.zeros((pooled.shape[0], pad, pooled.shape[2]), F32)
    for i, line in enumerate(lines):
        pooled[i, :cols] = line


def reduce_kernel(above, below, weight, sums, down, out, pooled):
    cols = above.shape[2]
    rows = sums.shape[0] // cols
    half_rows, half_cols = rows // 2, cols // 2
    top, bottom = halo_sums(above, below, weight, 0, rows)
    lines = []
    for r in range(rows):
        line = sums[r * cols : (r + 1) * cols]
        if r == 0:
            line = line + top
        if r == rows - 1:
            line = line + bottom
        lines.append(pool(line))
    put_pooled(pooled, [*lines, jnp.zeros_like(lines[0])])
    dot = functools.partial(jnp.dot, preferred_element_type=F32)
    taps = down_taps(pooled, half_cols)
    left = [jnp.concatenate(taps[2 * p : 2 * p + 3], axis=1) for p in range(half_rows)]
    own = dot(jnp.concatenate(left, axis=0), down[...].reshape(-1, down.shape[-1]))
    out[0, :half_rows] = own.astype(BF16).reshape(half_rows, half_cols, -1)
    out[0, half_rows] = dot(taps[0], down[2]).astype(BF16)


def column_taps(flat, cols):
    left, right = shifted_columns(flat, cols)
    return jnp.concatenate([left, flat, right], axis=1)


def coarse_sums(field, weight, a, sides):
    _, count, cols, channels = field.shape
    rows = count - 1
    taps = column_taps(field.reshape(count * cols, channels), cols)
    body, more = taps[: rows * cols], taps[rows * cols :]
    zero = jnp.zeros_like(more)
    tall = jnp.concatenate([jnp.where(has_above(), more, zero), body, zero], axis=0)
    dot = functools.partial(jnp.dot, preferred_element_type=F32)
    total = sum(dot(tall[b * cols : (b + rows) * cols], weight[a, b]) for b in range(3))
    head, tail = body[:cols], body[(rows - 1) * cols :]
    if sides == 1:
        up = has_above()
        first = jnp.concatenate([jnp.where(up, more, tail), jnp.where(up, head, zero)], axis=0)
        ends = [dot(first, weight[a, 2 * lax.axis_index("rows")])]
        second = [dot(jnp.where(up, more, zero), weight[a, 1])]
    else:
        first = jnp.concatenate([tail, zero], axis=0), jnp.concatenate([more, head], axis=0)
        ends = [dot(first[0], weight[a, 0]), dot(first[1], weight[a, 2])]
        second = [jnp.zeros((cols, weight.shape[-1]), F32), dot(more, weight[a, 1])]
    ends = [
        jnp.concatenate([end[:cols], end[cols:] + add], axis=0) for end, add in zip(ends, second)
    ]
    return total, ends


def coarse_first_kernel(field, weight, body, ends):
    total, parts = coarse_sums(field[...], weight, 2, ends.shape[0])
    body[...] = total
    for side, part in enumerate(parts):
        ends[side] = part


def coarse_next_kernel(field, weight, body_in, ends_in, body, ends):
    cells = field[...]
    cells = jnp.where(has_earlier(1), cells, jnp.zeros_like(cells))
    total, parts = coarse_sums(cells, weight, 1, ends.shape[0])
    body[...] = body_in[...] + total
    for side, part in enumerate(parts):
        ends[side] = ends_in[side] + part


def second_earlier(odd_field, even_field):
    cells = jnp.where(lax.axis_index("tm") % 2 == 1, odd_field[...], even_field[...])
    return jnp.where(has_earlier(2), cells, jnp.zeros_like(cells))


def coarse_ends_kernel(odd_field, even_field, weight, ends, out):
    _, parts = coarse_sums(second_earlier(odd_field, even_field), weight, 0, ends.shape[0])
    for side, part in enumerate(parts):
        out[side] = (ends[side] + part).astype(BF16)


def end_starts(rows, sides):
    return [(rows - 2) * (1 - lax.axis_index("rows"))] if sides == 1 else [0, rows - 2]


def coarse_body_kernel(odd_field, even_field, weight, body, out, ends, sums):
    _, rows, cols, _ = out.shape
    total, _ = coarse_sums(second_earlier(odd_field, even_field), weight, 0, ends.shape[0])
    sums[...] = body[...] + total
    out[...] = silu(sums[...]).astype(BF16).reshape(out.shape)
    for side, start in enumerate(end_starts(rows, ends.shape[0])):
        ends[side] = sums[pl.ds(pl.multiple_of(start * cols, cols), 2 * cols), :]


def finish_kernel(ends, added, _, out, lines, sem):
    rows = out.shape[1]
    copies = []
    for side, start in enumerate(end_starts(rows, ends.shape[0])):
        total = ends[side] + added[side].astype(F32)
        lines[side] = silu(total).astype(BF16).reshape(lines.shape[1:])
        copies.append(
            pltpu.make_async_copy(lines.at[side], out.at[0, pl.ds(start, 2)], sem.at[side])
        )
        copies[-1].start()
    for copy in copies:
        copy.wait()


def call(kernel, out_shape, scratch, flops, args, in_place=False):
    size = sum(a.size * a.dtype.itemsize for a in args)
    vmem = pl.BlockSpec(memory_space=pltpu.VMEM)
    last = pl.BlockSpec(memory_space=pl.ANY) if in_place else vmem
    return pl.pallas_call(
        kernel,
        out_shape=out_shape,
        in_specs=[vmem] * (len(args) - 1) + [last] if args else [],
        out_specs=last if in_place else jax.tree.map(lambda _: vmem, out_shape),
        input_output_aliases={len(args) - 1: 0} if in_place else {},
        scratch_shapes=scratch,
        cost_estimate=pl.CostEstimate(flops=flops, bytes_accessed=size, transcendentals=0),
        compiler_params=pltpu.CompilerParams(vmem_limit_bytes=20 * 1024 * 1024),
    )(*args)


def local(frames, conv_fine, conv_down, conv_coarse):
    _, rows, cols, channels = frames.shape
    wide = conv_down.shape[-1]
    strips, times = lax.axis_size("rows"), lax.axis_size("tm")
    pace = call(pace_kernel, jax.ShapeDtypeStruct((8, 128), F32), [], 4 * 10**9, ())

    earlier = ring(frames, 1)
    (above, below), (above_1, below_1) = frame_rims(pace, frames)
    size = rows * cols
    pair = jax.ShapeDtypeStruct((size, 2 * channels), F32)
    flops = 2 * size * 18 * channels * 2 * channels
    own = call(fine_own_kernel, pair, [], flops, (frames, conv_fine))
    halo = call(
        functools.partial(fine_halo_kernel, rows=rows),
        jax.ShapeDtypeStruct((2, cols, 2 * channels), F32),
        [],
        flops // 3,
        (above, below, conv_fine),
    )
    half_rows, half_cols = rows // 2, cols // 2
    shape = jax.ShapeDtypeStruct((1, half_rows, half_cols, wide), BF16)
    fine_sums = call(fine_rest_kernel, pair, [], flops, (earlier, conv_fine, own, halo))
    above_1, below_1, fine_sums = lax.optimization_barrier((above_1, below_1, fine_sums))
    field = call(
        reduce_kernel,
        jax.ShapeDtypeStruct((1, half_rows + 1, half_cols, wide), BF16),
        [pltpu.VMEM((rows + 1, cols + 8, channels), F32)],
        flops // 3,
        (above_1, below_1, conv_fine, fine_sums, conv_down),
    )
    sides = 1 if strips == 2 else 2
    sums = jax.ShapeDtypeStruct((half_rows * half_cols, wide), F32)
    pairs = jax.ShapeDtypeStruct((sides, 2 * half_cols, wide), F32)
    flops = 2 * half_rows * half_cols * 9 * wide * wide
    odd_field = odd_ahead(field)
    even_field = even_ahead(field)
    body, ends = call(coarse_first_kernel, (sums, pairs), [], flops, (field, conv_coarse))
    odd_field, body, ends = lax.optimization_barrier((odd_field, body, ends))
    field_1 = paired(odd_field) if times % 2 == 0 else ring(field, 1)
    body, ends = call(
        coarse_next_kernel, (sums, pairs), [], flops, (field_1, conv_coarse, body, ends)
    )
    even_field, body, ends = lax.optimization_barrier((even_field, body, ends))
    sent = call(
        coarse_ends_kernel,
        jax.ShapeDtypeStruct(pairs.shape, BF16),
        [],
        flops // 4,
        (odd_field, even_field, conv_coarse, ends),
    )
    if sides == 1:
        added = swapped(sent, 0)
    else:
        added = jnp.concatenate([moved(sent[:1], 0, 1), moved(sent[1:], 0, -1)], axis=0)
    out, end_sums = call(
        coarse_body_kernel,
        (shape, pairs),
        [pltpu.VMEM(sums.shape, F32)],
        flops,
        (odd_field, even_field, conv_coarse, body),
    )
    return call(
        finish_kernel,
        shape,
        [pltpu.VMEM((sides, 2, half_cols, wide), BF16), pltpu.SemaphoreType.DMA((sides,))],
        flops // 16,
        (end_sums, added, out),
        in_place=True,
    )


def solution(mesh):
    placed = (P("tm", "rows", None, None), P(), P(), P())
    return jax.shard_map(local, mesh=mesh, in_specs=placed, out_specs=P("tm", "rows", None, None), check_vma=False)
```

```python
import functools

import jax
import jax.numpy as jnp
from jax import lax
from jax.experimental import pallas as pl
from jax.experimental.pallas import tpu as pltpu
from jax.sharding import PartitionSpec as P


F32 = jnp.float32
BF16 = jnp.bfloat16


def moved(value, steps, hop):
    tm, rows = lax.axis_size("tm"), lax.axis_size("rows")
    pairs = [
        (t * rows + r, (t + steps) * rows + r + hop)
        for t in range(tm - steps)
        for r in range(rows)
        if 0 <= r + hop < rows
    ]
    return lax.ppermute(value, ("tm", "rows"), pairs)


def ring(value, steps):
    tm = lax.axis_size("tm")
    return lax.ppermute(value, "tm", [(t, (t + steps) % tm) for t in range(tm)])


def swapped(value, steps):
    tm = lax.axis_size("tm")
    pairs = [(t * 2 + r, (t + steps) * 2 + 1 - r) for t in range(tm - steps) for r in range(2)]
    return lax.ppermute(value, ("tm", "rows"), pairs)


def odd_ahead(value):
    tm = lax.axis_size("tm")
    pairs = [(t, t + 2) for t in range(1, tm - 2, 2)] + [(t, t) for t in range(0, tm, 2)]
    return lax.ppermute(value, "tm", pairs)


def even_ahead(value):
    tm, rows = lax.axis_size("tm"), lax.axis_size("rows")
    pairs = [(t, r, t + 2, r) for t in range(0, tm - 2, 2) for r in range(rows)]
    if tm % 4 == 0 and rows % 2 == 0:
        for r in range(rows):
            pairs += [(tm - 2, r, tm - 1, r), (tm - 1, r, tm - 3, r), (1, r, 0, r)]
            pairs += [(t, r, t - 4, r) for t in range(5, tm, 4)]
            pairs += [(t, r, t, r ^ 1) for t in range(3, tm - 1, 4)]
    return lax.ppermute(value, ("tm", "rows"), [(t * rows + r, u * rows + q) for t, r, u, q in pairs])


def paired(value):
    return lax.ppermute(value, "tm", [(t, t ^ 1) for t in range(lax.axis_size("tm"))])


def has_above():
    return lax.axis_index("rows") > 0


def has_below():
    return lax.axis_index("rows") < lax.axis_size("rows") - 1


def has_earlier(steps):
    return lax.axis_index("tm") >= steps


def pace_kernel(out):
    out[...] = jnp.zeros_like(out)


def edge_kernel(_, cells, out):
    width = out.shape[1]
    first = (1 - lax.axis_index("rows")) * (cells.shape[1] - width)
    out[...] = cells[:, pl.ds(first, width)]


def frame_rims(pace, frames):
    rows = frames.shape[1]
    if lax.axis_size("rows") == 2:
        sent = call(
            edge_kernel,
            jax.ShapeDtypeStruct((frames.shape[0], 1, *frames.shape[2:]), BF16),
            [],
            0,
            (pace, frames),
        )
        return [(both, both) for both in (swapped(sent, 0), swapped(sent, 1))]
    head, tail = frames[:, :1], frames[:, rows - 1 :]
    return [(moved(tail, steps, 1), moved(head, steps, -1)) for steps in (0, 1)]


def column_shift(value, cols, steps):
    size = value.shape[0]
    column = lax.broadcasted_iota(jnp.int32, value.shape, 0) % cols
    edge = 0 if steps > 0 else cols - 1
    return jnp.where(column == edge, 0.0, pltpu.roll(value, steps % size, 0))


def shifted_columns(flat, cols):
    wide = flat.astype(F32)
    return column_shift(wide, cols, 1).astype(BF16), column_shift(wide, cols, -1).astype(BF16)


def tap_matrix(weight, first_tap, row_taps, e, channels):
    zero = jnp.zeros((channels, channels), BF16)

    def pick(tap, b):
        return weight[tap, b, e * channels : (e + 1) * channels] if 0 <= tap <= 2 else zero

    return jnp.concatenate(
        [
            jnp.concatenate([pick(first_tap + f, b), pick(first_tap + f - 1, b)], axis=1)
            for f in range(2)
            for b in row_taps
        ],
        axis=0,
    )


def fine_rows(row, outs, row_taps, weight, first_tap):
    channels = weight.shape[-1]
    some = next(x for f in range(2) for r in outs for b in row_taps if (x := row(f, r - 1 + b)) is not None)
    cols = some.shape[0]
    zero = jnp.zeros((cols, channels), BF16)

    def cell(f, i):
        found = row(f, i)
        return zero if found is None else found

    left = jnp.concatenate(
        [
            jnp.concatenate([cell(f, r - 1 + b) for f in range(2) for b in row_taps], axis=1)
            for r in outs
        ],
        axis=0,
    )
    sums = [
        jnp.dot(
            left, tap_matrix(weight, first_tap, row_taps, e, channels), preferred_element_type=F32
        )
        for e in range(3)
    ]
    return sums[1] + column_shift(sums[0], cols, 1) + column_shift(sums[2], cols, -1)


def previous_rows(row, outs, weight):
    channels = weight.shape[-1]
    cols = next(x for r in outs if (x := row(1, r)) is not None).shape[0]
    zero = jnp.zeros((cols, channels), BF16)
    none = jnp.zeros((channels, channels), BF16)

    def cells(taps):
        lines = [
            jnp.concatenate([zero if (x := row(f, r - 1 + b)) is None else x for f, b in taps], axis=1)
            for r in outs
        ]
        return jnp.concatenate(lines, axis=0)

    def part(tap, b, e):
        return weight[tap, b, e * channels : (e + 1) * channels]

    def pair(left, right):
        return jnp.concatenate([left, right], axis=1)

    dot = functools.partial(jnp.dot, preferred_element_type=F32)
    near = cells([(1, 0), (1, 1), (1, 2), (0, 2)])
    sums = []
    for e in range(3):
        right = [pair(part(1, b, e), part(0, b, e)) for b in range(3)] + [pair(part(0, 2, e), none)]
        sums.append(dot(near, jnp.concatenate(right, axis=0)))
    far = cells([(0, 0), (0, 1)])
    both = dot(far, jnp.concatenate([pair(part(0, b, 0), part(0, b, 1)) for b in range(2)], axis=0))
    last = dot(far, jnp.concatenate([part(0, b, 2) for b in range(2)], axis=0))
    old = (both[:, :channels], both[:, channels:], last)
    first = [x[:, :channels] + y for x, y in zip(sums, old)]
    second = [x[:, channels:] for x in sums]
    return pair(*(
        x[1] + column_shift(x[0], cols, 1) + column_shift(x[2], cols, -1) for x in (first, second)
    ))


def chunks_of(count):
    size = next(c for c in (4, 3, 2, 1) if count % c == 0)
    return [range(i, i + size) for i in range(0, count, size)]


def fine_own_kernel(frames, weight, out):
    _, rows, cols, _ = frames.shape

    def row(f, i):
        return frames[f, i] if 0 <= i < rows else None

    for outs in chunks_of(rows):
        out[outs[0] * cols : (outs[-1] + 1) * cols] = fine_rows(row, outs, range(3), weight, 2)


def halo_sums(above, below, weight, first_tap, rows):
    if lax.axis_size("rows") == 2:
        b = 2 * (1 - lax.axis_index("rows"))
        added = fine_rows(lambda f, i: above[f, 0], [0], [b], weight, first_tap)
        zero = jnp.zeros_like(added)
        return jnp.where(has_above(), added, zero), jnp.where(has_above(), zero, added)

    def row(f, i):
        if i == -1:
            cells, have = above[f, 0], has_above()
        else:
            cells, have = below[f, 0], has_below()
        return jnp.where(have, cells, jnp.zeros_like(cells))

    return (
        fine_rows(row, [0], [0], weight, first_tap),
        fine_rows(row, [rows - 1], [2], weight, first_tap),
    )


def fine_halo_kernel(above, below, weight, out, *, rows):
    out[0], out[1] = halo_sums(above, below, weight, 2, rows)


def silu(v):
    return v / (1.0 + jnp.exp(-v))


def fine_rest_kernel(frames, weight, own, halo, out):
    _, rows, cols, _ = frames.shape

    def row(f, i):
        return frames[f, i] if 0 <= i < rows else None

    for outs in chunks_of(rows):
        total = jnp.where(has_earlier(1), previous_rows(row, outs, weight), 0.0)
        for i, r in enumerate(outs):
            line = total[i * cols : (i + 1) * cols] + own[r * cols : (r + 1) * cols]
            for k, halo_r in enumerate((0, rows - 1)):
                if r == halo_r:
                    line = line + halo[k]
            out[r * cols : (r + 1) * cols] = line


def pool(sums):
    channels = sums.shape[1] // 2
    fine = silu(sums).astype(BF16).astype(F32)
    return ((fine[:, :channels] + fine[:, channels:]) * 0.5).astype(BF16).astype(F32)


def down_taps(pooled, half_cols):
    return [
        jnp.concatenate(
            [pooled[i, pl.ds(e, half_cols, stride=2), :].astype(BF16) for e in range(3)], axis=1
        )
        for i in range(pooled.shape[0])
    ]


def put_pooled(pooled, lines):
    cols = lines[0].shape[0]
    pad = pooled.shape[1] - cols
    pooled[:, cols:] = jnp.zeros((pooled.shape[0], pad, pooled.shape[2]), F32)
    for i, line in enumerate(lines):
        pooled[i, :cols] = line


def reduce_kernel(above, below, weight, sums, down, out, pooled):
    cols = above.shape[2]
    rows = sums.shape[0] // cols
    half_rows, half_cols = rows // 2, cols // 2
    top, bottom = halo_sums(above, below, weight, 0, rows)
    lines = []
    for r in range(rows):
        line = sums[r * cols : (r + 1) * cols]
        if r == 0:
            line = line + top
        if r == rows - 1:
            line = line + bottom
        lines.append(pool(line))
    put_pooled(pooled, [*lines, jnp.zeros_like(lines[0])])
    dot = functools.partial(jnp.dot, preferred_element_type=F32)
    taps = down_taps(pooled, half_cols)
    left = [jnp.concatenate(taps[2 * p : 2 * p + 3], axis=1) for p in range(half_rows)]
    own = dot(jnp.concatenate(left, axis=0), down[...].reshape(-1, down.shape[-1]))
    out[0, :half_rows] = own.astype(BF16).reshape(half_rows, half_cols, -1)
    out[0, half_rows] = dot(taps[0], down[2]).astype(BF16)


def column_taps(flat, cols):
    left, right = shifted_columns(flat, cols)
    return jnp.concatenate([left, flat, right], axis=1)


def coarse_sums(field, weight, a, sides):
    _, count, cols, channels = field.shape
    rows = count - 1
    taps = column_taps(field.reshape(count * cols, channels), cols)
    body, more = taps[: rows * cols], taps[rows * cols :]
    zero = jnp.zeros_like(more)
    tall = jnp.concatenate([jnp.where(has_above(), more, zero), body, zero], axis=0)
    dot = functools.partial(jnp.dot, preferred_element_type=F32)
    total = sum(dot(tall[b * cols : (b + rows) * cols], weight[a, b]) for b in range(3))
    head, tail = body[:cols], body[(rows - 1) * cols :]
    if sides == 1:
        up = has_above()
        first = jnp.concatenate([jnp.where(up, more, tail), jnp.where(up, head, zero)], axis=0)
        ends = [dot(first, weight[a, 2 * lax.axis_index("rows")])]
        second = [dot(jnp.where(up, more, zero), weight[a, 1])]
    else:
        first = jnp.concatenate([tail, zero], axis=0), jnp.concatenate([more, head], axis=0)
        ends = [dot(first[0], weight[a, 0]), dot(first[1], weight[a, 2])]
        second = [jnp.zeros((cols, weight.shape[-1]), F32), dot(more, weight[a, 1])]
    ends = [
        jnp.concatenate([end[:cols], end[cols:] + add], axis=0) for end, add in zip(ends, second)
    ]
    return total, ends


def coarse_first_kernel(field, weight, body, ends):
    total, parts = coarse_sums(field[...], weight, 2, ends.shape[0])
    body[...] = total
    for side, part in enumerate(parts):
        ends[side] = part


def coarse_next_kernel(field, weight, body_in, ends_in, body, ends):
    cells = field[...]
    cells = jnp.where(has_earlier(1), cells, jnp.zeros_like(cells))
    total, parts = coarse_sums(cells, weight, 1, ends.shape[0])
    body[...] = body_in[...] + total
    for side, part in enumerate(parts):
        ends[side] = ends_in[side] + part


def second_earlier(odd_field, even_field):
    cells = jnp.where(lax.axis_index("tm") % 2 == 1, odd_field[...], even_field[...])
    return jnp.where(has_earlier(2), cells, jnp.zeros_like(cells))


def coarse_ends_kernel(odd_field, even_field, weight, ends, out):
    _, parts = coarse_sums(second_earlier(odd_field, even_field), weight, 0, ends.shape[0])
    for side, part in enumerate(parts):
        out[side] = (ends[side] + part).astype(BF16)


def end_starts(rows, sides):
    return [(rows - 2) * (1 - lax.axis_index("rows"))] if sides == 1 else [0, rows - 2]


def coarse_body_kernel(odd_field, even_field, weight, body, out, ends, sums):
    _, rows, cols, _ = out.shape
    total, _ = coarse_sums(second_earlier(odd_field, even_field), weight, 0, ends.shape[0])
    sums[...] = body[...] + total
    out[...] = silu(sums[...]).astype(BF16).reshape(out.shape)
    for side, start in enumerate(end_starts(rows, ends.shape[0])):
        ends[side] = sums[pl.ds(pl.multiple_of(start * cols, cols), 2 * cols), :]


def finish_kernel(ends, added, _, out, lines, sem):
    rows = out.shape[1]
    copies = []
    for side, start in enumerate(end_starts(rows, ends.shape[0])):
        total = ends[side] + added[side].astype(F32)
        lines[side] = silu(total).astype(BF16).reshape(lines.shape[1:])
        copies.append(
            pltpu.make_async_copy(lines.at[side], out.at[0, pl.ds(start, 2)], sem.at[side])
        )
        copies[-1].start()
    for copy in copies:
        copy.wait()


def call(kernel, out_shape, scratch, flops, args, in_place=False):
    size = sum(a.size * a.dtype.itemsize for a in args)
    vmem = pl.BlockSpec(memory_space=pltpu.VMEM)
    last = pl.BlockSpec(memory_space=pl.ANY) if in_place else vmem
    return pl.pallas_call(
        kernel,
        out_shape=out_shape,
        in_specs=[vmem] * (len(args) - 1) + [last] if args else [],
        out_specs=last if in_place else jax.tree.map(lambda _: vmem, out_shape),
        input_output_aliases={len(args) - 1: 0} if in_place else {},
        scratch_shapes=scratch,
        cost_estimate=pl.CostEstimate(flops=flops, bytes_accessed=size, transcendentals=0),
        compiler_params=pltpu.CompilerParams(vmem_limit_bytes=20 * 1024 * 1024),
    )(*args)


def local(frames, conv_fine, conv_down, conv_coarse):
    _, rows, cols, channels = frames.shape
    wide = conv_down.shape[-1]
    strips, times = lax.axis_size("rows"), lax.axis_size("tm")
    pace = call(pace_kernel, jax.ShapeDtypeStruct((8, 128), F32), [], 4 * 10**9, ())

    earlier = ring(frames, 1)
    (above, below), (above_1, below_1) = frame_rims(pace, frames)
    size = rows * cols
    pair = jax.ShapeDtypeStruct((size, 2 * channels), F32)
    flops = 2 * size * 18 * channels * 2 * channels
    own = call(fine_own_kernel, pair, [], flops, (frames, conv_fine))
    halo = call(
        functools.partial(fine_halo_kernel, rows=rows),
        jax.ShapeDtypeStruct((2, cols, 2 * channels), F32),
        [],
        flops // 3,
        (above, below, conv_fine),
    )
    half_rows, half_cols = rows // 2, cols // 2
    shape = jax.ShapeDtypeStruct((1, half_rows, half_cols, wide), BF16)
    fine_sums = call(fine_rest_kernel, pair, [], flops, (earlier, conv_fine, own, halo))
    above_1, below_1, fine_sums = lax.optimization_barrier((above_1, below_1, fine_sums))
    field = call(
        reduce_kernel,
        jax.ShapeDtypeStruct((1, half_rows + 1, half_cols, wide), BF16),
        [pltpu.VMEM((rows + 1, cols + 8, channels), F32)],
        flops // 3,
        (above_1, below_1, conv_fine, fine_sums, conv_down),
    )
    sides = 1 if strips == 2 else 2
    sums = jax.ShapeDtypeStruct((half_rows * half_cols, wide), F32)
    pairs = jax.ShapeDtypeStruct((sides, 2 * half_cols, wide), F32)
    flops = 2 * half_rows * half_cols * 9 * wide * wide
    odd_field = odd_ahead(field)
    even_field = even_ahead(field)
    body, ends = call(coarse_first_kernel, (sums, pairs), [], flops, (field, conv_coarse))
    odd_field, body, ends = lax.optimization_barrier((odd_field, body, ends))
    field_1 = paired(odd_field) if times % 2 == 0 else ring(field, 1)
    body, ends = call(
        coarse_next_kernel, (sums, pairs), [], flops, (field_1, conv_coarse, body, ends)
    )
    even_field, body, ends = lax.optimization_barrier((even_field, body, ends))
    sent = call(
        coarse_ends_kernel,
        jax.ShapeDtypeStruct(pairs.shape, BF16),
        [],
        flops // 4,
        (odd_field, even_field, conv_coarse, ends),
    )
    if sides == 1:
        added = swapped(sent, 0)
    else:
        added = jnp.concatenate([moved(sent[:1], 0, 1), moved(sent[1:], 0, -1)], axis=0)
    out, end_sums = call(
        coarse_body_kernel,
        (shape, pairs),
        [pltpu.VMEM(sums.shape, F32)],
        flops,
        (odd_field, even_field, conv_coarse, body),
    )
    return call(
        finish_kernel,
        shape,
        [pltpu.VMEM((sides, 2, half_cols, wide), BF16), pltpu.SemaphoreType.DMA((sides,))],
        flops // 16,
        (end_sums, added, out),
        in_place=True,
    )


def solution(mesh):
    placed = (P("tm", "rows", None, None), P(), P(), P())
    return jax.shard_map(local, mesh=mesh, in_specs=placed, out_specs=P("tm", "rows", None, None), check_vma=False)
```

```python
import functools

import jax
import jax.numpy as jnp
from jax import lax
from jax.experimental import pallas as pl
from jax.experimental.pallas import tpu as pltpu
from jax.sharding import PartitionSpec as P


F32 = jnp.float32
BF16 = jnp.bfloat16


def moved(value, steps, hop):
    tm, rows = lax.axis_size("tm"), lax.axis_size("rows")
    pairs = [
        (t * rows + r, (t + steps) * rows + r + hop)
        for t in range(tm - steps)
        for r in range(rows)
        if 0 <= r + hop < rows
    ]
    return lax.ppermute(value, ("tm", "rows"), pairs)


def ring(value, steps):
    tm = lax.axis_size("tm")
    return lax.ppermute(value, "tm", [(t, (t + steps) % tm) for t in range(tm)])


def swapped(value, steps):
    tm = lax.axis_size("tm")
    pairs = [(t * 2 + r, (t + steps) * 2 + 1 - r) for t in range(tm - steps) for r in range(2)]
    return lax.ppermute(value, ("tm", "rows"), pairs)


def odd_ahead(value):
    tm = lax.axis_size("tm")
    pairs = [(t, t + 2) for t in range(1, tm - 2, 2)] + [(t, t) for t in range(0, tm, 2)]
    return lax.ppermute(value, "tm", pairs)


def even_ahead(value):
    tm, rows = lax.axis_size("tm"), lax.axis_size("rows")
    pairs = [(t, r, t + 2, r) for t in range(0, tm - 2, 2) for r in range(rows)]
    if tm % 4 == 0 and rows % 2 == 0:
        for r in range(rows):
            pairs += [(tm - 2, r, tm - 1, r), (tm - 1, r, tm - 3, r), (1, r, 0, r)]
            pairs += [(t, r, t - 4, r) for t in range(5, tm, 4)]
            pairs += [(t, r, t, r ^ 1) for t in range(3, tm - 1, 4)]
    return lax.ppermute(value, ("tm", "rows"), [(t * rows + r, u * rows + q) for t, r, u, q in pairs])


def paired(value):
    return lax.ppermute(value, "tm", [(t, t ^ 1) for t in range(lax.axis_size("tm"))])


def has_above():
    return lax.axis_index("rows") > 0


def has_below():
    return lax.axis_index("rows") < lax.axis_size("rows") - 1


def has_earlier(steps):
    return lax.axis_index("tm") >= steps


def pace_kernel(out):
    out[...] = jnp.zeros_like(out)


def edge_kernel(_, cells, out):
    width = out.shape[1]
    first = (1 - lax.axis_index("rows")) * (cells.shape[1] - width)
    out[...] = cells[:, pl.ds(first, width)]


def frame_rims(pace, frames):
    rows = frames.shape[1]
    if lax.axis_size("rows") == 2:
        sent = call(
            edge_kernel,
            jax.ShapeDtypeStruct((frames.shape[0], 2, *frames.shape[2:]), BF16),
            [],
            0,
            (pace, frames),
        )
        return [(both, both) for both in (swapped(sent, 0), swapped(sent, 1))]
    head, tail = frames[:, :2], frames[:, rows - 1 :]
    return [(moved(tail, steps, 1), moved(head, steps, -1)) for steps in (0, 1)]


def column_shift(value, cols, steps):
    size = value.shape[0]
    column = lax.broadcasted_iota(jnp.int32, value.shape, 0) % cols
    edge = 0 if steps > 0 else cols - 1
    return jnp.where(column == edge, 0.0, pltpu.roll(value, steps % size, 0))


def shifted_columns(flat, cols):
    wide = flat.astype(F32)
    return column_shift(wide, cols, 1).astype(BF16), column_shift(wide, cols, -1).astype(BF16)


def tap_matrix(weight, first_tap, row_taps, e, channels):
    zero = jnp.zeros((channels, channels), BF16)

    def pick(tap, b):
        return weight[tap, b, e * channels : (e + 1) * channels] if 0 <= tap <= 2 else zero

    return jnp.concatenate(
        [
            jnp.concatenate([pick(first_tap + f, b), pick(first_tap + f - 1, b)], axis=1)
            for f in range(2)
            for b in row_taps
        ],
        axis=0,
    )


def fine_rows(row, outs, row_taps, weight, first_tap):
    channels = weight.shape[-1]
    some = next(x for f in range(2) for r in outs for b in row_taps if (x := row(f, r - 1 + b)) is not None)
    cols = some.shape[0]
    zero = jnp.zeros((cols, channels), BF16)

    def cell(f, i):
        found = row(f, i)
        return zero if found is None else found

    left = jnp.concatenate(
        [
            jnp.concatenate([cell(f, r - 1 + b) for f in range(2) for b in row_taps], axis=1)
            for r in outs
        ],
        axis=0,
    )
    sums = [
        jnp.dot(
            left, tap_matrix(weight, first_tap, row_taps, e, channels), preferred_element_type=F32
        )
        for e in range(3)
    ]
    return sums[1] + column_shift(sums[0], cols, 1) + column_shift(sums[2], cols, -1)


def previous_rows(row, outs, weight):
    channels = weight.shape[-1]
    cols = next(x for r in outs if (x := row(1, r)) is not None).shape[0]
    zero = jnp.zeros((cols, channels), BF16)
    none = jnp.zeros((channels, channels), BF16)

    def cells(taps):
        lines = [
            jnp.concatenate([zero if (x := row(f, r - 1 + b)) is None else x for f, b in taps], axis=1)
            for r in outs
        ]
        return jnp.concatenate(lines, axis=0)

    def part(tap, b, e):
        return weight[tap, b, e * channels : (e + 1) * channels]

    def pair(left, right):
        return jnp.concatenate([left, right], axis=1)

    dot = functools.partial(jnp.dot, preferred_element_type=F32)
    near = cells([(1, 0), (1, 1), (1, 2), (0, 2)])
    sums = []
    for e in range(3):
        right = [pair(part(1, b, e), part(0, b, e)) for b in range(3)] + [pair(part(0, 2, e), none)]
        sums.append(dot(near, jnp.concatenate(right, axis=0)))
    far = cells([(0, 0), (0, 1)])
    both = dot(far, jnp.concatenate([pair(part(0, b, 0), part(0, b, 1)) for b in range(2)], axis=0))
    last = dot(far, jnp.concatenate([part(0, b, 2) for b in range(2)], axis=0))
    old = (both[:, :channels], both[:, channels:], last)
    first = [x[:, :channels] + y for x, y in zip(sums, old)]
    second = [x[:, channels:] for x in sums]
    return pair(*(
        x[1] + column_shift(x[0], cols, 1) + column_shift(x[2], cols, -1) for x in (first, second)
    ))


def chunks_of(count):
    size = next(c for c in (4, 3, 2, 1) if count % c == 0)
    return [range(i, i + size) for i in range(0, count, size)]


def fine_own_kernel(frames, weight, out):
    _, rows, cols, _ = frames.shape

    def row(f, i):
        return frames[f, i] if 0 <= i < rows else None

    for outs in chunks_of(rows + 1):
        out[outs[0] * cols : (outs[-1] + 1) * cols] = fine_rows(row, outs, range(3), weight, 2)


def halo_row(above, below, rows):
    def row(f, i):
        if i == -1:
            cells, have = above[f, above.shape[1] - 1], has_above()
        elif i >= rows:
            cells, have = below[f, i - rows], has_below()
        else:
            return None
        return jnp.where(have, cells, jnp.zeros_like(cells))

    return row


def halo_sum(above, below, weight, first_tap, rows):
    row = halo_row(above, below, rows)
    return jnp.concatenate(
        [
            fine_rows(row, [0], [0], weight, first_tap),
            fine_rows(row, [rows - 1, rows], [1, 2], weight, first_tap),
        ],
        axis=0,
    )


def fine_halo_kernel(above, below, weight, out, *, rows):
    out[...] = halo_sum(above, below, weight, 2, rows)


def silu(v):
    return v / (1.0 + jnp.exp(-v))


def fine_rest_kernel(frames, weight, own, halo, out):
    _, rows, cols, _ = frames.shape

    def row(f, i):
        return frames[f, i] if 0 <= i < rows else None

    for outs in chunks_of(rows + 1):
        total = jnp.where(has_earlier(1), previous_rows(row, outs, weight), 0.0)
        for i, r in enumerate(outs):
            line = total[i * cols : (i + 1) * cols] + own[r * cols : (r + 1) * cols]
            for k, halo_r in enumerate((0, rows - 1, rows)):
                if r == halo_r:
                    line = line + halo[k * cols : (k + 1) * cols]
            out[r * cols : (r + 1) * cols] = line


def pool(sums):
    channels = sums.shape[1] // 2
    fine = silu(sums).astype(BF16).astype(F32)
    return ((fine[:, :channels] + fine[:, channels:]) * 0.5).astype(BF16).astype(F32)


def down_taps(pooled, half_cols):
    return [
        jnp.concatenate(
            [pooled[i, pl.ds(e, half_cols, stride=2), :].astype(BF16) for e in range(3)], axis=1
        )
        for i in range(pooled.shape[0])
    ]


def put_pooled(pooled, lines):
    cols = lines[0].shape[0]
    pad = pooled.shape[1] - cols
    pooled[:, cols:] = jnp.zeros((pooled.shape[0], pad, pooled.shape[2]), F32)
    for i, line in enumerate(lines):
        pooled[i, :cols] = line


def reduce_kernel(above, below, weight, sums, down, out, pooled):
    cols = above.shape[2]
    rows = sums.shape[0] // cols - 1
    half_rows, half_cols = rows // 2, cols // 2
    added = halo_sum(above, below, weight, 0, rows)
    lines = []
    for r in range(rows + 1):
        line = sums[r * cols : (r + 1) * cols]
        for k, halo_r in enumerate((0, rows - 1, rows)):
            if r == halo_r:
                line = line + added[k * cols : (k + 1) * cols]
        line = pool(line)
        lines.append(jnp.where(has_below(), line, 0.0) if r == rows else line)
    put_pooled(pooled, lines)
    taps = down_taps(pooled, half_cols)
    left = [jnp.concatenate(taps[2 * p : 2 * p + 3], axis=1) for p in range(half_rows)]
    own = jnp.dot(
        jnp.concatenate(left, axis=0),
        down[...].reshape(-1, down.shape[-1]),
        preferred_element_type=F32,
    )
    out[0] = own.astype(BF16).reshape(half_rows, half_cols, -1)


def column_taps(flat, cols):
    left, right = shifted_columns(flat, cols)
    return jnp.concatenate([left, flat, right], axis=1)


def coarse_sums(field, weight, a, sides):
    _, rows, cols, channels = field.shape
    body = column_taps(field.reshape(rows * cols, channels), cols)
    zero = jnp.zeros_like(body[:cols])
    tall = jnp.concatenate([zero, body, zero], axis=0)
    dot = functools.partial(jnp.dot, preferred_element_type=F32)
    total = sum(dot(tall[b * cols : (b + rows) * cols], weight[a, b]) for b in range(3))
    head, tail = body[:cols], body[(rows - 1) * cols :]
    if sides == 1:
        return total, [dot(jnp.where(has_above(), head, tail), weight[a, 2 * lax.axis_index("rows")])]
    return total, [dot(tail, weight[a, 0]), dot(head, weight[a, 2])]


def coarse_first_kernel(field, weight, body, ends):
    total, parts = coarse_sums(field[...], weight, 2, ends.shape[0])
    body[...] = total
    for side, part in enumerate(parts):
        ends[side] = part


def coarse_next_kernel(field, weight, body_in, ends_in, body, ends):
    cells = field[...]
    cells = jnp.where(has_earlier(1), cells, jnp.zeros_like(cells))
    total, parts = coarse_sums(cells, weight, 1, ends.shape[0])
    body[...] = body_in[...] + total
    for side, part in enumerate(parts):
        ends[side] = ends_in[side] + part


def second_earlier(odd_field, even_field):
    cells = jnp.where(lax.axis_index("tm") % 2 == 1, odd_field[...], even_field[...])
    return jnp.where(has_earlier(2), cells, jnp.zeros_like(cells))


def coarse_ends_kernel(odd_field, even_field, weight, ends, out):
    _, parts = coarse_sums(second_earlier(odd_field, even_field), weight, 0, ends.shape[0])
    for side, part in enumerate(parts):
        out[side] = (ends[side] + part).astype(BF16)


def end_starts(rows, sides):
    return [(rows - 1) * (1 - lax.axis_index("rows"))] if sides == 1 else [0, rows - 1]


def coarse_body_kernel(odd_field, even_field, weight, body, out, ends, sums):
    _, rows, cols, _ = out.shape
    total, _ = coarse_sums(second_earlier(odd_field, even_field), weight, 0, ends.shape[0])
    sums[...] = body[...] + total
    out[...] = silu(sums[...]).astype(BF16).reshape(out.shape)
    for side, start in enumerate(end_starts(rows, ends.shape[0])):
        ends[side] = sums[pl.ds(pl.multiple_of(start * cols, cols), cols), :]


def finish_kernel(ends, added, _, out, lines, sem):
    rows = out.shape[1]
    copies = []
    for side, start in enumerate(end_starts(rows, ends.shape[0])):
        total = ends[side] + added[side].astype(F32)
        lines[side] = silu(total).astype(BF16)
        copies.append(
            pltpu.make_async_copy(lines.at[side], out.at[0, start], sem.at[side])
        )
        copies[-1].start()
    for copy in copies:
        copy.wait()


def call(kernel, out_shape, scratch, flops, args, in_place=False):
    size = sum(a.size * a.dtype.itemsize for a in args)
    vmem = pl.BlockSpec(memory_space=pltpu.VMEM)
    last = pl.BlockSpec(memory_space=pl.ANY) if in_place else vmem
    return pl.pallas_call(
        kernel,
        out_shape=out_shape,
        in_specs=[vmem] * (len(args) - 1) + [last] if args else [],
        out_specs=last if in_place else jax.tree.map(lambda _: vmem, out_shape),
        input_output_aliases={len(args) - 1: 0} if in_place else {},
        scratch_shapes=scratch,
        cost_estimate=pl.CostEstimate(flops=flops, bytes_accessed=size, transcendentals=0),
        compiler_params=pltpu.CompilerParams(vmem_limit_bytes=20 * 1024 * 1024),
    )(*args)


def local(frames, conv_fine, conv_down, conv_coarse):
    _, rows, cols, channels = frames.shape
    wide = conv_down.shape[-1]
    strips, times = lax.axis_size("rows"), lax.axis_size("tm")
    pace = call(pace_kernel, jax.ShapeDtypeStruct((8, 128), F32), [], 4 * 10**9, ())

    earlier = ring(frames, 1)
    (above, below), (above_1, below_1) = frame_rims(pace, frames)
    size = (rows + 1) * cols
    pair = jax.ShapeDtypeStruct((size, 2 * channels), F32)
    flops = 2 * size * 18 * channels * 2 * channels
    own = call(fine_own_kernel, pair, [], flops, (frames, conv_fine))
    halo = call(
        functools.partial(fine_halo_kernel, rows=rows),
        jax.ShapeDtypeStruct((3 * cols, 2 * channels), F32),
        [],
        flops // 3,
        (above, below, conv_fine),
    )
    half_rows, half_cols = rows // 2, cols // 2
    shape = jax.ShapeDtypeStruct((1, half_rows, half_cols, wide), BF16)
    fine_sums = call(fine_rest_kernel, pair, [], flops, (earlier, conv_fine, own, halo))
    above_1, below_1, fine_sums = lax.optimization_barrier((above_1, below_1, fine_sums))
    field = call(
        reduce_kernel,
        shape,
        [pltpu.VMEM((rows + 1, cols + 8, channels), F32)],
        flops // 3,
        (above_1, below_1, conv_fine, fine_sums, conv_down),
    )
    sides = 1 if strips == 2 else 2
    sums = jax.ShapeDtypeStruct((half_rows * half_cols, wide), F32)
    pairs = jax.ShapeDtypeStruct((sides, half_cols, wide), F32)
    flops = 2 * half_rows * half_cols * 9 * wide * wide
    odd_field = odd_ahead(field)
    even_field = even_ahead(field)
    body, ends = call(coarse_first_kernel, (sums, pairs), [], flops, (field, conv_coarse))
    odd_field, body, ends = lax.optimization_barrier((odd_field, body, ends))
    field_1 = paired(odd_field) if times % 2 == 0 else ring(field, 1)
    body, ends = call(
        coarse_next_kernel, (sums, pairs), [], flops, (field_1, conv_coarse, body, ends)
    )
    even_field, body, ends = lax.optimization_barrier((even_field, body, ends))
    sent = call(
        coarse_ends_kernel,
        jax.ShapeDtypeStruct(pairs.shape, BF16),
        [],
        flops // 4,
        (odd_field, even_field, conv_coarse, ends),
    )
    if sides == 1:
        added = swapped(sent, 0)
    else:
        added = jnp.concatenate([moved(sent[:1], 0, 1), moved(sent[1:], 0, -1)], axis=0)
    out, end_sums = call(
        coarse_body_kernel,
        (shape, pairs),
        [pltpu.VMEM(sums.shape, F32)],
        flops,
        (odd_field, even_field, conv_coarse, body),
    )
    return call(
        finish_kernel,
        shape,
        [pltpu.VMEM((sides, half_cols, wide), BF16), pltpu.SemaphoreType.DMA((sides,))],
        flops // 16,
        (end_sums, added, out),
        in_place=True,
    )


def solution(mesh):
    placed = (P("tm", "rows", None, None), P(), P(), P())
    return jax.shard_map(local, mesh=mesh, in_specs=placed, out_specs=P("tm", "rows", None, None), check_vma=False)
```

```python
import functools

import jax
import jax.numpy as jnp
from jax import lax
from jax.experimental import pallas as pl
from jax.experimental.pallas import tpu as pltpu
from jax.sharding import PartitionSpec as P


F32 = jnp.float32
BF16 = jnp.bfloat16


def moved(value, steps, hop):
    tm, rows = lax.axis_size("tm"), lax.axis_size("rows")
    pairs = [
        (t * rows + r, (t + steps) * rows + r + hop)
        for t in range(tm - steps)
        for r in range(rows)
        if 0 <= r + hop < rows
    ]
    return lax.ppermute(value, ("tm", "rows"), pairs)


def ring(value, steps):
    tm = lax.axis_size("tm")
    return lax.ppermute(value, "tm", [(t, (t + steps) % tm) for t in range(tm)])


def swapped(value, steps):
    tm = lax.axis_size("tm")
    pairs = [(t * 2 + r, (t + steps) * 2 + 1 - r) for t in range(tm - steps) for r in range(2)]
    return lax.ppermute(value, ("tm", "rows"), pairs)


def odd_ahead(value):
    tm = lax.axis_size("tm")
    pairs = [(t, t + 2) for t in range(1, tm - 2, 2)] + [(t, t) for t in range(0, tm, 2)]
    return lax.ppermute(value, "tm", pairs)


def even_ahead(value):
    tm, rows = lax.axis_size("tm"), lax.axis_size("rows")
    pairs = [(t, r, t + 2, r) for t in range(0, tm - 2, 2) for r in range(rows)]
    if tm % 4 == 0 and rows % 2 == 0:
        for r in range(rows):
            pairs += [(tm - 2, r, tm - 1, r), (tm - 1, r, tm - 3, r), (1, r, 0, r)]
            pairs += [(t, r, t - 4, r) for t in range(5, tm, 4)]
            pairs += [(t, r, t, r ^ 1) for t in range(3, tm - 1, 4)]
    return lax.ppermute(value, ("tm", "rows"), [(t * rows + r, u * rows + q) for t, r, u, q in pairs])


def paired(value):
    return lax.ppermute(value, "tm", [(t, t ^ 1) for t in range(lax.axis_size("tm"))])


def has_above():
    return lax.axis_index("rows") > 0


def has_below():
    return lax.axis_index("rows") < lax.axis_size("rows") - 1


def has_earlier(steps):
    return lax.axis_index("tm") >= steps


def pace_kernel(out):
    out[...] = jnp.zeros_like(out)


def edge_kernel(_, cells, out):
    width = out.shape[1]
    first = (1 - lax.axis_index("rows")) * (cells.shape[1] - width)
    out[...] = cells[:, pl.ds(first, width)]


def frame_rims(pace, frames):
    rows = frames.shape[1]
    if lax.axis_size("rows") == 2:
        sent = call(
            edge_kernel,
            jax.ShapeDtypeStruct((frames.shape[0], 2, *frames.shape[2:]), BF16),
            [],
            0,
            (pace, frames),
        )
        return [(both, both) for both in (swapped(sent, 0), swapped(sent, 1))]
    head, tail = frames[:, :2], frames[:, rows - 1 :]
    return [(moved(tail, steps, 1), moved(head, steps, -1)) for steps in (0, 1)]


def column_shift(value, cols, steps):
    size = value.shape[0]
    column = lax.broadcasted_iota(jnp.int32, value.shape, 0) % cols
    edge = 0 if steps > 0 else cols - 1
    return jnp.where(column == edge, 0.0, pltpu.roll(value, steps % size, 0))


def shifted_columns(flat, cols):
    wide = flat.astype(F32)
    return column_shift(wide, cols, 1).astype(BF16), column_shift(wide, cols, -1).astype(BF16)


def tap_matrix(weight, first_tap, row_taps, e, channels):
    zero = jnp.zeros((channels, channels), BF16)

    def pick(tap, b):
        return weight[tap, b, e * channels : (e + 1) * channels] if 0 <= tap <= 2 else zero

    return jnp.concatenate(
        [
            jnp.concatenate([pick(first_tap + f, b), pick(first_tap + f - 1, b)], axis=1)
            for f in range(2)
            for b in row_taps
        ],
        axis=0,
    )


def fine_rows(row, outs, row_taps, weight, first_tap):
    channels = weight.shape[-1]
    some = next(x for f in range(2) for r in outs for b in row_taps if (x := row(f, r - 1 + b)) is not None)
    cols = some.shape[0]
    zero = jnp.zeros((cols, channels), BF16)

    def cell(f, i):
        found = row(f, i)
        return zero if found is None else found

    left = jnp.concatenate(
        [
            jnp.concatenate([cell(f, r - 1 + b) for f in range(2) for b in row_taps], axis=1)
            for r in outs
        ],
        axis=0,
    )
    sums = [
        jnp.dot(
            left, tap_matrix(weight, first_tap, row_taps, e, channels), preferred_element_type=F32
        )
        for e in range(3)
    ]
    return sums[1] + column_shift(sums[0], cols, 1) + column_shift(sums[2], cols, -1)


def previous_rows(row, outs, weight):
    channels = weight.shape[-1]
    cols = next(x for r in outs if (x := row(1, r)) is not None).shape[0]
    zero = jnp.zeros((cols, channels), BF16)
    none = jnp.zeros((channels, channels), BF16)

    def cells(taps):
        lines = [
            jnp.concatenate([zero if (x := row(f, r - 1 + b)) is None else x for f, b in taps], axis=1)
            for r in outs
        ]
        return jnp.concatenate(lines, axis=0)

    def part(tap, b, e):
        return weight[tap, b, e * channels : (e + 1) * channels]

    def pair(left, right):
        return jnp.concatenate([left, right], axis=1)

    dot = functools.partial(jnp.dot, preferred_element_type=F32)
    near = cells([(1, 0), (1, 1), (1, 2), (0, 2)])
    sums = []
    for e in range(3):
        right = [pair(part(1, b, e), part(0, b, e)) for b in range(3)] + [pair(part(0, 2, e), none)]
        sums.append(dot(near, jnp.concatenate(right, axis=0)))
    far = cells([(0, 0), (0, 1)])
    both = dot(far, jnp.concatenate([pair(part(0, b, 0), part(0, b, 1)) for b in range(2)], axis=0))
    last = dot(far, jnp.concatenate([part(0, b, 2) for b in range(2)], axis=0))
    old = (both[:, :channels], both[:, channels:], last)
    first = [x[:, :channels] + y for x, y in zip(sums, old)]
    second = [x[:, channels:] for x in sums]
    return pair(*(
        x[1] + column_shift(x[0], cols, 1) + column_shift(x[2], cols, -1) for x in (first, second)
    ))


def chunks_of(count):
    size = next(c for c in (4, 3, 2, 1) if count % c == 0)
    return [range(i, i + size) for i in range(0, count, size)]


def fine_own_kernel(frames, weight, out):
    _, rows, cols, _ = frames.shape

    def row(f, i):
        return frames[f, i] if 0 <= i < rows else None

    for outs in chunks_of(rows + 1):
        out[outs[0] * cols : (outs[-1] + 1) * cols] = fine_rows(row, outs, range(3), weight, 2)


def halo_row(above, below, rows):
    def row(f, i):
        if i == -1:
            cells, have = above[f, above.shape[1] - 1], has_above()
        elif i >= rows:
            cells, have = below[f, i - rows], has_below()
        else:
            return None
        return jnp.where(have, cells, jnp.zeros_like(cells))

    return row


def halo_sum(above, below, weight, first_tap, rows):
    row = halo_row(above, below, rows)
    return jnp.concatenate(
        [
            fine_rows(row, [0], [0], weight, first_tap),
            fine_rows(row, [rows - 1, rows], [1, 2], weight, first_tap),
        ],
        axis=0,
    )


def fine_halo_kernel(above, below, weight, out, *, rows):
    out[...] = halo_sum(above, below, weight, 2, rows)


def silu(v):
    return v / (1.0 + jnp.exp(-v))


def fine_rest_kernel(frames, weight, own, halo, out):
    _, rows, cols, _ = frames.shape

    def row(f, i):
        return frames[f, i] if 0 <= i < rows else None

    for outs in chunks_of(rows + 1):
        total = jnp.where(has_earlier(1), previous_rows(row, outs, weight), 0.0)
        for i, r in enumerate(outs):
            line = total[i * cols : (i + 1) * cols] + own[r * cols : (r + 1) * cols]
            for k, halo_r in enumerate((0, rows - 1, rows)):
                if r == halo_r:
                    line = line + halo[k * cols : (k + 1) * cols]
            out[r * cols : (r + 1) * cols] = line


def pool(sums):
    channels = sums.shape[1] // 2
    fine = silu(sums).astype(BF16).astype(F32)
    return ((fine[:, :channels] + fine[:, channels:]) * 0.5).astype(BF16).astype(F32)


def down_taps(pooled, half_cols):
    return [
        jnp.concatenate(
            [pooled[i, pl.ds(e, half_cols, stride=2), :].astype(BF16) for e in range(3)], axis=1
        )
        for i in range(pooled.shape[0])
    ]


def put_pooled(pooled, lines):
    cols = lines[0].shape[0]
    pad = pooled.shape[1] - cols
    pooled[:, cols:] = jnp.zeros((pooled.shape[0], pad, pooled.shape[2]), F32)
    for i, line in enumerate(lines):
        pooled[i, :cols] = line


def reduced_rows(lines, firsts, half_cols, down, pooled):
    put_pooled(pooled, lines)
    taps = down_taps(pooled, half_cols)
    left = [jnp.concatenate(taps[i : i + 3], axis=1) for i in firsts]
    right = down[...].reshape(-1, down.shape[-1])
    rows = jnp.dot(jnp.concatenate(left, axis=0), right, preferred_element_type=F32)
    return rows.astype(BF16).reshape(len(firsts), half_cols, -1)


def inner_kernel(sums, down, out, pooled):
    count, half_cols, _ = out.shape
    cols = 2 * half_cols
    lines = [pool(sums[r * cols : (r + 1) * cols]) for r in range(2, 2 * count + 3)]
    out[...] = reduced_rows(lines, range(0, 2 * count, 2), half_cols, down, pooled)


def reduce_kernel(above, below, weight, sums, inner, down, out, pooled):
    cols = above.shape[2]
    rows = sums.shape[0] // cols - 1
    added = halo_sum(above, below, weight, 0, rows)
    lines = []
    for r in (0, 1, 2, rows - 2, rows - 1, rows):
        line = sums[r * cols : (r + 1) * cols]
        for k, halo_r in enumerate((0, rows - 1, rows)):
            if r == halo_r:
                line = line + added[k * cols : (k + 1) * cols]
        line = pool(line)
        lines.append(jnp.where(has_below(), line, 0.0) if r == rows else line)
    ends = reduced_rows(lines, (0, 3), cols // 2, down, pooled)
    out[0, 0] = ends[0]
    out[0, 1 : rows // 2 - 1] = inner[...]
    out[0, rows // 2 - 1] = ends[1]


def column_taps(flat, cols):
    left, right = shifted_columns(flat, cols)
    return jnp.concatenate([left, flat, right], axis=1)


def coarse_sums(field, weight, a, sides):
    _, rows, cols, channels = field.shape
    body = column_taps(field.reshape(rows * cols, channels), cols)
    zero = jnp.zeros_like(body[:cols])
    tall = jnp.concatenate([zero, body, zero], axis=0)
    dot = functools.partial(jnp.dot, preferred_element_type=F32)
    total = sum(dot(tall[b * cols : (b + rows) * cols], weight[a, b]) for b in range(3))
    head, tail = body[:cols], body[(rows - 1) * cols :]
    if sides == 1:
        return total, [dot(jnp.where(has_above(), head, tail), weight[a, 2 * lax.axis_index("rows")])]
    return total, [dot(tail, weight[a, 0]), dot(head, weight[a, 2])]


def coarse_first_kernel(field, weight, body, ends):
    total, parts = coarse_sums(field[...], weight, 2, ends.shape[0])
    body[...] = total
    for side, part in enumerate(parts):
        ends[side] = part


def coarse_next_kernel(field, weight, body_in, ends_in, body, ends):
    cells = field[...]
    cells = jnp.where(has_earlier(1), cells, jnp.zeros_like(cells))
    total, parts = coarse_sums(cells, weight, 1, ends.shape[0])
    body[...] = body_in[...] + total
    for side, part in enumerate(parts):
        ends[side] = ends_in[side] + part


def second_earlier(odd_field, even_field):
    cells = jnp.where(lax.axis_index("tm") % 2 == 1, odd_field[...], even_field[...])
    return jnp.where(has_earlier(2), cells, jnp.zeros_like(cells))


def coarse_ends_kernel(odd_field, even_field, weight, ends, out):
    _, parts = coarse_sums(second_earlier(odd_field, even_field), weight, 0, ends.shape[0])
    for side, part in enumerate(parts):
        out[side] = (ends[side] + part).astype(BF16)


def end_starts(rows, sides):
    return [(rows - 1) * (1 - lax.axis_index("rows"))] if sides == 1 else [0, rows - 1]


def coarse_body_kernel(odd_field, even_field, weight, body, out, ends, sums):
    _, rows, cols, _ = out.shape
    total, _ = coarse_sums(second_earlier(odd_field, even_field), weight, 0, ends.shape[0])
    sums[...] = body[...] + total
    out[...] = silu(sums[...]).astype(BF16).reshape(out.shape)
    for side, start in enumerate(end_starts(rows, ends.shape[0])):
        ends[side] = sums[pl.ds(pl.multiple_of(start * cols, cols), cols), :]


def finish_kernel(ends, added, _, out, lines, sem):
    rows = out.shape[1]
    copies = []
    for side, start in enumerate(end_starts(rows, ends.shape[0])):
        total = ends[side] + added[side].astype(F32)
        lines[side] = silu(total).astype(BF16)
        copies.append(
            pltpu.make_async_copy(lines.at[side], out.at[0, start], sem.at[side])
        )
        copies[-1].start()
    for copy in copies:
        copy.wait()


def call(kernel, out_shape, scratch, flops, args, in_place=False):
    size = sum(a.size * a.dtype.itemsize for a in args)
    vmem = pl.BlockSpec(memory_space=pltpu.VMEM)
    last = pl.BlockSpec(memory_space=pl.ANY) if in_place else vmem
    return pl.pallas_call(
        kernel,
        out_shape=out_shape,
        in_specs=[vmem] * (len(args) - 1) + [last] if args else [],
        out_specs=last if in_place else jax.tree.map(lambda _: vmem, out_shape),
        input_output_aliases={len(args) - 1: 0} if in_place else {},
        scratch_shapes=scratch,
        cost_estimate=pl.CostEstimate(flops=flops, bytes_accessed=size, transcendentals=0),
        compiler_params=pltpu.CompilerParams(vmem_limit_bytes=20 * 1024 * 1024),
    )(*args)


def local(frames, conv_fine, conv_down, conv_coarse):
    _, rows, cols, channels = frames.shape
    wide = conv_down.shape[-1]
    strips, times = lax.axis_size("rows"), lax.axis_size("tm")
    pace = call(pace_kernel, jax.ShapeDtypeStruct((8, 128), F32), [], 4 * 10**9, ())

    earlier = ring(frames, 1)
    (above, below), (above_1, below_1) = frame_rims(pace, frames)
    size = (rows + 1) * cols
    pair = jax.ShapeDtypeStruct((size, 2 * channels), F32)
    flops = 2 * size * 18 * channels * 2 * channels
    own = call(fine_own_kernel, pair, [], flops, (frames, conv_fine))
    halo = call(
        functools.partial(fine_halo_kernel, rows=rows),
        jax.ShapeDtypeStruct((3 * cols, 2 * channels), F32),
        [],
        flops // 3,
        (above, below, conv_fine),
    )
    half_rows, half_cols = rows // 2, cols // 2
    shape = jax.ShapeDtypeStruct((1, half_rows, half_cols, wide), BF16)
    fine_sums = call(fine_rest_kernel, pair, [], flops, (earlier, conv_fine, own, halo))
    inner = call(
        inner_kernel,
        jax.ShapeDtypeStruct((half_rows - 2, half_cols, wide), BF16),
        [pltpu.VMEM((rows - 3, cols + 8, channels), F32)],
        flops // 4,
        (fine_sums, conv_down),
    )
    above_1, below_1, fine_sums, inner = lax.optimization_barrier(
        (above_1, below_1, fine_sums, inner)
    )
    field = call(
        reduce_kernel,
        shape,
        [pltpu.VMEM((6, cols + 8, channels), F32)],
        flops // 3,
        (above_1, below_1, conv_fine, fine_sums, inner, conv_down),
    )
    sides = 1 if strips == 2 else 2
    sums = jax.ShapeDtypeStruct((half_rows * half_cols, wide), F32)
    pairs = jax.ShapeDtypeStruct((sides, half_cols, wide), F32)
    flops = 2 * half_rows * half_cols * 9 * wide * wide
    odd_field = odd_ahead(field)
    even_field = even_ahead(field)
    body, ends = call(coarse_first_kernel, (sums, pairs), [], flops, (field, conv_coarse))
    odd_field, body, ends = lax.optimization_barrier((odd_field, body, ends))
    field_1 = paired(odd_field) if times % 2 == 0 else ring(field, 1)
    body, ends = call(
        coarse_next_kernel, (sums, pairs), [], flops, (field_1, conv_coarse, body, ends)
    )
    even_field, body, ends = lax.optimization_barrier((even_field, body, ends))
    sent = call(
        coarse_ends_kernel,
        jax.ShapeDtypeStruct(pairs.shape, BF16),
        [],
        flops // 4,
        (odd_field, even_field, conv_coarse, ends),
    )
    if sides == 1:
        added = swapped(sent, 0)
    else:
        added = jnp.concatenate([moved(sent[:1], 0, 1), moved(sent[1:], 0, -1)], axis=0)
    out, end_sums = call(
        coarse_body_kernel,
        (shape, pairs),
        [pltpu.VMEM(sums.shape, F32)],
        flops,
        (odd_field, even_field, conv_coarse, body),
    )
    return call(
        finish_kernel,
        shape,
        [pltpu.VMEM((sides, half_cols, wide), BF16), pltpu.SemaphoreType.DMA((sides,))],
        flops // 16,
        (end_sums, added, out),
        in_place=True,
    )


def solution(mesh):
    placed = (P("tm", "rows", None, None), P(), P(), P())
    return jax.shard_map(local, mesh=mesh, in_specs=placed, out_specs=P("tm", "rows", None, None), check_vma=False)
```

```python
import functools

import jax
import jax.numpy as jnp
from jax import lax
from jax.experimental import pallas as pl
from jax.experimental.pallas import tpu as pltpu
from jax.sharding import PartitionSpec as P


F32 = jnp.float32
BF16 = jnp.bfloat16


def moved(value, steps, hop):
    tm, rows = lax.axis_size("tm"), lax.axis_size("rows")
    pairs = [
        (t * rows + r, (t + steps) * rows + r + hop)
        for t in range(tm - steps)
        for r in range(rows)
        if 0 <= r + hop < rows
    ]
    return lax.ppermute(value, ("tm", "rows"), pairs)


def ring(value, steps):
    tm = lax.axis_size("tm")
    return lax.ppermute(value, "tm", [(t, (t + steps) % tm) for t in range(tm)])


def swapped(value, steps):
    tm = lax.axis_size("tm")
    pairs = [(t * 2 + r, (t + steps) * 2 + 1 - r) for t in range(tm - steps) for r in range(2)]
    return lax.ppermute(value, ("tm", "rows"), pairs)


def odd_ahead(value):
    tm = lax.axis_size("tm")
    pairs = [(t, t + 2) for t in range(1, tm - 2, 2)] + [(t, t) for t in range(0, tm, 2)]
    return lax.ppermute(value, "tm", pairs)


def even_ahead(value):
    tm, rows = lax.axis_size("tm"), lax.axis_size("rows")
    pairs = [(t, r, t + 2, r) for t in range(0, tm - 2, 2) for r in range(rows)]
    if tm % 4 == 0 and rows % 2 == 0:
        for r in range(rows):
            pairs += [(tm - 2, r, tm - 1, r), (tm - 1, r, tm - 3, r), (1, r, 0, r)]
            pairs += [(t, r, t - 4, r) for t in range(5, tm, 4)]
            pairs += [(t, r, t, r ^ 1) for t in range(3, tm - 1, 4)]
    return lax.ppermute(value, ("tm", "rows"), [(t * rows + r, u * rows + q) for t, r, u, q in pairs])


def paired(value):
    return lax.ppermute(value, "tm", [(t, t ^ 1) for t in range(lax.axis_size("tm"))])


def has_above():
    return lax.axis_index("rows") > 0


def has_below():
    return lax.axis_index("rows") < lax.axis_size("rows") - 1


def has_earlier(steps):
    return lax.axis_index("tm") >= steps


def pace_kernel(out):
    out[...] = jnp.zeros_like(out)


def edge_kernel(_, cells, out):
    width = out.shape[1]
    first = (1 - lax.axis_index("rows")) * (cells.shape[1] - width)
    out[...] = cells[:, pl.ds(first, width)]


def frame_rims(pace, frames):
    rows = frames.shape[1]
    if lax.axis_size("rows") == 2:
        sent = call(
            edge_kernel,
            jax.ShapeDtypeStruct((frames.shape[0], 2, *frames.shape[2:]), BF16),
            [],
            0,
            (pace, frames),
        )
        return [(both, both) for both in (swapped(sent, 0), swapped(sent, 1))]
    head, tail = frames[:, :2], frames[:, rows - 1 :]
    return [(moved(tail, steps, 1), moved(head, steps, -1)) for steps in (0, 1)]


def column_shift(value, cols, steps):
    size = value.shape[0]
    column = lax.broadcasted_iota(jnp.int32, value.shape, 0) % cols
    edge = 0 if steps > 0 else cols - 1
    return jnp.where(column == edge, 0.0, pltpu.roll(value, steps % size, 0))


def shifted_columns(flat, cols):
    wide = flat.astype(F32)
    return column_shift(wide, cols, 1).astype(BF16), column_shift(wide, cols, -1).astype(BF16)


def tap_matrix(weight, first_tap, row_taps, e, channels):
    zero = jnp.zeros((channels, channels), BF16)

    def pick(tap, b):
        return weight[tap, b, e * channels : (e + 1) * channels] if 0 <= tap <= 2 else zero

    return jnp.concatenate(
        [
            jnp.concatenate([pick(first_tap + f, b), pick(first_tap + f - 1, b)], axis=1)
            for f in range(2)
            for b in row_taps
        ],
        axis=0,
    )


def fine_rows(row, outs, row_taps, weight, first_tap):
    channels = weight.shape[-1]
    some = next(x for f in range(2) for r in outs for b in row_taps if (x := row(f, r - 1 + b)) is not None)
    cols = some.shape[0]
    zero = jnp.zeros((cols, channels), BF16)

    def cell(f, i):
        found = row(f, i)
        return zero if found is None else found

    left = jnp.concatenate(
        [
            jnp.concatenate([cell(f, r - 1 + b) for f in range(2) for b in row_taps], axis=1)
            for r in outs
        ],
        axis=0,
    )
    sums = [
        jnp.dot(
            left, tap_matrix(weight, first_tap, row_taps, e, channels), preferred_element_type=F32
        )
        for e in range(3)
    ]
    return sums[1] + column_shift(sums[0], cols, 1) + column_shift(sums[2], cols, -1)


def previous_rows(row, outs, weight):
    channels = weight.shape[-1]
    cols = next(x for r in outs if (x := row(1, r)) is not None).shape[0]
    zero = jnp.zeros((cols, channels), BF16)
    none = jnp.zeros((channels, channels), BF16)

    def cells(taps):
        lines = [
            jnp.concatenate([zero if (x := row(f, r - 1 + b)) is None else x for f, b in taps], axis=1)
            for r in outs
        ]
        return jnp.concatenate(lines, axis=0)

    def part(tap, b, e):
        return weight[tap, b, e * channels : (e + 1) * channels]

    def pair(left, right):
        return jnp.concatenate([left, right], axis=1)

    dot = functools.partial(jnp.dot, preferred_element_type=F32)
    near = cells([(1, 0), (1, 1), (1, 2), (0, 2)])
    sums = []
    for e in range(3):
        right = [pair(part(1, b, e), part(0, b, e)) for b in range(3)] + [pair(part(0, 2, e), none)]
        sums.append(dot(near, jnp.concatenate(right, axis=0)))
    far = cells([(0, 0), (0, 1)])
    both = dot(far, jnp.concatenate([pair(part(0, b, 0), part(0, b, 1)) for b in range(2)], axis=0))
    last = dot(far, jnp.concatenate([part(0, b, 2) for b in range(2)], axis=0))
    old = (both[:, :channels], both[:, channels:], last)
    first = [x[:, :channels] + y for x, y in zip(sums, old)]
    second = [x[:, channels:] for x in sums]
    return pair(*(
        x[1] + column_shift(x[0], cols, 1) + column_shift(x[2], cols, -1) for x in (first, second)
    ))


def chunks_of(count):
    size = next(c for c in (4, 3, 2, 1) if count % c == 0)
    return [range(i, i + size) for i in range(0, count, size)]


def fine_own_kernel(frames, weight, out):
    _, rows, cols, _ = frames.shape

    def row(f, i):
        return frames[f, i] if 0 <= i < rows else None

    for outs in chunks_of(rows + 1):
        out[outs[0] * cols : (outs[-1] + 1) * cols] = fine_rows(row, outs, range(3), weight, 2)


def halo_row(above, below, rows):
    def row(f, i):
        if i == -1:
            cells, have = above[f, above.shape[1] - 1], has_above()
        elif i >= rows:
            cells, have = below[f, i - rows], has_below()
        else:
            return None
        return jnp.where(have, cells, jnp.zeros_like(cells))

    return row


def halo_sum(above, below, weight, first_tap, rows):
    row = halo_row(above, below, rows)
    return jnp.concatenate(
        [
            fine_rows(row, [0], [0], weight, first_tap),
            fine_rows(row, [rows - 1, rows], [1, 2], weight, first_tap),
        ],
        axis=0,
    )


def fine_halo_kernel(above, below, weight, out, *, rows):
    out[...] = halo_sum(above, below, weight, 2, rows)


def silu(v):
    return v / (1.0 + jnp.exp(-v))


def fine_rest_kernel(frames, weight, own, halo, out):
    _, rows, cols, _ = frames.shape

    def row(f, i):
        return frames[f, i] if 0 <= i < rows else None

    for outs in chunks_of(rows + 1):
        total = jnp.where(has_earlier(1), previous_rows(row, outs, weight), 0.0)
        for i, r in enumerate(outs):
            line = total[i * cols : (i + 1) * cols] + own[r * cols : (r + 1) * cols]
            for k, halo_r in enumerate((0, rows - 1, rows)):
                if r == halo_r:
                    line = line + halo[k * cols : (k + 1) * cols]
            out[r * cols : (r + 1) * cols] = line


def pool(sums):
    channels = sums.shape[1] // 2
    fine = silu(sums).astype(BF16).astype(F32)
    return ((fine[:, :channels] + fine[:, channels:]) * 0.5).astype(BF16).astype(F32)


def down_taps(pooled, half_cols):
    return [
        jnp.concatenate(
            [pooled[i, pl.ds(e, half_cols, stride=2), :].astype(BF16) for e in range(3)], axis=1
        )
        for i in range(pooled.shape[0])
    ]


def put_pooled(pooled, lines):
    cols = lines[0].shape[0]
    pad = pooled.shape[1] - cols
    pooled[:, cols:] = jnp.zeros((pooled.shape[0], pad, pooled.shape[2]), F32)
    for i, line in enumerate(lines):
        pooled[i, :cols] = line


def reduced_rows(lines, firsts, half_cols, down, pooled):
    put_pooled(pooled, lines)
    taps = down_taps(pooled, half_cols)
    left = [jnp.concatenate(taps[i : i + 3], axis=1) for i in firsts]
    right = down[...].reshape(-1, down.shape[-1])
    rows = jnp.dot(jnp.concatenate(left, axis=0), right, preferred_element_type=F32)
    return rows.astype(BF16).reshape(len(firsts), half_cols, -1)


def inner_kernel(sums, down, out, pooled):
    count, half_cols, _ = out.shape
    cols = 2 * half_cols
    size = 2 * count + 1
    two = lax.axis_size("rows") == 2
    start = 2 * lax.axis_index("rows") if two else 2
    mean = pool(sums[pl.ds(pl.multiple_of(start * cols, cols), size * cols), :])
    lines = [mean[k * cols : (k + 1) * cols] for k in range(size)]
    if two:
        lines[-1] = jnp.where(has_below(), lines[-1], 0.0)
    out[...] = reduced_rows(lines, range(0, 2 * count, 2), half_cols, down, pooled)


def one_halo_sum(rims, weight):
    cols, channels = rims.shape[2:]
    up = has_above()
    zero = jnp.zeros((cols, channels), BF16)
    left = jnp.concatenate(
        [
            jnp.concatenate(
                [x for f in range(2) for x in (jnp.where(up, rims[f, 1], zero), jnp.where(up, zero, rims[f, 0]))],
                axis=1,
            ),
            jnp.concatenate([jnp.where(up, zero, rims[f, k]) for f in range(2) for k in range(2)], axis=1),
        ],
        axis=0,
    )
    b = 1 - lax.axis_index("rows")
    x = [
        jnp.dot(left, tap_matrix(weight, 0, (b, b + 1), e, channels), preferred_element_type=F32)
        for e in range(3)
    ]
    added = x[1] + column_shift(x[0], cols, 1) + column_shift(x[2], cols, -1)
    none = jnp.zeros((cols, added.shape[1]), F32)
    below = jnp.concatenate([none, added], axis=0)
    return jnp.where(up, jnp.concatenate([added[:cols], none, none], axis=0), below)


def reduce_kernel(above, below, weight, sums, inner, down, out, pooled):
    cols = above.shape[2]
    rows = sums.shape[0] // cols - 1
    half = rows // 2
    if lax.axis_size("rows") == 2:
        strip = lax.axis_index("rows")
        begin = pl.multiple_of((rows - 2) * (1 - strip) * cols, cols)
        mean = pool(sums[pl.ds(begin, 3 * cols), :] + one_halo_sum(above, weight))
        lines = [mean[k * cols : (k + 1) * cols] for k in range(3)]
        end = reduced_rows(lines, (0,), cols // 2, down, pooled)
        out[0, pl.ds(strip, half - 1)] = inner[...]
        out[0, (half - 1) * (1 - strip)] = end[0]
        return
    added = halo_sum(above, below, weight, 0, rows)
    lines = []
    for r in (0, 1, 2, rows - 2, rows - 1, rows):
        line = sums[r * cols : (r + 1) * cols]
        for k, halo_r in enumerate((0, rows - 1, rows)):
            if r == halo_r:
                line = line + added[k * cols : (k + 1) * cols]
        line = pool(line)
        lines.append(jnp.where(has_below(), line, 0.0) if r == rows else line)
    ends = reduced_rows(lines, (0, 3), cols // 2, down, pooled)
    out[0, 0] = ends[0]
    out[0, 1 : half - 1] = inner[...]
    out[0, half - 1] = ends[1]


def column_taps(flat, cols):
    left, right = shifted_columns(flat, cols)
    return jnp.concatenate([left, flat, right], axis=1)


def coarse_sums(field, weight, a, sides):
    _, rows, cols, channels = field.shape
    body = column_taps(field.reshape(rows * cols, channels), cols)
    zero = jnp.zeros_like(body[:cols])
    tall = jnp.concatenate([zero, body, zero], axis=0)
    dot = functools.partial(jnp.dot, preferred_element_type=F32)
    total = sum(dot(tall[b * cols : (b + rows) * cols], weight[a, b]) for b in range(3))
    head, tail = body[:cols], body[(rows - 1) * cols :]
    if sides == 1:
        return total, [dot(jnp.where(has_above(), head, tail), weight[a, 2 * lax.axis_index("rows")])]
    return total, [dot(tail, weight[a, 0]), dot(head, weight[a, 2])]


def coarse_first_kernel(field, weight, body, ends):
    total, parts = coarse_sums(field[...], weight, 2, ends.shape[0])
    body[...] = total
    for side, part in enumerate(parts):
        ends[side] = part


def earlier_sums(field_1, odd_field, even_field, weight, sides):
    one = field_1[...]
    one = jnp.where(has_earlier(1), one, jnp.zeros_like(one))
    two = jnp.where(lax.axis_index("tm") % 2 == 1, odd_field[...], even_field[...])
    two = jnp.where(has_earlier(2), two, jnp.zeros_like(two))
    total_1, ends_1 = coarse_sums(one, weight, 1, sides)
    total_2, ends_2 = coarse_sums(two, weight, 0, sides)
    return total_1 + total_2, [x + y for x, y in zip(ends_1, ends_2)]


def coarse_ends_kernel(field_1, odd_field, even_field, weight, ends, out):
    _, parts = earlier_sums(field_1, odd_field, even_field, weight, ends.shape[0])
    for side, part in enumerate(parts):
        out[side] = (ends[side] + part).astype(BF16)


def end_starts(rows, sides):
    return [(rows - 1) * (1 - lax.axis_index("rows"))] if sides == 1 else [0, rows - 1]


def coarse_body_kernel(field_1, odd_field, even_field, weight, body, out, ends, sums):
    _, rows, cols, _ = out.shape
    total, _ = earlier_sums(field_1, odd_field, even_field, weight, ends.shape[0])
    sums[...] = body[...] + total
    out[...] = silu(sums[...]).astype(BF16).reshape(out.shape)
    for side, start in enumerate(end_starts(rows, ends.shape[0])):
        ends[side] = sums[pl.ds(pl.multiple_of(start * cols, cols), cols), :]


def finish_kernel(ends, added, _, out, lines, sem):
    rows = out.shape[1]
    copies = []
    for side, start in enumerate(end_starts(rows, ends.shape[0])):
        total = ends[side] + added[side].astype(F32)
        lines[side] = silu(total).astype(BF16)
        copies.append(
            pltpu.make_async_copy(lines.at[side], out.at[0, start], sem.at[side])
        )
        copies[-1].start()
    for copy in copies:
        copy.wait()


def call(kernel, out_shape, scratch, flops, args, in_place=False):
    size = sum(a.size * a.dtype.itemsize for a in args)
    vmem = pl.BlockSpec(memory_space=pltpu.VMEM)
    last = pl.BlockSpec(memory_space=pl.ANY) if in_place else vmem
    return pl.pallas_call(
        kernel,
        out_shape=out_shape,
        in_specs=[vmem] * (len(args) - 1) + [last] if args else [],
        out_specs=last if in_place else jax.tree.map(lambda _: vmem, out_shape),
        input_output_aliases={len(args) - 1: 0} if in_place else {},
        scratch_shapes=scratch,
        cost_estimate=pl.CostEstimate(flops=flops, bytes_accessed=size, transcendentals=0),
        compiler_params=pltpu.CompilerParams(vmem_limit_bytes=20 * 1024 * 1024),
    )(*args)


def local(frames, conv_fine, conv_down, conv_coarse):
    _, rows, cols, channels = frames.shape
    wide = conv_down.shape[-1]
    strips, times = lax.axis_size("rows"), lax.axis_size("tm")
    pace = call(pace_kernel, jax.ShapeDtypeStruct((8, 128), F32), [], 4 * 10**9, ())

    earlier = ring(frames, 1)
    (above, below), (above_1, below_1) = frame_rims(pace, frames)
    size = (rows + 1) * cols
    pair = jax.ShapeDtypeStruct((size, 2 * channels), F32)
    flops = 2 * size * 18 * channels * 2 * channels
    own = call(fine_own_kernel, pair, [], flops, (frames, conv_fine))
    halo = call(
        functools.partial(fine_halo_kernel, rows=rows),
        jax.ShapeDtypeStruct((3 * cols, 2 * channels), F32),
        [],
        flops // 3,
        (above, below, conv_fine),
    )
    half_rows, half_cols = rows // 2, cols // 2
    shape = jax.ShapeDtypeStruct((1, half_rows, half_cols, wide), BF16)
    fine_sums = call(fine_rest_kernel, pair, [], flops, (earlier, conv_fine, own, halo))
    inner = call(
        inner_kernel,
        jax.ShapeDtypeStruct((half_rows - (1 if strips == 2 else 2), half_cols, wide), BF16),
        [pltpu.VMEM((rows - (1 if strips == 2 else 3), cols + 8, channels), F32)],
        flops // 4,
        (fine_sums, conv_down),
    )
    above_1, below_1, fine_sums, inner = lax.optimization_barrier(
        (above_1, below_1, fine_sums, inner)
    )
    field = call(
        reduce_kernel,
        shape,
        [pltpu.VMEM((3 if strips == 2 else 6, cols + 8, channels), F32)],
        flops // 3,
        (above_1, below_1, conv_fine, fine_sums, inner, conv_down),
    )
    sides = 1 if strips == 2 else 2
    sums = jax.ShapeDtypeStruct((half_rows * half_cols, wide), F32)
    pairs = jax.ShapeDtypeStruct((sides, half_cols, wide), F32)
    flops = 2 * half_rows * half_cols * 9 * wide * wide
    odd_field = odd_ahead(field)
    even_field = even_ahead(field)
    body, ends = call(coarse_first_kernel, (sums, pairs), [], flops, (field, conv_coarse))
    odd_field, body, ends = lax.optimization_barrier((odd_field, body, ends))
    field_1 = paired(odd_field) if times % 2 == 0 else ring(field, 1)
    sent = call(
        coarse_ends_kernel,
        jax.ShapeDtypeStruct(pairs.shape, BF16),
        [],
        flops // 4,
        (field_1, odd_field, even_field, conv_coarse, ends),
    )
    if sides == 1:
        added = swapped(sent, 0)
    else:
        added = jnp.concatenate([moved(sent[:1], 0, 1), moved(sent[1:], 0, -1)], axis=0)
    out, end_sums = call(
        coarse_body_kernel,
        (shape, pairs),
        [pltpu.VMEM(sums.shape, F32)],
        flops,
        (field_1, odd_field, even_field, conv_coarse, body),
    )
    return call(
        finish_kernel,
        shape,
        [pltpu.VMEM((sides, half_cols, wide), BF16), pltpu.SemaphoreType.DMA((sides,))],
        flops // 16,
        (end_sums, added, out),
        in_place=True,
    )


def solution(mesh):
    placed = (P("tm", "rows", None, None), P(), P(), P())
    return jax.shard_map(local, mesh=mesh, in_specs=placed, out_specs=P("tm", "rows", None, None), check_vma=False)
```

```python
import functools

import jax
import jax.numpy as jnp
from jax import lax
from jax.experimental import pallas as pl
from jax.experimental.pallas import tpu as pltpu
from jax.sharding import PartitionSpec as P


F32 = jnp.float32
BF16 = jnp.bfloat16


def moved(value, steps, hop):
    tm, rows = lax.axis_size("tm"), lax.axis_size("rows")
    pairs = [
        (t * rows + r, (t + steps) * rows + r + hop)
        for t in range(tm - steps)
        for r in range(rows)
        if 0 <= r + hop < rows
    ]
    return lax.ppermute(value, ("tm", "rows"), pairs)


def ring(value, steps):
    tm = lax.axis_size("tm")
    return lax.ppermute(value, "tm", [(t, (t + steps) % tm) for t in range(tm)])


def swapped(value, steps):
    tm = lax.axis_size("tm")
    pairs = [(t * 2 + r, (t + steps) * 2 + 1 - r) for t in range(tm - steps) for r in range(2)]
    return lax.ppermute(value, ("tm", "rows"), pairs)


def odd_ahead(value):
    tm = lax.axis_size("tm")
    pairs = [(t, t + 2) for t in range(1, tm - 2, 2)] + [(t, t) for t in range(0, tm, 2)]
    return lax.ppermute(value, "tm", pairs)


def even_ahead(value):
    tm, rows = lax.axis_size("tm"), lax.axis_size("rows")
    pairs = [(t, r, t + 2, r) for t in range(0, tm - 2, 2) for r in range(rows)]
    if tm % 4 == 0 and rows % 2 == 0:
        for r in range(rows):
            pairs += [(tm - 2, r, tm - 1, r), (tm - 1, r, tm - 3, r), (1, r, 0, r)]
            pairs += [(t, r, t - 4, r) for t in range(5, tm, 4)]
            pairs += [(t, r, t, r ^ 1) for t in range(3, tm - 1, 4)]
    return lax.ppermute(value, ("tm", "rows"), [(t * rows + r, u * rows + q) for t, r, u, q in pairs])


def paired(value):
    return lax.ppermute(value, "tm", [(t, t ^ 1) for t in range(lax.axis_size("tm"))])


def has_above():
    return lax.axis_index("rows") > 0


def has_below():
    return lax.axis_index("rows") < lax.axis_size("rows") - 1


def has_earlier(steps):
    return lax.axis_index("tm") >= steps


def pace_kernel(out):
    out[...] = jnp.zeros_like(out)


def edge_kernel(_, cells, out):
    width = out.shape[1]
    first = (1 - lax.axis_index("rows")) * (cells.shape[1] - width)
    out[...] = cells[:, pl.ds(first, width)]


def frame_rims(pace, frames):
    rows = frames.shape[1]
    if lax.axis_size("rows") == 2:
        sent = call(
            edge_kernel,
            jax.ShapeDtypeStruct((frames.shape[0], 2, *frames.shape[2:]), BF16),
            [],
            0,
            (pace, frames),
        )
        return [(both, both) for both in (swapped(sent, 0), swapped(sent, 1))]
    head, tail = frames[:, :2], frames[:, rows - 1 :]
    return [(moved(tail, steps, 1), moved(head, steps, -1)) for steps in (0, 1)]


def column_shift(value, cols, steps):
    size = value.shape[0]
    column = lax.broadcasted_iota(jnp.int32, value.shape, 0) % cols
    edge = 0 if steps > 0 else cols - 1
    return jnp.where(column == edge, 0.0, pltpu.roll(value, steps % size, 0))


def shifted_columns(flat, cols):
    wide = flat.astype(F32)
    return column_shift(wide, cols, 1).astype(BF16), column_shift(wide, cols, -1).astype(BF16)


def tap_matrix(weight, first_tap, row_taps, e, channels):
    zero = jnp.zeros((channels, channels), BF16)

    def pick(tap, b):
        return weight[tap, b, e * channels : (e + 1) * channels] if 0 <= tap <= 2 else zero

    return jnp.concatenate(
        [
            jnp.concatenate([pick(first_tap + f, b), pick(first_tap + f - 1, b)], axis=1)
            for f in range(2)
            for b in row_taps
        ],
        axis=0,
    )


def fine_rows(row, outs, row_taps, weight, first_tap):
    channels = weight.shape[-1]
    some = next(x for f in range(2) for r in outs for b in row_taps if (x := row(f, r - 1 + b)) is not None)
    cols = some.shape[0]
    zero = jnp.zeros((cols, channels), BF16)

    def cell(f, i):
        found = row(f, i)
        return zero if found is None else found

    left = jnp.concatenate(
        [
            jnp.concatenate([cell(f, r - 1 + b) for f in range(2) for b in row_taps], axis=1)
            for r in outs
        ],
        axis=0,
    )
    sums = [
        jnp.dot(
            left, tap_matrix(weight, first_tap, row_taps, e, channels), preferred_element_type=F32
        )
        for e in range(3)
    ]
    return sums[1] + column_shift(sums[0], cols, 1) + column_shift(sums[2], cols, -1)


def previous_rows(row, outs, weight):
    channels = weight.shape[-1]
    cols = next(x for r in outs if (x := row(1, r)) is not None).shape[0]
    zero = jnp.zeros((cols, channels), BF16)
    none = jnp.zeros((channels, channels), BF16)

    def cells(taps):
        lines = [
            jnp.concatenate([zero if (x := row(f, r - 1 + b)) is None else x for f, b in taps], axis=1)
            for r in outs
        ]
        return jnp.concatenate(lines, axis=0)

    def part(tap, b, e):
        return weight[tap, b, e * channels : (e + 1) * channels]

    def pair(left, right):
        return jnp.concatenate([left, right], axis=1)

    dot = functools.partial(jnp.dot, preferred_element_type=F32)
    near = cells([(1, 0), (1, 1), (1, 2), (0, 2)])
    sums = []
    for e in range(3):
        right = [pair(part(1, b, e), part(0, b, e)) for b in range(3)] + [pair(part(0, 2, e), none)]
        sums.append(dot(near, jnp.concatenate(right, axis=0)))
    far = cells([(0, 0), (0, 1)])
    both = dot(far, jnp.concatenate([pair(part(0, b, 0), part(0, b, 1)) for b in range(2)], axis=0))
    last = dot(far, jnp.concatenate([part(0, b, 2) for b in range(2)], axis=0))
    old = (both[:, :channels], both[:, channels:], last)
    first = [x[:, :channels] + y for x, y in zip(sums, old)]
    second = [x[:, channels:] for x in sums]
    return pair(*(
        x[1] + column_shift(x[0], cols, 1) + column_shift(x[2], cols, -1) for x in (first, second)
    ))


def chunks_of(count):
    size = next(c for c in (4, 3, 2, 1) if count % c == 0)
    return [range(i, i + size) for i in range(0, count, size)]


def fine_own_kernel(frames, weight, out):
    _, rows, cols, _ = frames.shape

    def row(f, i):
        return frames[f, i] if 0 <= i < rows else None

    for outs in chunks_of(rows + 1):
        out[outs[0] * cols : (outs[-1] + 1) * cols] = fine_rows(row, outs, range(3), weight, 2)


def halo_row(above, below, rows):
    def row(f, i):
        if i == -1:
            cells, have = above[f, above.shape[1] - 1], has_above()
        elif i >= rows:
            cells, have = below[f, i - rows], has_below()
        else:
            return None
        return jnp.where(have, cells, jnp.zeros_like(cells))

    return row


def halo_sum(above, below, weight, first_tap, rows):
    row = halo_row(above, below, rows)
    return jnp.concatenate(
        [
            fine_rows(row, [0], [0], weight, first_tap),
            fine_rows(row, [rows - 1, rows], [1, 2], weight, first_tap),
        ],
        axis=0,
    )


def fine_halo_kernel(above, below, weight, out, *, rows):
    out[...] = halo_sum(above, below, weight, 2, rows)


def silu(v):
    half = 0.5 * v
    return half + half * jnp.tanh(half)


def fine_rest_kernel(frames, weight, own, halo, out):
    _, rows, cols, _ = frames.shape

    def row(f, i):
        return frames[f, i] if 0 <= i < rows else None

    for outs in chunks_of(rows + 1):
        total = jnp.where(has_earlier(1), previous_rows(row, outs, weight), 0.0)
        for i, r in enumerate(outs):
            line = total[i * cols : (i + 1) * cols] + own[r * cols : (r + 1) * cols]
            for k, halo_r in enumerate((0, rows - 1, rows)):
                if r == halo_r:
                    line = line + halo[k * cols : (k + 1) * cols]
            out[r * cols : (r + 1) * cols] = line


def pool(sums):
    channels = sums.shape[1] // 2
    fine = silu(sums).astype(BF16).astype(F32)
    return ((fine[:, :channels] + fine[:, channels:]) * 0.5).astype(BF16).astype(F32)


def down_taps(pooled, half_cols):
    return [
        jnp.concatenate(
            [pooled[i, pl.ds(e, half_cols, stride=2), :].astype(BF16) for e in range(3)], axis=1
        )
        for i in range(pooled.shape[0])
    ]


def put_pooled(pooled, lines):
    cols = lines[0].shape[0]
    pad = pooled.shape[1] - cols
    pooled[:, cols:] = jnp.zeros((pooled.shape[0], pad, pooled.shape[2]), F32)
    for i, line in enumerate(lines):
        pooled[i, :cols] = line


def reduced_rows(lines, firsts, half_cols, down, pooled):
    put_pooled(pooled, lines)
    taps = down_taps(pooled, half_cols)
    left = [jnp.concatenate(taps[i : i + 3], axis=1) for i in firsts]
    right = down[...].reshape(-1, down.shape[-1])
    rows = jnp.dot(jnp.concatenate(left, axis=0), right, preferred_element_type=F32)
    return rows.astype(BF16).reshape(len(firsts), half_cols, -1)


def inner_kernel(sums, down, out, pooled):
    count, half_cols, _ = out.shape
    cols = 2 * half_cols
    size = 2 * count + 1
    two = lax.axis_size("rows") == 2
    start = 2 * lax.axis_index("rows") if two else 2
    mean = pool(sums[pl.ds(pl.multiple_of(start * cols, cols), size * cols), :])
    lines = [mean[k * cols : (k + 1) * cols] for k in range(size)]
    if two:
        lines[-1] = jnp.where(has_below(), lines[-1], 0.0)
    out[...] = reduced_rows(lines, range(0, 2 * count, 2), half_cols, down, pooled)


def one_halo_sum(rims, weight):
    cols, channels = rims.shape[2:]
    up = has_above()
    zero = jnp.zeros((cols, channels), BF16)
    left = jnp.concatenate(
        [
            jnp.concatenate(
                [x for f in range(2) for x in (jnp.where(up, rims[f, 1], zero), jnp.where(up, zero, rims[f, 0]))],
                axis=1,
            ),
            jnp.concatenate([jnp.where(up, zero, rims[f, k]) for f in range(2) for k in range(2)], axis=1),
        ],
        axis=0,
    )
    b = 1 - lax.axis_index("rows")
    x = [
        jnp.dot(left, tap_matrix(weight, 0, (b, b + 1), e, channels), preferred_element_type=F32)
        for e in range(3)
    ]
    added = x[1] + column_shift(x[0], cols, 1) + column_shift(x[2], cols, -1)
    none = jnp.zeros((cols, added.shape[1]), F32)
    below = jnp.concatenate([none, added], axis=0)
    return jnp.where(up, jnp.concatenate([added[:cols], none, none], axis=0), below)


def reduce_kernel(above, below, weight, sums, inner, down, out, pooled):
    cols = above.shape[2]
    rows = sums.shape[0] // cols - 1
    half = rows // 2
    if lax.axis_size("rows") == 2:
        strip = lax.axis_index("rows")
        begin = pl.multiple_of((rows - 2) * (1 - strip) * cols, cols)
        mean = pool(sums[pl.ds(begin, 3 * cols), :] + one_halo_sum(above, weight))
        lines = [mean[k * cols : (k + 1) * cols] for k in range(3)]
        end = reduced_rows(lines, (0,), cols // 2, down, pooled)
        out[0, pl.ds(strip, half - 1)] = inner[...]
        out[0, (half - 1) * (1 - strip)] = end[0]
        return
    added = halo_sum(above, below, weight, 0, rows)
    lines = []
    for r in (0, 1, 2, rows - 2, rows - 1, rows):
        line = sums[r * cols : (r + 1) * cols]
        for k, halo_r in enumerate((0, rows - 1, rows)):
            if r == halo_r:
                line = line + added[k * cols : (k + 1) * cols]
        line = pool(line)
        lines.append(jnp.where(has_below(), line, 0.0) if r == rows else line)
    ends = reduced_rows(lines, (0, 3), cols // 2, down, pooled)
    out[0, 0] = ends[0]
    out[0, 1 : half - 1] = inner[...]
    out[0, half - 1] = ends[1]


def column_taps(flat, cols):
    left, right = shifted_columns(flat, cols)
    return jnp.concatenate([left, flat, right], axis=1)


def coarse_sums(field, weight, a, sides):
    _, rows, cols, channels = field.shape
    body = column_taps(field.reshape(rows * cols, channels), cols)
    zero = jnp.zeros_like(body[:cols])
    tall = jnp.concatenate([zero, body, zero], axis=0)
    dot = functools.partial(jnp.dot, preferred_element_type=F32)
    total = sum(dot(tall[b * cols : (b + rows) * cols], weight[a, b]) for b in range(3))
    head, tail = body[:cols], body[(rows - 1) * cols :]
    if sides == 1:
        return total, [dot(jnp.where(has_above(), head, tail), weight[a, 2 * lax.axis_index("rows")])]
    return total, [dot(tail, weight[a, 0]), dot(head, weight[a, 2])]


def coarse_first_kernel(field, weight, body, ends):
    total, parts = coarse_sums(field[...], weight, 2, ends.shape[0])
    body[...] = total
    for side, part in enumerate(parts):
        ends[side] = part


def coarse_next_kernel(field, weight, body_in, ends_in, body, ends):
    cells = field[...]
    cells = jnp.where(has_earlier(1), cells, jnp.zeros_like(cells))
    total, parts = coarse_sums(cells, weight, 1, ends.shape[0])
    body[...] = body_in[...] + total
    for side, part in enumerate(parts):
        ends[side] = ends_in[side] + part


def second_earlier(odd_field, even_field):
    cells = jnp.where(lax.axis_index("tm") % 2 == 1, odd_field[...], even_field[...])
    return jnp.where(has_earlier(2), cells, jnp.zeros_like(cells))


def coarse_ends_kernel(odd_field, even_field, weight, ends, out):
    _, parts = coarse_sums(second_earlier(odd_field, even_field), weight, 0, ends.shape[0])
    for side, part in enumerate(parts):
        out[side] = (ends[side] + part).astype(BF16)


def end_starts(rows, sides):
    return [(rows - 1) * (1 - lax.axis_index("rows"))] if sides == 1 else [0, rows - 1]


def coarse_body_kernel(odd_field, even_field, weight, body, out, ends, sums):
    _, rows, cols, _ = out.shape
    total, _ = coarse_sums(second_earlier(odd_field, even_field), weight, 0, ends.shape[0])
    sums[...] = body[...] + total
    out[...] = silu(sums[...]).astype(BF16).reshape(out.shape)
    for side, start in enumerate(end_starts(rows, ends.shape[0])):
        ends[side] = sums[pl.ds(pl.multiple_of(start * cols, cols), cols), :]


def finish_kernel(ends, added, _, out, lines, sem):
    rows = out.shape[1]
    copies = []
    for side, start in enumerate(end_starts(rows, ends.shape[0])):
        total = ends[side] + added[side].astype(F32)
        lines[side] = silu(total).astype(BF16)
        copies.append(
            pltpu.make_async_copy(lines.at[side], out.at[0, start], sem.at[side])
        )
        copies[-1].start()
    for copy in copies:
        copy.wait()


def call(kernel, out_shape, scratch, flops, args, in_place=False):
    size = sum(a.size * a.dtype.itemsize for a in args)
    vmem = pl.BlockSpec(memory_space=pltpu.VMEM)
    last = pl.BlockSpec(memory_space=pl.ANY) if in_place else vmem
    return pl.pallas_call(
        kernel,
        out_shape=out_shape,
        in_specs=[vmem] * (len(args) - 1) + [last] if args else [],
        out_specs=last if in_place else jax.tree.map(lambda _: vmem, out_shape),
        input_output_aliases={len(args) - 1: 0} if in_place else {},
        scratch_shapes=scratch,
        cost_estimate=pl.CostEstimate(flops=flops, bytes_accessed=size, transcendentals=0),
        compiler_params=pltpu.CompilerParams(vmem_limit_bytes=20 * 1024 * 1024),
    )(*args)


def local(frames, conv_fine, conv_down, conv_coarse):
    _, rows, cols, channels = frames.shape
    wide = conv_down.shape[-1]
    strips, times = lax.axis_size("rows"), lax.axis_size("tm")
    pace = call(pace_kernel, jax.ShapeDtypeStruct((8, 128), F32), [], 4 * 10**9, ())

    earlier = ring(frames, 1)
    (above, below), (above_1, below_1) = frame_rims(pace, frames)
    size = (rows + 1) * cols
    pair = jax.ShapeDtypeStruct((size, 2 * channels), F32)
    flops = 2 * size * 18 * channels * 2 * channels
    own = call(fine_own_kernel, pair, [], flops, (frames, conv_fine))
    halo = call(
        functools.partial(fine_halo_kernel, rows=rows),
        jax.ShapeDtypeStruct((3 * cols, 2 * channels), F32),
        [],
        flops // 3,
        (above, below, conv_fine),
    )
    half_rows, half_cols = rows // 2, cols // 2
    shape = jax.ShapeDtypeStruct((1, half_rows, half_cols, wide), BF16)
    fine_sums = call(fine_rest_kernel, pair, [], flops, (earlier, conv_fine, own, halo))
    inner = call(
        inner_kernel,
        jax.ShapeDtypeStruct((half_rows - (1 if strips == 2 else 2), half_cols, wide), BF16),
        [pltpu.VMEM((rows - (1 if strips == 2 else 3), cols + 8, channels), F32)],
        flops // 4,
        (fine_sums, conv_down),
    )
    above_1, below_1, fine_sums, inner = lax.optimization_barrier(
        (above_1, below_1, fine_sums, inner)
    )
    field = call(
        reduce_kernel,
        shape,
        [pltpu.VMEM((3 if strips == 2 else 6, cols + 8, channels), F32)],
        flops // 3,
        (above_1, below_1, conv_fine, fine_sums, inner, conv_down),
    )
    sides = 1 if strips == 2 else 2
    sums = jax.ShapeDtypeStruct((half_rows * half_cols, wide), F32)
    pairs = jax.ShapeDtypeStruct((sides, half_cols, wide), F32)
    flops = 2 * half_rows * half_cols * 9 * wide * wide
    odd_field = odd_ahead(field)
    even_field = even_ahead(field)
    body, ends = call(coarse_first_kernel, (sums, pairs), [], flops, (field, conv_coarse))
    odd_field, body, ends = lax.optimization_barrier((odd_field, body, ends))
    field_1 = paired(odd_field) if times % 2 == 0 else ring(field, 1)
    body, ends = call(
        coarse_next_kernel, (sums, pairs), [], flops, (field_1, conv_coarse, body, ends)
    )
    even_field, body, ends = lax.optimization_barrier((even_field, body, ends))
    sent = call(
        coarse_ends_kernel,
        jax.ShapeDtypeStruct(pairs.shape, BF16),
        [],
        flops // 4,
        (odd_field, even_field, conv_coarse, ends),
    )
    if sides == 1:
        added = swapped(sent, 0)
    else:
        added = jnp.concatenate([moved(sent[:1], 0, 1), moved(sent[1:], 0, -1)], axis=0)
    out, end_sums = call(
        coarse_body_kernel,
        (shape, pairs),
        [pltpu.VMEM(sums.shape, F32)],
        flops,
        (odd_field, even_field, conv_coarse, body),
    )
    return call(
        finish_kernel,
        shape,
        [pltpu.VMEM((sides, half_cols, wide), BF16), pltpu.SemaphoreType.DMA((sides,))],
        flops // 16,
        (end_sums, added, out),
        in_place=True,
    )


def solution(mesh):
    placed = (P("tm", "rows", None, None), P(), P(), P())
    return jax.shard_map(local, mesh=mesh, in_specs=placed, out_specs=P("tm", "rows", None, None), check_vma=False)
```
